32 devices in a mesh: dp: 16 (over z, y, x), seq: 2 (over core).
Axes of the slice: x: 2, y: 2, z: 4, core: 2. Of those that a mesh axis runs over, the one named last changes fastest.
Arguments:
- tokens: bfloat16 [64, 512, 768], P('dp', 'seq'), may hold values from -6 to 6
- lengths: int32 [64, 6], P('dp'), may hold values from 1 to 192, 512 in all within a row
- w_qkv: bfloat16 [768, 2304], replicated, may hold values from -0.21875 to 0.21875
- w_out: bfloat16 [768, 768], replicated, may hold values from -1.75 to 1.75
- w_in: bfloat16 [768, 3072], replicated, may hold values from -0.21875 to 0.21875
- w_back: bfloat16 [3072, 768], replicated, may hold values from -0.109375 to 0.109375
- bias_q: float32 [768], replicated, may hold values from -3 to 3
- value_bias_vector: float32 [768], replicated, may hold values from -3 to 3
- bias_out: float32 [768], replicated, may hold values from -3 to 3
- gain1: float32 [768], replicated, may hold values from 0.25 to 1.75
- shift1: float32 [768], replicated, may hold values from -3 to 3
- bias_in: float32 [3072], replicated, may hold values from -3 to 3
- bias_back: float32 [768], replicated, may hold values from -3 to 3
- gain2: float32 [768], replicated, may hold values from 0.25 to 1.75
- shift2: float32 [768], replicated, may hold values from -3 to 3
- cotangent: bfloat16 [64, 512, 768], P('dp', 'seq'), may hold values from -6 to 6
Outputs:
- layer_output: bfloat16 [64, 512, 768], P('dp', 'seq')
- cls_vectors: bfloat16 [64, 6, 768], P('dp')
- input_grad: bfloat16 [64, 512, 768], P('dp', 'seq')
- grad_qkv: float32 [1769472], P(('dp', 'seq'))
- grad_out: float32 [589824], P(('dp', 'seq'))
- grad_in: float32 [2359296], P(('dp', 'seq'))
- grad_back: float32 [2359296], P(('dp', 'seq'))
- vector_grads: float32 [9216], P(('dp', 'seq'))
The draws below stay inside these ranges and needn't reach their ends.
Inputs may be any that keep to these rules, and one draw needn't show every extreme that they name: Each row's 6 lengths sum to 512, and the longest in every row is exactly 192; a passage's first position holds its CLS token.
All inputs are finite; a program needn't handle non-finite values.
Results may differ from the reference program's by a relative error of at most 0.015.
Values may be sent and summed in bfloat16 or wider, within the bound.
No kernel may reach another device: no remote copies, remote signals or barrier semaphores. Data moves between devices by JAX's collectives and lax.ppermute only.
A program may use at most 192 MiB of HBM per device.

```python
import math
import jax
import jax.numpy as jnp
import numpy as np
from jax import lax

D = 768
HEADS = 12
HEAD_SIZE = 64
FF = 3072
L = 512
SEG = 6
MOST = 192
MB = 2
RPM = 2
ROWS = 64
N_DP = 16


def level_of(stream_key, dims, split, smallest, high):
    loudness = 1.0
    for position, shards_of in split:
        draws = jax.random.uniform(jax.random.fold_in(jax.random.fold_in(stream_key, 6), position), (shards_of,), jnp.float32, smallest / len(split), high / len(split))
        loudness = loudness * jnp.repeat(jnp.exp(draws), dims[position] // shards_of).reshape((-1,) + (1,) * (len(dims) - 1 - position))
    return loudness


def split_up(number_of, total, bound, skew):
    loads = [(1 << 20) // math.isqrt(grade ** skew) + 1 for grade in range(2, number_of + 1)]
    surplus, given = total - bound - (number_of - 1), [1] * (number_of - 1)
    while surplus > 0:
        movable = [i for i in range(number_of - 1) if given[i] < bound]
        pool, budget = sum([loads[i] for i in movable]), surplus
        for i in movable:
            more = min(bound - given[i], max(1, budget * loads[i] // pool), surplus)
            given[i] = given[i] + more
            surplus = surplus - more
    return np.array([bound] + given)


def uneven(stream_key, amount, total, limit, slope):
    if amount == 2:
        one = jax.random.randint(stream_key, (), max(1, total - limit), min(limit, total - 1) + 1)
        return jnp.stack([one, total - one])
    tallies = jnp.asarray(split_up(amount, total, limit, slope), jnp.int32)
    couples = (amount - 1) // 2
    donor, receiver = tallies[1:1 + 2 * couples:2], tallies[2:2 + 2 * couples:2]
    slack = jnp.minimum(donor - 1, limit - receiver)
    shifted = jax.random.randint(jax.random.fold_in(stream_key, 1), (couples,), 0, 1 << 20) % (slack + 1)
    tallies = tallies.at[1:1 + 2 * couples:2].set(donor - shifted).at[2:2 + 2 * couples:2].set(receiver + shifted)
    return tallies[jax.random.permutation(jax.random.fold_in(stream_key, 2), amount)]


def gaussian(key, shape, width, most, shards=(), kind=jnp.bfloat16):
    result = width * jax.random.normal(key, shape, jnp.float32)
    if shards:
        result = result * level_of(key, shape, shards, -0.22, 0.18)
    return jnp.clip(result, -most, most).astype(kind)


def setup_inputs(seed: int = 0) -> dict:
    seeds = jax.random.split(jax.random.key(seed), 17)
    tokens = gaussian(seeds[0], (ROWS, L, D), 1.0, 6.0, ((0, 16), (1, 2)))
    lengths = jax.vmap(lambda own: uneven(own, SEG, L, MOST, 2))(jax.random.split(seeds[1], ROWS)).reshape((ROWS, SEG)).astype(jnp.int32)
    w_qkv = gaussian(seeds[2], (D, 3 * D), D ** -0.5, 0.21875)
    w_out = gaussian(seeds[3], (D, D), (D // 64) ** -0.5, 1.75)
    w_in = gaussian(seeds[4], (D, FF), D ** -0.5, 0.21875)
    w_back = gaussian(seeds[5], (FF, D), FF ** -0.5, 0.109375)
    bias_q = gaussian(seeds[6], (D,), 0.5, 3.0, (), jnp.float32)
    value_bias_vector = gaussian(seeds[7], (D,), 0.5, 3.0, (), jnp.float32)
    bias_out = gaussian(seeds[8], (D,), 0.5, 3.0, (), jnp.float32)
    gain1 = jnp.clip(1.0 + 0.15 * jax.random.normal(seeds[9], (D,), jnp.float32), 0.25, 1.75)
    shift1 = gaussian(seeds[10], (D,), 0.5, 3.0, (), jnp.float32)
    bias_in = gaussian(seeds[11], (FF,), 0.5, 3.0, (), jnp.float32)
    bias_back = gaussian(seeds[12], (D,), 0.5, 3.0, (), jnp.float32)
    gain2 = jnp.clip(1.0 + 0.15 * jax.random.normal(seeds[13], (D,), jnp.float32), 0.25, 1.75)
    shift2 = gaussian(seeds[14], (D,), 0.5, 3.0, (), jnp.float32)
    cotangent = gaussian(seeds[15], (ROWS, L, D), 1.0, 6.0, ((0, 16), (1, 2)))
    return dict(tokens=tokens, lengths=lengths, w_qkv=w_qkv, w_out=w_out, w_in=w_in, w_back=w_back, bias_q=bias_q, value_bias_vector=value_bias_vector, bias_out=bias_out, gain1=gain1, shift1=shift1, bias_in=bias_in, bias_back=bias_back, gain2=gain2, shift2=shift2, cotangent=cotangent)


@jax.custom_vjp
def low(v):
    return lax.optimization_barrier(v.astype(jnp.bfloat16)).astype(jnp.float32)

@jax.custom_vjp
def low_back(v):
    return v

def low_keep(v):
    return (low(v), None)

def low_pass(kept, grad):
    return (grad,)

def back_keep(v):
    return (v, None)

def back_low(kept, grad):
    return (low(grad),)
low.defvjp(low_keep, low_pass)
low_back.defvjp(back_keep, back_low)
EPS = 1e-12

def layer_norm(hidden, gain, shift):
    center = hidden - lax.optimization_barrier(jnp.mean(hidden, axis=-1, keepdims=True))
    feature_variance = lax.optimization_barrier(jnp.mean(center * center, axis=-1, keepdims=True))
    return center * lax.rsqrt(feature_variance + EPS) * gain + shift

def segment_table(row_lengths, positions):
    starts = jnp.cumsum(row_lengths, axis=1) - row_lengths
    return lax.optimization_barrier(jnp.sum((positions[None, :, None] >= starts[:, None, :]).astype(jnp.int32), axis=-1)) - 1

def forward(params, inputs, segment):
    w_qkv, w_out, w_in, w_back, bias_q, value_bias_vector, bias_out, gain1, shift1, bias_in, bias_back, gain2, shift2 = params
    exact = lax.Precision.HIGHEST
    row_count = inputs.shape[0]
    rounded = low(inputs)
    projected = jnp.einsum('rtd,de->rte', rounded, w_qkv, precision=exact)
    queries = low(low_back(projected[..., :D] + bias_q)).reshape(row_count, L, HEADS, HEAD_SIZE)
    keys_all = low(low_back(projected[..., D:2 * D])).reshape(row_count, L, HEADS, HEAD_SIZE)
    values_all = low(low_back(projected[..., 2 * D:] + value_bias_vector)).reshape(row_count, L, HEADS, HEAD_SIZE)
    scores = low_back(jnp.einsum('rqhd,rkhd->rhqk', queries, keys_all, precision=exact) * HEAD_SIZE ** (-0.5))
    same_segment = (segment[:, :, None] == segment[:, None, :])[:, None]
    weights = jax.nn.softmax(jnp.where(same_segment, scores, -1e+30), axis=-1)
    mixed = jnp.einsum('rhqk,rkhd->rqhd', low(weights), values_all, precision=exact).reshape(row_count, L, D)
    mixed = low(low_back(mixed))
    branch = low_back(jnp.einsum('rtd,de->rte', mixed, w_out, precision=exact) + bias_out)
    normed1 = layer_norm(inputs + branch, gain1, shift1)
    inner_pre = low_back(jnp.einsum('rtd,df->rtf', low(normed1), w_in, precision=exact) + bias_in)
    activation = low(jax.nn.gelu(inner_pre, approximate=False))
    feed = low_back(jnp.einsum('rtf,fd->rtd', activation, w_back, precision=exact) + bias_back)
    return layer_norm(normed1 + feed, gain2, shift2)

def pick_rows(rows_block, starts):
    return rows_block[starts]

def reference(tokens, lengths, w_qkv, w_out, w_in, w_back, bias_q, value_bias_vector, bias_out, gain1, shift1, bias_in, bias_back, gain2, shift2, cotangent):
    params = tuple((item.astype(jnp.float32) for item in (w_qkv, w_out, w_in, w_back, bias_q, value_bias_vector, bias_out, gain1, shift1, bias_in, bias_back, gain2, shift2)))
    group = RPM * MB
    positions = jnp.arange(L, dtype=jnp.int32)
    token_groups = tokens.reshape(N_DP, group, L, D)
    length_groups = lengths.reshape(N_DP, group, SEG)
    cot_groups = cotangent.reshape(N_DP, group, L, D)

    def one_group(sums, pieces):
        token_block, length_block, cot_block = pieces
        segment = segment_table(length_block, positions)

        def apply_layer(weights_set, inputs):
            return forward(weights_set, inputs, segment)
        output, pull = jax.vjp(apply_layer, params, token_block.astype(jnp.float32))
        weight_grads, grad_inputs = pull(cot_block.astype(jnp.float32))
        output_low = output.astype(jnp.bfloat16)
        starts = (jnp.cumsum(length_block, axis=1) - length_block).astype(jnp.int32)
        cls_block = jax.vmap(pick_rows)(output_low, starts)
        sums = jax.tree.map(jnp.add, sums, weight_grads)
        return (sums, (output_low, cls_block, grad_inputs.astype(jnp.bfloat16)))
    zeros = jax.tree.map(jnp.zeros_like, params)
    sums, (outputs, cls_all, grad_all) = lax.scan(one_group, zeros, (token_groups, length_groups, cot_groups))
    vector = jnp.concatenate(sums[4:], axis=0)
    return (outputs.reshape(ROWS, L, D), cls_all.reshape(ROWS, SEG, D), grad_all.reshape(ROWS, L, D), sums[0].reshape(-1), sums[1].reshape(-1), sums[2].reshape(-1), sums[3].reshape(-1), vector)
```

```python
from functools import partial

import jax
import jax.numpy as jnp
from jax import lax
from jax.sharding import PartitionSpec as P

HEADS = 12
EPS = 1e-12
BF = jnp.bfloat16
F32 = jnp.float32


def normalize(hidden):
    center = hidden - jnp.mean(hidden, axis=-1, keepdims=True)
    variance = jnp.mean(center * center, axis=-1, keepdims=True)
    inverse = lax.rsqrt(variance + EPS)
    return center * inverse, inverse


def norm_backward(grad_hat, normed, inverse):
    first = jnp.mean(grad_hat, axis=-1, keepdims=True)
    second = jnp.mean(grad_hat * normed, axis=-1, keepdims=True)
    return inverse * (grad_hat - first - normed * second)


def swap(value):
    return lax.ppermute(value, "seq", [(0, 1), (1, 0)])


def pick(value, index, axis):
    return lax.dynamic_index_in_dim(value, index, axis, keepdims=False)


def reduce_stages(part, order, dp_bits, dp):
    me = lax.axis_index("dp")
    n_halving = dp_bits - 2
    shape = part.shape[1:]
    current = part.reshape((2,) * dp_bits + shape)
    left = list(range(dp_bits - 1, -1, -1))
    for bit in order[:n_halving]:
        axis = left.index(bit)
        mine = (me >> bit) & 1
        pairs = [(i, i ^ (1 << bit)) for i in range(dp)]
        send = pick(current, 1 - mine, axis).astype(BF)
        got = lax.ppermute(send, "dp", pairs)
        keep = pick(current, mine, axis)
        current = keep.astype(F32) + got.astype(F32)
        left.remove(bit)
    high, low = left
    group = (((me >> high) & 1) << 1) | ((me >> low) & 1)
    current = current.reshape((4,) + shape)
    total = pick(current, group, 0).astype(F32)
    for other in (1, 2, 3):
        flip = ((other >> 1) << high) | ((other & 1) << low)
        pairs = [(i, i ^ flip) for i in range(dp)]
        send = pick(current, group ^ other, 0).astype(BF)
        total = total + lax.ppermute(send, "dp", pairs).astype(F32)
    return total


def reduce_scatter(grad, order, dp, dp_bits):
    core = lax.axis_index("seq")
    rows = grad.shape[0] // (2 * dp)
    blocks = grad.reshape(dp, 2, rows, grad.shape[1])
    send = pick(blocks, 1 - core, 1).astype(BF)
    keep = pick(blocks, core, 1)
    part = keep.astype(F32) + swap(send).astype(F32)
    return reduce_stages(part, order, dp_bits, dp)


def on_device(tokens, lengths, w_qkv, w_out, w_in, w_back, bias_q, value_bias, bias_out, gain1, shift1, bias_in, bias_back, gain2, shift2, cotangent):
    rows_local, half, width = tokens.shape
    dp = lax.axis_size("dp")
    dp_bits = dp.bit_length() - 1
    core = lax.axis_index("seq")
    rows = rows_local // 2
    length = 2 * half
    head_size = width // HEADS
    scale = head_size ** -0.5

    def gather_rows(value):
        own = lax.dynamic_slice_in_dim(value, core * rows, rows, 0)
        other = swap(lax.dynamic_slice_in_dim(value, (1 - core) * rows, rows, 0))
        return jnp.concatenate([own, other], axis=1)

    def spread_rows(value):
        got = swap(value[:, half:])
        out = jnp.zeros((rows_local, half, width), value.dtype)
        out = lax.dynamic_update_slice_in_dim(out, value[:, :half], core * rows, 0)
        return lax.dynamic_update_slice_in_dim(out, got, (1 - core) * rows, 0)

    tok = gather_rows(tokens)
    cot = gather_rows(cotangent)
    row_lengths = lax.dynamic_slice_in_dim(lengths, core * rows, rows, 0)
    local = jnp.arange(half, dtype=jnp.int32)
    positions = jnp.concatenate([core * half + local, (1 - core) * half + local])
    starts = jnp.cumsum(row_lengths, axis=1) - row_lengths
    segment = jnp.sum((positions[None, :, None] >= starts[:, None, :]).astype(jnp.int32), axis=-1)
    same = (segment[:, :, None] == segment[:, None, :])[:, None]

    flat = tok.reshape(-1, width)
    projected = jnp.dot(flat, w_qkv, preferred_element_type=F32)
    q = (projected[:, :width] + bias_q).astype(BF)
    k = projected[:, width : 2 * width].astype(BF)
    v = (projected[:, 2 * width :] + value_bias).astype(BF)
    qh, kh, vh = (x.reshape(rows, length, HEADS, head_size) for x in (q, k, v))
    scores = jnp.einsum("bqhd,bkhd->bhqk", qh, kh, preferred_element_type=F32) * scale
    masked = jnp.where(same, scores, -1e30)
    weight = jnp.exp(masked - jnp.max(masked, axis=-1, keepdims=True))
    probs = (weight / jnp.sum(weight, axis=-1, keepdims=True)).astype(BF)
    mixed = jnp.einsum("bhqk,bkhd->bqhd", probs, vh, preferred_element_type=F32)
    mixed = mixed.reshape(-1, width).astype(BF)
    hat1, inv1 = normalize(flat.astype(F32) + jnp.dot(mixed, w_out, preferred_element_type=F32) + bias_out)
    normed1 = hat1 * gain1 + shift1
    normed_low = normed1.astype(BF)
    inner = jnp.dot(normed_low, w_in, preferred_element_type=F32) + bias_in
    act, gelu_back = jax.vjp(partial(jax.nn.gelu, approximate=False), inner)
    act_low = act.astype(BF)
    hat2, inv2 = normalize(normed1 + jnp.dot(act_low, w_back, preferred_element_type=F32) + bias_back)
    output = (hat2 * gain2 + shift2).astype(BF).reshape(rows, length, width)
    choose = (starts[:, :, None] == positions[None, None, :]).astype(BF)
    cls_own = jnp.einsum("rsp,rpd->rsd", choose, output, preferred_element_type=F32).astype(BF)
    cls_other = swap(cls_own)
    cls = jnp.zeros((rows_local,) + cls_own.shape[1:], BF)
    cls = lax.dynamic_update_slice_in_dim(cls, cls_own, core * rows, 0)
    cls = lax.dynamic_update_slice_in_dim(cls, cls_other, (1 - core) * rows, 0)

    dy = cot.reshape(-1, width).astype(F32)
    g_gain2 = jnp.sum(dy * hat2, axis=0)
    g_shift2 = jnp.sum(dy, axis=0)
    dpre2 = norm_backward(dy * gain2, hat2, inv2)
    dfeed = dpre2.astype(BF)
    g_bias_back = jnp.sum(dfeed.astype(F32), axis=0)
    g_back = jnp.einsum("tf,td->fd", act_low, dfeed, preferred_element_type=F32)
    r_back = reduce_scatter(g_back, (0, 1) + tuple(range(2, dp_bits)), dp, dp_bits)
    dact = jnp.einsum("td,fd->tf", dfeed, w_back, preferred_element_type=F32)
    dinner = gelu_back(dact)[0].astype(BF)
    g_bias_in = jnp.sum(dinner.astype(F32), axis=0)
    g_in = jnp.einsum("td,tf->df", normed_low, dinner, preferred_element_type=F32)
    r_in = reduce_scatter(g_in, (1, 0) + tuple(range(2, dp_bits)), dp, dp_bits)
    dnormed1 = dpre2 + jnp.einsum("tf,df->td", dinner, w_in, preferred_element_type=F32)
    g_gain1 = jnp.sum(dnormed1 * hat1, axis=0)
    g_shift1 = jnp.sum(dnormed1, axis=0)
    dpre1 = norm_backward(dnormed1 * gain1, hat1, inv1)
    dbranch = dpre1.astype(BF)
    g_bias_out = jnp.sum(dbranch.astype(F32), axis=0)
    g_out = jnp.einsum("tc,td->cd", mixed, dbranch, preferred_element_type=F32)
    r_out = reduce_scatter(g_out, (0, 1) + tuple(range(2, dp_bits)), dp, dp_bits)
    dmixed = jnp.einsum("td,cd->tc", dbranch, w_out, preferred_element_type=F32).astype(BF)
    dmh = dmixed.reshape(rows, length, HEADS, head_size)
    dprobs = jnp.einsum("bqhd,bkhd->bhqk", dmh, vh, preferred_element_type=F32)
    pf = probs.astype(F32)
    delta = jnp.sum(pf * dprobs, axis=-1, keepdims=True)
    dscores = (pf * (dprobs - delta)).astype(BF)
    dq = (jnp.einsum("bhqk,bkhd->bqhd", dscores, kh, preferred_element_type=F32) * scale).astype(BF)
    dk = (jnp.einsum("bhqk,bqhd->bkhd", dscores, qh, preferred_element_type=F32) * scale).astype(BF)
    dv = jnp.einsum("bhqk,bqhd->bkhd", probs, dmh, preferred_element_type=F32).astype(BF)
    dproj = jnp.concatenate([x.reshape(-1, width) for x in (dq, dk, dv)], axis=1)
    g_proj_bias = jnp.sum(dproj.astype(F32), axis=0)
    g_qkv = jnp.einsum("td,te->de", flat, dproj, preferred_element_type=F32)
    vectors = jnp.concatenate([g_proj_bias[:width], g_proj_bias[2 * width :], g_bias_out, g_gain1, g_shift1, g_bias_in, g_bias_back, g_gain2, g_shift2])
    vectors = vectors.reshape(2 * dp, 1, -1)
    n_vec = vectors.shape[-1]
    vectors = jnp.pad(vectors, ((0, 0), (0, 7), (0, g_qkv.shape[1] - n_vec)))
    joined = jnp.concatenate([g_qkv.reshape(2 * dp, -1, g_qkv.shape[1]), vectors], axis=1)
    r_qkv = reduce_scatter(joined.reshape(-1, g_qkv.shape[1]), (1, 0) + tuple(range(2, dp_bits)), dp, dp_bits)
    r_vec = r_qkv[-8, :n_vec]
    r_qkv = r_qkv[:-8]
    dinput = dpre1 + jnp.einsum("te,de->td", dproj, w_qkv, preferred_element_type=F32)
    dinput = dinput.astype(BF).reshape(rows, length, width)
    return (
        spread_rows(output),
        cls,
        spread_rows(dinput),
        r_qkv.reshape(-1),
        r_out.reshape(-1),
        r_in.reshape(-1),
        r_back.reshape(-1),
        r_vec,
    )


def solution(mesh):
    row = P("dp", "seq", None)
    both = P(("dp", "seq"))
    return jax.shard_map(
        on_device,
        mesh=mesh,
        in_specs=(row, P("dp", None)) + (P(),) * 13 + (row,),
        out_specs=(row, P("dp", None, None), row, both, both, both, both, both),
        check_vma=False,
    )
```

```python
from functools import partial

import jax
import jax.numpy as jnp
from jax import lax
from jax.experimental import pallas as pl
from jax.experimental.pallas import tpu as pltpu
from jax.sharding import PartitionSpec as P

HEADS = 12
EPS = 1e-12
BF = jnp.bfloat16
F32 = jnp.float32
VMEM_LIMIT = 60 << 20
RSQRT2 = 0.7071067811865476
RSQRT2PI = 0.3989422804014327


def row_dot(left, right):
    return lax.dot_general(left, right, (((1,), (0,)), ((), ())), preferred_element_type=F32)


def row_dot_t(left, right):
    return lax.dot_general(left, right, (((1,), (1,)), ((), ())), preferred_element_type=F32)


def col_dot(left, right):
    return lax.dot_general(left, right, (((0,), (0,)), ((), ())), preferred_element_type=F32)


def gelu_pair(value):
    expo = jnp.exp(value * value * -0.5)
    t = 1.0 / (1.0 + (0.3275911 * RSQRT2) * jnp.abs(value))
    poly = t * (0.5 * 0.254829592 + t * (0.5 * -0.284496736 + t * (0.5 * 1.421413741 + t * (0.5 * -1.453152027 + t * (0.5 * 1.061405429)))))
    tail = poly * expo
    phi = jnp.where(value < 0.0, tail, 1.0 - tail)
    return value * phi, phi + value * expo * RSQRT2PI


def forward_kernel(
    core_ref, len_ref, own_ref, other_ref, cot_own_ref, cot_other_ref, wqkv_hbm, wout_hbm, win_hbm, wback_hbm,
    bq_ref, bv_ref, bo_ref, g1_ref, s1_ref, bi_ref, bb_ref, g2_ref, s2_ref,
    qkv_ref, probs_hbm, mixed_ref, low_ref, hat1_ref, inv1_ref, act_ref, slope_ref, out_ref, out_other_ref, cls_ref, dfeed_ref,
    gg2_ref, gs2_ref, gbb_ref,
    x_ref, cot_ref, bias_ref, normed_ref, acc_ref, outf_ref, wqkv_ref, wout_ref, win_ref, wback_ref, p_ref, w_sem, p_sem,
):
    step = pl.program_id(0)
    core = core_ref[0]
    rows = pl.num_programs(0)
    half, width = own_ref.shape[1:]
    length = 2 * half
    pairs = width // 128
    block = 256
    hidden = win_ref.shape[1]
    chunk = 512

    copies = [
        pltpu.make_async_copy(src, dst, w_sem.at[i])
        for i, (src, dst) in enumerate(
            ((wqkv_hbm, wqkv_ref), (wout_hbm, wout_ref), (win_hbm, win_ref), (wback_hbm, wback_ref))
        )
    ]

    @pl.when(step == 0)
    def _():
        for copy in copies:
            copy.start()
        gg2_ref[...] = jnp.zeros_like(gg2_ref)
        gs2_ref[...] = jnp.zeros_like(gs2_ref)
        gbb_ref[...] = jnp.zeros_like(gbb_ref)

    own_at = pl.multiple_of(core * half, half)
    other_at = pl.multiple_of((1 - core) * half, half)
    x_ref[pl.ds(own_at, half), :] = own_ref[0]
    x_ref[pl.ds(other_at, half), :] = other_ref[0]
    cot_ref[pl.ds(own_at, half), :] = cot_own_ref[0]
    cot_ref[pl.ds(other_at, half), :] = cot_other_ref[0]

    row = core * rows + step
    count = len_ref.shape[1]
    starts = [jnp.int32(0)]
    for j in range(count - 1):
        starts.append(starts[-1] + len_ref[row, j])
    down = lax.broadcasted_iota(jnp.int32, (length, 1), 0)
    across = lax.broadcasted_iota(jnp.int32, (1, length), 1)
    seg_down = jnp.zeros((length, 1), jnp.int32)
    seg_across = jnp.zeros((1, length), jnp.int32)
    for j in range(1, count):
        seg_down += (down >= starts[j]).astype(jnp.int32)
        seg_across += (across >= starts[j]).astype(jnp.int32)
    bias_ref[...] = jnp.where(seg_down == seg_across, 0.0, -1e30)

    @pl.when(step == 0)
    def _():
        copies[0].wait()

    for n in range(3):
        part = row_dot(x_ref[...], wqkv_ref[:, n * width : (n + 1) * width])
        if n == 0:
            part = (part + bq_ref[...]) * (width // HEADS) ** -0.5
        if n == 2:
            part = part + bv_ref[...]
        qkv_ref[0, :, n * width : (n + 1) * width] = part.astype(BF)

    lane = lax.broadcasted_iota(jnp.int32, (1, 128), 1)
    first = lane < 64

    def pair_body(pair, carry):
        slot = lax.rem(pair, 2)
        out_copy = pltpu.make_async_copy(p_ref.at[slot], probs_hbm.at[step, pair], p_sem.at[slot])

        @pl.when(pair >= 2)
        def _():
            out_copy.wait()

        q_at = pl.multiple_of(pair * 128, 128)
        k_pair = qkv_ref[0, :, pl.ds(pl.multiple_of(width + pair * 128, 128), 128)]
        v_pair = qkv_ref[0, :, pl.ds(pl.multiple_of(2 * width + pair * 128, 128), 128)]
        for b in range(length // block):
            q_pair = qkv_ref[0, b * block : (b + 1) * block, pl.ds(q_at, 128)]
            outs = []
            for h in range(2):
                q_one = jnp.where(first if h == 0 else jnp.logical_not(first), q_pair, jnp.zeros_like(q_pair))
                s = row_dot_t(q_one, k_pair) + bias_ref[b * block : (b + 1) * block, :]
                e = jnp.exp(s - jnp.max(s, axis=-1, keepdims=True))
                p = (e * (1.0 / jnp.sum(e, axis=-1, keepdims=True))).astype(BF)
                p_ref[slot, h, b * block : (b + 1) * block, :] = p
                outs.append(row_dot(p, v_pair))
            mixed_ref[0, b * block : (b + 1) * block, pl.ds(q_at, 128)] = jnp.where(first, outs[0], outs[1]).astype(BF)
        out_copy.start()
        return carry

    lax.fori_loop(0, pairs, pair_body, 0)
    for tail in (pairs - 2, pairs - 1):
        pltpu.make_async_copy(p_ref.at[tail % 2], probs_hbm.at[step, tail], p_sem.at[tail % 2]).wait()

    @pl.when(step == 0)
    def _():
        for copy in copies[1:]:
            copy.wait()

    def token_body(b, carry):
        at = pl.ds(pl.multiple_of(b * block, block), block)
        pre = x_ref[at, :].astype(F32) + row_dot(mixed_ref[0, at, :], wout_ref[...]) + bo_ref[...]
        center = pre - jnp.mean(pre, axis=-1, keepdims=True)
        inv = lax.rsqrt(jnp.mean(center * center, axis=-1, keepdims=True) + EPS)
        hat = center * inv
        hat1_ref[0, at, :] = hat.astype(BF)
        inv1_ref[0, at, :] = inv
        normed = hat * g1_ref[...] + s1_ref[...]
        normed_ref[...] = normed + bb_ref[...]
        low_ref[0, at, :] = normed.astype(BF)
        for c in range(hidden // chunk):
            cols = slice(c * chunk, (c + 1) * chunk)
            inner = row_dot(low_ref[0, at, :], win_ref[:, cols]) + bi_ref[:, cols]
            act, slope = gelu_pair(inner)
            act_ref[0, at, cols] = act.astype(BF)
            slope_ref[0, at, cols] = slope.astype(BF)
        pre = normed_ref[...] + row_dot(act_ref[0, at, :], wback_ref[...])
        center = pre - jnp.mean(pre, axis=-1, keepdims=True)
        inv = lax.rsqrt(jnp.mean(center * center, axis=-1, keepdims=True) + EPS)
        hat = center * inv
        outf_ref[at, :] = (hat * g2_ref[...] + s2_ref[...]).astype(BF)
        dy = cot_ref[at, :].astype(F32)
        gg2_ref[...] += jnp.sum(dy * hat, axis=0, keepdims=True)
        gs2_ref[...] += jnp.sum(dy, axis=0, keepdims=True)
        g = dy * g2_ref[...]
        dpre = inv * (g - jnp.mean(g, axis=-1, keepdims=True) - hat * jnp.mean(g * hat, axis=-1, keepdims=True))
        dfeed = dpre.astype(BF)
        dfeed_ref[0, at, :] = dfeed
        gbb_ref[...] += jnp.sum(dfeed.astype(F32), axis=0, keepdims=True)
        return carry

    lax.fori_loop(0, length // block, token_body, 0)
    out_ref[0] = outf_ref[pl.ds(own_at, half), :]
    out_other_ref[0] = outf_ref[pl.ds(other_at, half), :]
    which = lax.broadcasted_iota(jnp.int32, (8, 1), 0)
    start_down = jnp.full((8, 1), -1, jnp.int32)
    for j in range(count):
        start_down = jnp.where(which == j, starts[j], start_down)
    choose = (start_down == across).astype(F32).astype(BF)
    cls_ref[0] = row_dot(choose, outf_ref[...]).astype(BF)


def whole(shape):
    return pl.BlockSpec(shape, lambda *_: (0,) * len(shape))


ANY = pl.BlockSpec(memory_space=pl.ANY)


def forward_call(core, lengths, tokens, other, cot, cot_other, weights, vectors):
    rows_local, half, width = tokens.shape
    rows = rows_local // 2
    length = 2 * half
    hidden = weights[2].shape[1]
    own_row = pl.BlockSpec((1, half, width), lambda r, core, lens: (core[0] * rows + r, 0, 0))
    plain_row = pl.BlockSpec((1, half, width), lambda r, *_: (r, 0, 0))

    def full(n):
        return pl.BlockSpec((1, length, n), lambda r, *_: (r, 0, 0))

    shapes = [
        jax.ShapeDtypeStruct((rows, length, 3 * width), BF),
        jax.ShapeDtypeStruct((rows, HEADS // 2, 2, length, length), BF),
        jax.ShapeDtypeStruct((rows, length, width), BF),
        jax.ShapeDtypeStruct((rows, length, width), BF),
        jax.ShapeDtypeStruct((rows, length, width), BF),
        jax.ShapeDtypeStruct((rows, length, 1), F32),
        jax.ShapeDtypeStruct((rows, length, hidden), BF),
        jax.ShapeDtypeStruct((rows, length, hidden), BF),
        jax.ShapeDtypeStruct((rows_local, half, width), BF),
        jax.ShapeDtypeStruct((rows, half, width), BF),
        jax.ShapeDtypeStruct((rows, 8, width), BF),
        jax.ShapeDtypeStruct((rows, length, width), BF),
    ] + [jax.ShapeDtypeStruct((1, width), F32)] * 3
    out_specs = [full(3 * width), ANY, full(width), full(width), full(width), full(1), full(hidden), full(hidden), own_row, plain_row,
                 pl.BlockSpec((1, 8, width), lambda r, *_: (r, 0, 0)), full(width)] + [whole((1, width))] * 3
    flops = 2 * rows * length * width * (3 * width + width + 2 * hidden) + 4 * rows * length * length * width
    return pl.pallas_call(
        forward_kernel,
        name="forward_rows",
        out_shape=shapes,
        grid_spec=pltpu.PrefetchScalarGridSpec(
            num_scalar_prefetch=2,
            grid=(rows,),
            in_specs=[own_row, plain_row, own_row, plain_row, ANY, ANY, ANY, ANY] + [whole(v.shape) for v in vectors],
            out_specs=out_specs,
            scratch_shapes=[
                pltpu.VMEM((length, width), BF),
                pltpu.VMEM((length, width), BF),
                pltpu.VMEM((length, length), F32),
                pltpu.VMEM((256, width), F32),
                pltpu.VMEM((8, 128), F32),
                pltpu.VMEM((length, width), BF),
            ]
            + [pltpu.VMEM(w.shape, BF) for w in weights]
            + [pltpu.VMEM((2, 2, length, length), BF), pltpu.SemaphoreType.DMA((4,)), pltpu.SemaphoreType.DMA((2,))],
        ),
        compiler_params=pltpu.CompilerParams(vmem_limit_bytes=VMEM_LIMIT),
        cost_estimate=pl.CostEstimate(flops=flops, bytes_accessed=50 << 20, transcendentals=rows * length * hidden * 2),
    )(core, lengths, tokens, other, cot, cot_other, *weights, *vectors)


def weight_grad(left, right, block_m, block_n, name):
    total, m = left.shape
    n = right.shape[1]

    def body(l_ref, r_ref, o_ref, t_ref):
        @pl.when(pl.program_id(1) == 0)
        def _():
            t_ref[...] = l_ref[...].T

        o_ref[...] = row_dot(t_ref[...], r_ref[...]).astype(BF)

    return pl.pallas_call(
        body,
        name=name,
        out_shape=jax.ShapeDtypeStruct((m, n), BF),
        grid=(m // block_m, n // block_n),
        in_specs=[pl.BlockSpec((total, block_m), lambda i, j: (0, i)), pl.BlockSpec((total, block_n), lambda i, j: (0, j))],
        out_specs=pl.BlockSpec((block_m, block_n), lambda i, j: (i, j)),
        scratch_shapes=[pltpu.VMEM((block_m, total), BF)],
        compiler_params=pltpu.CompilerParams(vmem_limit_bytes=VMEM_LIMIT),
        cost_estimate=pl.CostEstimate(flops=2 * total * m * n, bytes_accessed=2 * (total * (m + n) + m * n), transcendentals=0),
    )(left, right)


def inner_grad(dfeed, slope, w_back):
    total, width = dfeed.shape
    hidden = slope.shape[1]
    block = 512

    def body(d_ref, s_ref, w_ref, o_ref, b_ref):
        value = (row_dot_t(d_ref[...], w_ref[...]) * s_ref[...].astype(F32)).astype(BF)
        o_ref[...] = value
        b_ref[...] = jnp.sum(value.astype(F32), axis=0, keepdims=True)

    return pl.pallas_call(
        body,
        name="inner_grad",
        out_shape=[jax.ShapeDtypeStruct((total, hidden), BF), jax.ShapeDtypeStruct((1, hidden), F32)],
        grid=(hidden // block,),
        in_specs=[whole((total, width)), pl.BlockSpec((total, block), lambda j: (0, j)), pl.BlockSpec((block, width), lambda j: (j, 0))],
        out_specs=[pl.BlockSpec((total, block), lambda j: (0, j)), pl.BlockSpec((1, block), lambda j: (0, j))],
        compiler_params=pltpu.CompilerParams(vmem_limit_bytes=VMEM_LIMIT),
        cost_estimate=pl.CostEstimate(flops=2 * total * width * hidden, bytes_accessed=20 << 20, transcendentals=0),
    )(dfeed, slope, w_back)


def branch_grad(dinner, dfeed, hat1, inv1, w_in, w_out, gain1):
    total, width = dfeed.shape
    hidden = dinner.shape[1]
    block = 256

    def body(i_ref, f_ref, h_ref, v_ref, wi_ref, wo_ref, g_ref, branch_ref, mixed_ref, gg_ref, gs_ref, gb_ref):
        @pl.when(pl.program_id(0) == 0)
        def _():
            gg_ref[...] = jnp.zeros_like(gg_ref)
            gs_ref[...] = jnp.zeros_like(gs_ref)
            gb_ref[...] = jnp.zeros_like(gb_ref)

        dn = f_ref[...].astype(F32) + row_dot_t(i_ref[...], wi_ref[...])
        hat = h_ref[...].astype(F32)
        gg_ref[...] += jnp.sum(dn * hat, axis=0, keepdims=True)
        gs_ref[...] += jnp.sum(dn, axis=0, keepdims=True)
        g = dn * g_ref[...]
        dpre = v_ref[...] * (g - jnp.mean(g, axis=-1, keepdims=True) - hat * jnp.mean(g * hat, axis=-1, keepdims=True))
        branch = dpre.astype(BF)
        branch_ref[...] = branch
        gb_ref[...] += jnp.sum(branch.astype(F32), axis=0, keepdims=True)
        mixed_ref[...] = row_dot_t(branch, wo_ref[...]).astype(BF)

    def rows(n):
        return pl.BlockSpec((block, n), lambda i: (i, 0))

    one = jax.ShapeDtypeStruct((1, width), F32)
    return pl.pallas_call(
        body,
        name="branch_grad",
        out_shape=[jax.ShapeDtypeStruct((total, width), BF), jax.ShapeDtypeStruct((total, width), BF), one, one, one],
        grid=(total // block,),
        in_specs=[rows(hidden), rows(width), rows(width), rows(1), whole(w_in.shape), whole(w_out.shape), whole(gain1.shape)],
        out_specs=[rows(width), rows(width)] + [whole((1, width))] * 3,
        compiler_params=pltpu.CompilerParams(vmem_limit_bytes=VMEM_LIMIT),
        cost_estimate=pl.CostEstimate(flops=2 * total * width * (hidden + width), bytes_accessed=20 << 20, transcendentals=0),
    )(dinner, dfeed, hat1, inv1, w_in, w_out, gain1)


def attention_grad(qkv, probs, mixed, dmixed):
    rows, length, width = mixed.shape
    pairs = width // 128
    scale = (width // HEADS) ** -0.5

    def body(q_ref, k_ref, v_ref, p_ref, m_ref, d_ref, dq_ref, dk_ref, dv_ref, bq_ref, bv_ref):
        @pl.when(pl.program_id(1) == 0)
        def _():
            bq_ref[...] = jnp.zeros_like(bq_ref)
            bv_ref[...] = jnp.zeros_like(bv_ref)

        lane = lax.broadcasted_iota(jnp.int32, (1, 128), 1)
        first = lane < 64
        q, k, v, d = q_ref[0], k_ref[0], v_ref[0], d_ref[0]
        product = d.astype(F32) * m_ref[0].astype(F32)
        q_t, d_t = q.T, d.T
        dqs, dks, dvs = [], [], []
        for h in range(2):
            on = first if h == 0 else jnp.logical_not(first)
            delta = jnp.sum(jnp.where(on, product, 0.0), axis=-1, keepdims=True)
            dprobs = row_dot_t(jnp.where(on, d, jnp.zeros_like(d)), v)
            p = p_ref[0, 0, h]
            ds = (p.astype(F32) * (dprobs - delta)).astype(BF)
            dqs.append(row_dot(ds, k))
            half = slice(h * 64, (h + 1) * 64)
            dks.append(row_dot(q_t[half], ds))
            dvs.append(row_dot(d_t[half], p))
        dq = (jnp.where(first, dqs[0], dqs[1]) * scale).astype(BF)
        dk = jnp.concatenate(dks, axis=0).T.astype(BF)
        dv = jnp.concatenate(dvs, axis=0).T.astype(BF)
        dq_ref[0] = dq
        dk_ref[0] = dk
        dv_ref[0] = dv
        bq_ref[...] += jnp.sum(dq.astype(F32), axis=0, keepdims=True)
        bv_ref[...] += jnp.sum(dv.astype(F32), axis=0, keepdims=True)

    def cols(base):
        return pl.BlockSpec((1, length, 128), lambda p, r: (r, 0, base + p))

    vec = pl.BlockSpec((1, 128), lambda p, r: (0, p))
    out = jax.ShapeDtypeStruct((rows, length, width), BF)
    one = jax.ShapeDtypeStruct((1, width), F32)
    return pl.pallas_call(
        body,
        name="attention_grad",
        out_shape=[out, out, out, one, one],
        grid=(pairs, rows),
        in_specs=[cols(0), cols(pairs), cols(2 * pairs), pl.BlockSpec((1, 1, 2, length, length), lambda p, r: (r, p, 0, 0, 0)), cols(0), cols(0)],
        out_specs=[cols(0), cols(0), cols(0), vec, vec],
        compiler_params=pltpu.CompilerParams(vmem_limit_bytes=VMEM_LIMIT),
        cost_estimate=pl.CostEstimate(flops=8 * rows * length * length * width, bytes_accessed=30 << 20, transcendentals=0),
    )(qkv, qkv, qkv, probs, mixed, dmixed)


def input_grad_call(dq, dk, dv, dpre, w_qkv):
    total, width = dpre.shape
    block = 256

    def body(q_ref, k_ref, v_ref, d_ref, w_ref, o_ref):
        total = d_ref[...].astype(F32)
        for n, ref in enumerate((q_ref, k_ref, v_ref)):
            total = total + row_dot_t(ref[...], w_ref[:, n * width : (n + 1) * width])
        o_ref[...] = total.astype(BF)

    rows = pl.BlockSpec((block, width), lambda i: (i, 0))
    return pl.pallas_call(
        body,
        name="input_grad",
        out_shape=jax.ShapeDtypeStruct((total, width), BF),
        grid=(total // block,),
        in_specs=[rows, rows, rows, rows, whole(w_qkv.shape)],
        out_specs=rows,
        compiler_params=pltpu.CompilerParams(vmem_limit_bytes=VMEM_LIMIT),
        cost_estimate=pl.CostEstimate(flops=6 * total * width * width, bytes_accessed=10 << 20, transcendentals=0),
    )(dq, dk, dv, dpre, w_qkv)


def swap(value):
    return lax.ppermute(value, "seq", [(0, 1), (1, 0)])


def pick(value, index, axis):
    return lax.dynamic_index_in_dim(value, index, axis, keepdims=False)


def reduce_stages(part, order, dp_bits, dp):
    me = lax.axis_index("dp")
    n_halving = dp_bits - 2
    shape = part.shape[1:]
    current = part.reshape((2,) * dp_bits + shape)
    left = list(range(dp_bits - 1, -1, -1))
    for bit in order[:n_halving]:
        axis = left.index(bit)
        mine = (me >> bit) & 1
        pairs = [(i, i ^ (1 << bit)) for i in range(dp)]
        send = pick(current, 1 - mine, axis).astype(BF)
        got = lax.ppermute(send, "dp", pairs)
        keep = pick(current, mine, axis)
        current = (keep.astype(F32) + got.astype(F32)).astype(BF)
        left.remove(bit)
    high, low = left
    group = (((me >> high) & 1) << 1) | ((me >> low) & 1)
    current = current.reshape((4,) + shape)
    total = pick(current, group, 0).astype(F32)
    for other in (1, 2, 3):
        flip = ((other >> 1) << high) | ((other & 1) << low)
        pairs = [(i, i ^ flip) for i in range(dp)]
        send = pick(current, group ^ other, 0).astype(BF)
        total = total + lax.ppermute(send, "dp", pairs).astype(F32)
    return total


def reduce_scatter(grad, order, dp, dp_bits):
    core = lax.axis_index("seq")
    rows = grad.shape[0] // (2 * dp)
    blocks = grad.reshape(dp, 2, rows, grad.shape[1])
    send = pick(blocks, 1 - core, 1).astype(BF)
    keep = pick(blocks, core, 1)
    part = (keep.astype(F32) + swap(send).astype(F32)).astype(BF)
    return reduce_stages(part, order, dp_bits, dp)


def on_device(tokens, lengths, w_qkv, w_out, w_in, w_back, bias_q, value_bias, bias_out, gain1, shift1, bias_in, bias_back, gain2, shift2, cotangent):
    rows_local, half, width = tokens.shape
    dp = lax.axis_size("dp")
    dp_bits = dp.bit_length() - 1
    core = lax.axis_index("seq")
    rows = rows_local // 2
    length = 2 * half
    total = rows * length
    order_a = (0, 1) + tuple(range(2, dp_bits))
    order_b = (1, 0) + tuple(range(2, dp_bits))

    def send_rows(value):
        return swap(lax.dynamic_slice_in_dim(value, (1 - core) * rows, rows, 0))

    other = send_rows(tokens)
    cot_other = send_rows(cotangent)
    vectors = [v.reshape(1, -1) for v in (bias_q, value_bias, bias_out, gain1, shift1, bias_in, bias_back, gain2, shift2)]
    (qkv, probs, mixed, low, hat1, inv1, act, slope, output, output_other, cls_own, dfeed, g_gain2, g_shift2, g_bias_back) = forward_call(
        core.reshape(1).astype(jnp.int32), lengths, tokens, other, cotangent, cot_other, (w_qkv, w_out, w_in, w_back), vectors
    )

    def flat(value):
        return value.reshape(total, value.shape[-1])

    g_back = weight_grad(flat(act), flat(dfeed), 512, width, "grad_back")
    r_back = reduce_scatter(g_back, order_a, dp, dp_bits)
    dinner, g_bias_in = inner_grad(flat(dfeed), flat(slope), w_back)
    g_in = weight_grad(flat(low), dinner, width, 512, "grad_in")
    r_in = reduce_scatter(g_in, order_b, dp, dp_bits)
    dpre1, dmixed, g_gain1, g_shift1, g_bias_out = branch_grad(dinner, flat(dfeed), flat(hat1), flat(inv1), w_in, w_out, vectors[3])
    g_out = weight_grad(flat(mixed), dpre1, width, width, "grad_out")
    r_out = reduce_scatter(g_out, order_a, dp, dp_bits)
    dq, dk, dv, g_bias_q, g_bias_v = attention_grad(qkv, probs, mixed, dmixed.reshape(rows, length, width))

    own_first = tokens_global = None
    own = lax.dynamic_slice_in_dim(tokens, core * rows, rows, 0)
    front = jnp.where(core == 0, own, other)
    rear = jnp.where(core == 0, other, own)
    full_tokens = jnp.concatenate([front, rear], axis=1).reshape(total, width)
    g_parts = [weight_grad(full_tokens, flat(d), width, width, "grad_qkv") for d in (dq, dk, dv)]
    g_qkv = jnp.concatenate(g_parts, axis=1)
    vector_parts = [g_bias_q, g_bias_v, g_bias_out, g_gain1, g_shift1, g_bias_in, g_bias_back, g_gain2, g_shift2]
    joined = jnp.concatenate([v.reshape(-1) for v in vector_parts]).reshape(2 * dp, 1, -1)
    n_vec = joined.shape[-1]
    joined = jnp.pad(joined, ((0, 0), (0, 7), (0, g_qkv.shape[1] - n_vec))).astype(BF)
    joined = jnp.concatenate([g_qkv.reshape(2 * dp, -1, g_qkv.shape[1]), joined], axis=1)
    r_qkv = reduce_scatter(joined.reshape(-1, g_qkv.shape[1]), order_b, dp, dp_bits)
    r_vec = r_qkv[-8, :n_vec]
    r_qkv = r_qkv[:-8]
    dinput = input_grad_call(flat(dq), flat(dk), flat(dv), dpre1, w_qkv).reshape(rows, length, width)

    out_got = swap(output_other)
    output = lax.dynamic_update_slice_in_dim(output, out_got, (1 - core) * rows, 0)
    count = lengths.shape[1]
    cls_own = cls_own[:, :count]
    cls_got = swap(cls_own)
    cls = jnp.where(core == 0, jnp.concatenate([cls_own, cls_got], axis=0), jnp.concatenate([cls_got, cls_own], axis=0))
    in_own = lax.dynamic_slice_in_dim(dinput, core * half, half, 1)
    in_got = swap(lax.dynamic_slice_in_dim(dinput, (1 - core) * half, half, 1))
    input_grad = jnp.where(core == 0, jnp.concatenate([in_own, in_got], axis=0), jnp.concatenate([in_got, in_own], axis=0))
    return (
        output,
        cls,
        input_grad,
        r_qkv.reshape(-1),
        r_out.reshape(-1),
        r_in.reshape(-1),
        r_back.reshape(-1),
        r_vec,
    )


def solution(mesh):
    row = P("dp", "seq", None)
    both = P(("dp", "seq"))
    return jax.shard_map(
        on_device,
        mesh=mesh,
        in_specs=(row, P("dp", None)) + (P(),) * 13 + (row,),
        out_specs=(row, P("dp", None, None), row, both, both, both, both, both),
        check_vma=False,
    )
```

```python
from functools import partial

import jax
import jax.numpy as jnp
from jax import lax
from jax.experimental import pallas as pl
from jax.experimental.pallas import tpu as pltpu
from jax.sharding import PartitionSpec as P

HEADS = 12
EPS = 1e-12
BF = jnp.bfloat16
F32 = jnp.float32
VMEM_LIMIT = 60 << 20
RSQRT2 = 0.7071067811865476
RSQRT2PI = 0.3989422804014327


def row_dot(left, right):
    return lax.dot_general(left, right, (((1,), (0,)), ((), ())), preferred_element_type=F32)


def row_dot_t(left, right):
    return lax.dot_general(left, right, (((1,), (1,)), ((), ())), preferred_element_type=F32)


def col_dot(left, right):
    return lax.dot_general(left, right, (((0,), (0,)), ((), ())), preferred_element_type=F32)


def gelu_pair(value):
    expo = jnp.exp(value * value * -0.5)
    phi = 0.5 + 0.5 * lax.erf(value * RSQRT2)
    return value * phi, phi + value * expo * RSQRT2PI


def whole(shape):
    return pl.BlockSpec(shape, lambda *_: (0,) * len(shape))


ANY = pl.BlockSpec(memory_space=pl.ANY)
HBM = pl.BlockSpec(memory_space=pltpu.HBM)


def params(mib):
    return pltpu.CompilerParams(vmem_limit_bytes=mib << 20)


def row_starts(len_ref, row):
    starts = [jnp.int32(0)]
    for j in range(len_ref.shape[1] - 1):
        starts.append(starts[-1] + len_ref[row, j])
    return starts


def attention_kernel(
    core_ref, len_ref, own_ref, other_ref, wqkv_hbm, wout_hbm, bq_ref, bv_ref, bo_ref, g1_ref, s1_ref,
    qkv_hbm, probs_hbm, x_ref, mixed_ref, low_ref, hat1_ref, inv1_ref, scale_ref,
    bias_ref, qkv_ref, wqkv_ref, wout_ref, p_ref, w_sem, p_sem, q_sem,
):
    step = pl.program_id(0)
    core = core_ref[0]
    rows = pl.num_programs(0)
    half, width = own_ref.shape[1:]
    length = 2 * half
    pairs = width // 128
    parts = [slice(n * width, (n + 1) * width) for n in range(3)]
    copies = [pltpu.make_async_copy(wqkv_hbm.at[:, part], wqkv_ref.at[:, part], w_sem.at[n]) for n, part in enumerate(parts)]
    copies.append(pltpu.make_async_copy(wout_hbm, wout_ref, w_sem.at[3]))

    @pl.when(step == 0)
    def _():
        for copy in copies:
            copy.start()

    x_ref[0, pl.ds(pl.multiple_of(core * half, half), half), :] = own_ref[0]
    x_ref[0, pl.ds(pl.multiple_of((1 - core) * half, half), half), :] = other_ref[0]
    starts = row_starts(len_ref, core * rows + step)
    down = lax.broadcasted_iota(jnp.int32, (length, 1), 0)
    across = lax.broadcasted_iota(jnp.int32, (1, length), 1)
    seg_down = jnp.zeros((length, 1), jnp.int32)
    seg_across = jnp.zeros((1, length), jnp.int32)
    for start in starts[1:]:
        seg_down += (down >= start).astype(jnp.int32)
        seg_across += (across >= start).astype(jnp.int32)
    bias_ref[...] = jnp.where(seg_down == seg_across, 0.0, -1e30)

    for n, part in enumerate(parts):
        @pl.when(step == 0)
        def _():
            copies[n].wait()

        value = row_dot(x_ref[0], wqkv_ref[:, part])
        if n == 0:
            value = (value + bq_ref[...]) * (width // HEADS) ** -0.5
        if n == 2:
            value = value + bv_ref[...]
        qkv_ref[:, part] = value.astype(BF)
    save = pltpu.make_async_copy(qkv_ref, qkv_hbm.at[step], q_sem)
    save.start()

    first = lax.broadcasted_iota(jnp.int32, (1, 128), 1) < 64

    def pair_body(pair, carry):
        slot = lax.rem(pair, 2)
        out_copy = pltpu.make_async_copy(p_ref.at[slot], probs_hbm.at[step, pair], p_sem.at[slot])

        @pl.when(pair >= 2)
        def _():
            out_copy.wait()

        at = pl.ds(pl.multiple_of(pair * 128, 128), 128)
        q_pair = qkv_ref[:, at]
        k_pair = qkv_ref[:, pl.ds(pl.multiple_of(width + pair * 128, 128), 128)]
        v_pair = qkv_ref[:, pl.ds(pl.multiple_of(2 * width + pair * 128, 128), 128)]
        outs = []
        for h in range(2):
            on = first if h == 0 else jnp.logical_not(first)
            s = row_dot_t(jnp.where(on, q_pair, jnp.zeros_like(q_pair)), k_pair) + bias_ref[...]
            e = jnp.exp(s - jnp.max(s, axis=-1, keepdims=True)).astype(BF)
            p_ref[slot, h] = e
            outs.append(row_dot(e, jnp.where(on, v_pair, jnp.ones_like(v_pair))))
        sums = pltpu.roll(jnp.where(first, outs[1], outs[0]), 64, 1)
        inverse = 1.0 / sums
        scale_ref[0, :, at] = inverse
        mixed_ref[0, :, at] = (jnp.where(first, outs[0], outs[1]) * inverse).astype(BF)
        out_copy.start()
        return carry

    lax.fori_loop(0, pairs, pair_body, 0)
    for tail in (pairs - 2, pairs - 1):
        pltpu.make_async_copy(p_ref.at[tail % 2], probs_hbm.at[step, tail], p_sem.at[tail % 2]).wait()

    @pl.when(step == 0)
    def _():
        copies[3].wait()

    pre = x_ref[0].astype(F32) + row_dot(mixed_ref[0], wout_ref[...]) + bo_ref[...]
    center = pre - jnp.mean(pre, axis=-1, keepdims=True)
    inv = lax.rsqrt(jnp.mean(center * center, axis=-1, keepdims=True) + EPS)
    hat = center * inv
    hat1_ref[0] = hat.astype(BF)
    inv1_ref[0] = inv
    low_ref[0] = (hat * g1_ref[...] + s1_ref[...]).astype(BF)
    save.wait()


def attention_call(core, lengths, tokens, other, w_qkv, w_out, vectors):
    rows_local, half, width = tokens.shape
    rows = rows_local // 2
    length = 2 * half
    pairs = width // 128

    def full(n):
        return pl.BlockSpec((1, length, n), lambda r, *_: (r, 0, 0))

    def row(n, kind=BF):
        return jax.ShapeDtypeStruct((rows, length, n), kind)

    return pl.pallas_call(
        attention_kernel,
        name="attention_rows",
        out_shape=[
            row(3 * width), jax.ShapeDtypeStruct((rows, pairs, 2, length, length), BF), row(width), row(width), row(width), row(width),
            row(1, F32), row(width, F32),
        ],
        grid_spec=pltpu.PrefetchScalarGridSpec(
            num_scalar_prefetch=2,
            grid=(rows,),
            in_specs=[
                pl.BlockSpec((1, half, width), lambda r, core, lens: (core[0] * rows + r, 0, 0)),
                pl.BlockSpec((1, half, width), lambda r, *_: (r, 0, 0)),
                ANY,
                ANY,
            ]
            + [whole(v.shape) for v in vectors],
            out_specs=[HBM, HBM] + [full(width)] * 4 + [full(1), full(width)],
            scratch_shapes=[
                pltpu.VMEM((length, length), F32),
                pltpu.VMEM((length, 3 * width), BF),
                pltpu.VMEM(w_qkv.shape, BF),
                pltpu.VMEM(w_out.shape, BF),
                pltpu.VMEM((2, 2, length, length), BF),
                pltpu.SemaphoreType.DMA((4,)),
                pltpu.SemaphoreType.DMA((2,)),
                pltpu.SemaphoreType.DMA,
            ],
        ),
        compiler_params=params(54),
        cost_estimate=pl.CostEstimate(
            flops=8 * rows * length * width * width + 4 * rows * length * length * width,
            bytes_accessed=35 << 20,
            transcendentals=rows * HEADS * length * length,
        ),
    )(core, lengths, tokens, other, w_qkv, w_out, *vectors)


def feed_forward_kernel(
    split, rows, core_ref, len_ref, low_ref, win_ref, wback_ref, bi_ref, bb_ref, g2_ref, s2_ref, cot_hbm, cot_other_hbm,
    slope_ref, out_hbm, other_hbm, cls_ref, dfeed_ref, gg_ref, gs_ref, gb_ref, *rest
):
    if split:
        keep_ref, send_ref, act_ref, acc_ref, cot_ref, out_ref, grad_ref, c_sem, o_sem = rest
    else:
        act_hbm, act_ref, acc_ref, cot_ref, out_ref, c_sem, o_sem = rest
    step = pl.program_id(0)
    core = core_ref[0]
    total, width = low_ref.shape
    group, length = cot_ref.shape[:2]
    half = length // 2
    own_at = pl.ds(pl.multiple_of(core * half, half), half)
    other_at = pl.ds(pl.multiple_of((1 - core) * half, half), half)
    chunk = win_ref.shape[1]
    chunks = act_ref.shape[1] // chunk
    loads, stores = [], []
    for r in range(group):
        loads.append(pltpu.make_async_copy(cot_hbm.at[core * group + r], cot_ref.at[r, own_at], c_sem.at[r]))
        loads.append(pltpu.make_async_copy(cot_other_hbm.at[r], cot_ref.at[r, other_at], c_sem.at[group + r]))
        stores.append(pltpu.make_async_copy(out_ref.at[r, other_at], other_hbm.at[r], o_sem.at[group + r]))
        stores.append(pltpu.make_async_copy(out_ref.at[r, own_at], out_hbm.at[core * group + r], o_sem.at[r]))

    @pl.when(step == 0)
    def _():
        for load in loads:
            load.start()

    @pl.when(step < chunks)
    def _():
        base = pl.multiple_of(step * chunk, chunk)
        piece = 256
        for n in range(chunk // piece):
            cols = slice(n * piece, (n + 1) * piece)
            inner = row_dot(low_ref[...], win_ref[:, cols]) + bi_ref[:, cols]
            act, slope = gelu_pair(inner)
            act_ref[:, pl.ds(base + n * piece, piece)] = act.astype(BF)
            slope_ref[:, cols] = slope.astype(BF)
        value = row_dot(act_ref[:, pl.ds(base, chunk)], wback_ref[...])

        @pl.when(step == 0)
        def _():
            acc_ref[...] = value + bb_ref[...]

        @pl.when(step > 0)
        def _():
            acc_ref[...] += value

    @pl.when(step == chunks - 1)
    def _():
        for load in loads:
            load.wait()
        gg_ref[...] = jnp.zeros_like(gg_ref)
        gs_ref[...] = jnp.zeros_like(gs_ref)
        gb_ref[...] = jnp.zeros_like(gb_ref)
        block = 256
        per = length // block

        def token_body(i, carry):
            at = pl.ds(pl.multiple_of(i * block, block), block)
            row = lax.div(i, per)
            inside = pl.ds(pl.multiple_of(lax.rem(i, per) * block, block), block)
            pre = low_ref[at, :].astype(F32) + acc_ref[at, :]
            center = pre - jnp.mean(pre, axis=-1, keepdims=True)
            inv = lax.rsqrt(jnp.mean(center * center, axis=-1, keepdims=True) + EPS)
            hat = center * inv
            out_ref[row, inside, :] = (hat * g2_ref[...] + s2_ref[...]).astype(BF)
            dy = cot_ref[row, inside, :].astype(F32)
            gg_ref[...] += jnp.sum(dy * hat, axis=0, keepdims=True)
            gs_ref[...] += jnp.sum(dy, axis=0, keepdims=True)
            g = dy * g2_ref[...]
            dpre = inv * (g - jnp.mean(g, axis=-1, keepdims=True) - hat * jnp.mean(g * hat, axis=-1, keepdims=True))
            dfeed = dpre.astype(BF)
            dfeed_ref[at, :] = dfeed
            gb_ref[...] += jnp.sum(dfeed.astype(F32), axis=0, keepdims=True)
            return carry

        lax.fori_loop(0, total // block, token_body, 0)
        for store in stores:
            store.start()
        which = lax.broadcasted_iota(jnp.int32, (8, 1), 0)
        across = lax.broadcasted_iota(jnp.int32, (1, length), 1)
        for r in range(group):
            down = jnp.full((8, 1), -1, jnp.int32)
            for j, start in enumerate(row_starts(len_ref, core * group + r)):
                down = jnp.where(which == j, start, down)
            cls_ref[r] = row_dot((down == across).astype(F32).astype(BF), out_ref[r]).astype(BF)
        if not split:
            save = pltpu.make_async_copy(act_ref, act_hbm, o_sem.at[2 * group])
            save.start()
            save.wait()
            for store in stores:
                store.wait()

    if split:
        @pl.when(step >= chunks)
        def _():
            at = pl.ds(pl.multiple_of((step - chunks) * grad_ref.shape[0], 128), grad_ref.shape[0])
            grad_ref[...] = col_dot(act_ref[:, at], dfeed_ref[...])
            split_store(grad_ref, keep_ref, send_ref, core, rows, width // LANES)

        @pl.when(step == pl.num_programs(0) - 1)
        def _():
            for store in stores:
                store.wait()


def feed_forward_call(core, lengths, low, w_in, w_back, vectors, cot, cot_other, dp, split):
    total, width = low.shape
    rows_local, half, _ = cot.shape
    group = rows_local // 2
    length = 2 * half
    hidden = w_in.shape[1]
    chunk = width
    chunks = hidden // chunk
    rows = hidden // (2 * dp)
    bias_in, bias_back, gain2, shift2 = vectors

    def at(j):
        return jnp.minimum(j, chunks - 1)

    one = jax.ShapeDtypeStruct((1, width), F32)
    shapes = [
        jax.ShapeDtypeStruct((total, hidden), BF),
        jax.ShapeDtypeStruct(cot.shape, BF),
        jax.ShapeDtypeStruct(cot_other.shape, BF),
        jax.ShapeDtypeStruct((group, 8, width), BF),
        jax.ShapeDtypeStruct((total, width), BF),
        one,
        one,
        one,
    ]
    specs = [pl.BlockSpec((total, chunk), lambda j, *_: (0, at(j))), HBM, HBM, whole((group, 8, width)), whole((total, width))] + [whole((1, width))] * 3
    scratch = [
        pltpu.VMEM((total, hidden), BF),
        pltpu.VMEM((total, width), F32),
        pltpu.VMEM((group, length, width), BF),
        pltpu.VMEM((group, length, width), BF),
    ]
    if split:
        devices = 4
        half_shape = jax.ShapeDtypeStruct((width // LANES, dp, rows, LANES), BF)
        half_spec = pl.BlockSpec((width // LANES, devices, rows, LANES), lambda j, *_: (0, jnp.maximum(j - chunks, 0), 0, 0))
        shapes += [half_shape] * 2
        specs += [half_spec] * 2
        scratch.append(pltpu.VMEM((devices * 2 * rows, width), F32))
        steps = chunks + dp // devices
    else:
        shapes.append(jax.ShapeDtypeStruct((total, hidden), BF))
        specs.append(HBM)
        steps = chunks
    scratch += [pltpu.SemaphoreType.DMA((2 * group,)), pltpu.SemaphoreType.DMA((2 * group + 1,))]
    return pl.pallas_call(
        partial(feed_forward_kernel, split, rows),
        name="feed_forward",
        out_shape=shapes,
        grid_spec=pltpu.PrefetchScalarGridSpec(
            num_scalar_prefetch=2,
            grid=(steps,),
            in_specs=[
                whole((total, width)),
                pl.BlockSpec((width, chunk), lambda j, *_: (0, at(j))),
                pl.BlockSpec((chunk, width), lambda j, *_: (at(j), 0)),
                pl.BlockSpec((1, chunk), lambda j, *_: (0, at(j))),
                whole((width,)),
                whole((width,)),
                whole((width,)),
                ANY,
                ANY,
            ],
            out_specs=specs,
            scratch_shapes=scratch,
        ),
        compiler_params=params(57),
        cost_estimate=pl.CostEstimate(flops=6 * total * width * hidden, bytes_accessed=30 << 20, transcendentals=2 * total * hidden),
    )(core, lengths, low, w_in, w_back, bias_in, bias_back, gain2, shift2, cot, cot_other)


def weight_grad(left, right, block_m, block_n, name):
    total, m = left.shape
    n = right.shape[1]

    def body(l_ref, r_ref, o_ref, t_ref):
        @pl.when(pl.program_id(1) == 0)
        def _():
            t_ref[...] = l_ref[...].T

        o_ref[...] = row_dot(t_ref[...], r_ref[...]).astype(BF)

    return pl.pallas_call(
        body,
        name=name,
        out_shape=jax.ShapeDtypeStruct((m, n), BF),
        grid=(m // block_m, n // block_n),
        in_specs=[pl.BlockSpec((total, block_m), lambda i, j: (0, i)), pl.BlockSpec((total, block_n), lambda i, j: (0, j))],
        out_specs=pl.BlockSpec((block_m, block_n), lambda i, j: (i, j)),
        scratch_shapes=[pltpu.VMEM((block_m, total), BF)],
        compiler_params=params(60),
        cost_estimate=pl.CostEstimate(flops=2 * total * m * n, bytes_accessed=2 * (total * (m + n) + m * n), transcendentals=0),
    )(left, right)


def branch_grad(core, dfeed, slope, low, mixed, hat1, inv1, w_in, w_back, w_out, gain1, dp, split):
    total, width = dfeed.shape
    hidden = slope.shape[1]
    chunk = width
    chunks = hidden // chunk
    steps = chunks + (1 if split else 0)
    rows = width // (2 * dp)

    def body(core_ref, f_ref, s_ref, l_ref, m_ref, h_ref, v_ref, wb_ref, wi_ref, wo_ref, g_ref, branch_ref, mixed_ref, gi_ref, gg_ref, gs_ref, gb_ref, *rest):
        step = pl.program_id(0)
        if split:
            keep_ref, send_ref, acc_ref, inner_ref, grad_ref = rest
        else:
            inner_ref, acc_ref = rest

        @pl.when(step < chunks)
        def _():
            inner = (row_dot_t(f_ref[...], wb_ref[...]) * s_ref[...].astype(F32)).astype(BF)
            inner_ref[...] = inner
            gi_ref[...] = jnp.sum(inner.astype(F32), axis=0, keepdims=True)
            value = row_dot_t(inner_ref[...], wi_ref[...])

            @pl.when(step == 0)
            def _():
                acc_ref[...] = value

            @pl.when(step > 0)
            def _():
                acc_ref[...] += value

            if split:
                grad_ref[...] = col_dot(l_ref[...], inner_ref[...])
                split_store(grad_ref, keep_ref, send_ref, core_ref[0], rows, 2)

        @pl.when(step == chunks - 1)
        def _():
            gg_ref[...] = jnp.zeros_like(gg_ref)
            gs_ref[...] = jnp.zeros_like(gs_ref)
            gb_ref[...] = jnp.zeros_like(gb_ref)
            block = 256

            def token_body(i, carry):
                at = pl.ds(pl.multiple_of(i * block, block), block)
                dn = f_ref[at, :].astype(F32) + acc_ref[at, :]
                hat = h_ref[at, :].astype(F32)
                gg_ref[...] += jnp.sum(dn * hat, axis=0, keepdims=True)
                gs_ref[...] += jnp.sum(dn, axis=0, keepdims=True)
                g = dn * g_ref[...]
                dpre = v_ref[at, :] * (g - jnp.mean(g, axis=-1, keepdims=True) - hat * jnp.mean(g * hat, axis=-1, keepdims=True))
                branch = dpre.astype(BF)
                branch_ref[at, :] = branch
                gb_ref[...] += jnp.sum(branch.astype(F32), axis=0, keepdims=True)
                return carry

            lax.fori_loop(0, total // block, token_body, 0)
            mixed_ref[...] = row_dot_t(branch_ref[...], wo_ref[...]).astype(BF)

        if split:
            @pl.when(step == chunks)
            def _():
                grad_ref[...] = col_dot(m_ref[...], branch_ref[...])
                split_store(grad_ref, keep_ref, send_ref, core_ref[0], rows, 2)

    def at(j):
        return jnp.minimum(j, chunks - 1)

    one = jax.ShapeDtypeStruct((1, width), F32)
    row = jax.ShapeDtypeStruct((total, width), BF)
    shapes = [row, row, jax.ShapeDtypeStruct((1, hidden), F32), one, one, one]
    specs = [whole((total, width))] * 2 + [pl.BlockSpec((1, chunk), lambda j, *_: (0, at(j)))] + [whole((1, width))] * 3
    scratch = [pltpu.VMEM((total, width), F32)]
    if split:
        shapes += [jax.ShapeDtypeStruct((2 * steps, dp, rows, LANES), BF)] * 2
        specs += [pl.BlockSpec((2, dp, rows, LANES), lambda j, *_: (j, 0, 0, 0))] * 2
        scratch += [pltpu.VMEM((total, chunk), BF), pltpu.VMEM((width, chunk), F32)]
    else:
        shapes.append(jax.ShapeDtypeStruct((total, hidden), BF))
        specs.append(pl.BlockSpec((total, chunk), lambda j, *_: (0, at(j))))
    return pl.pallas_call(
        body,
        name="branch_grad",
        out_shape=shapes,
        grid_spec=pltpu.PrefetchScalarGridSpec(
            num_scalar_prefetch=1,
            grid=(steps,),
            in_specs=[
                whole((total, width)),
                pl.BlockSpec((total, chunk), lambda j, *_: (0, at(j))),
                whole((total, width)),
                whole((total, width)),
                whole((total, width)),
                whole((total, 1)),
                pl.BlockSpec((chunk, width), lambda j, *_: (at(j), 0)),
                pl.BlockSpec((width, chunk), lambda j, *_: (0, at(j))),
                whole(w_out.shape),
                whole(gain1.shape),
            ],
            out_specs=specs,
            scratch_shapes=scratch,
        ),
        compiler_params=params(52),
        cost_estimate=pl.CostEstimate(flops=2 * total * width * (3 * hidden + width), bytes_accessed=30 << 20, transcendentals=0),
    )(core, dfeed, slope, low, mixed, hat1, inv1, w_back, w_in, w_out, gain1)


def attention_grad(qkv, probs, mixed, dmixed, inverse, lower, count, partial_out=None):
    rows, length, width = mixed.shape
    pairs = width // 128
    scale = (width // HEADS) ** -0.5

    def body(q_ref, k_ref, v_ref, p_ref, m_ref, d_ref, i_ref, *rest):
        out_ref, bq_ref, bv_ref = rest[-3:]

        @pl.when(pl.program_id(1) == 0)
        def _():
            bq_ref[...] = jnp.zeros_like(bq_ref)
            bv_ref[...] = jnp.zeros_like(bv_ref)

        lane = lax.broadcasted_iota(jnp.int32, (1, 128), 1)
        first = lane < 64
        q, k, v = q_ref[0], k_ref[0], v_ref[0]
        scaled = d_ref[0].astype(F32) * i_ref[0]
        d = scaled.astype(BF)
        product = scaled * m_ref[0].astype(F32)
        q_t, d_t, k_t = q.T, d.T, k.T
        dqs, dks, dvs = [], [], []
        for h in range(2):
            on = first if h == 0 else jnp.logical_not(first)
            delta = jnp.sum(jnp.where(on, product, 0.0), axis=-1, keepdims=True)
            dprobs = row_dot_t(jnp.where(on, d, jnp.zeros_like(d)), v)
            p = p_ref[0, 0, h]
            ds = (p.astype(F32) * (dprobs - delta)).astype(BF)
            half = slice(h * 64, (h + 1) * 64)
            dqs.append(row_dot_t(k_t[half], ds))
            dks.append(row_dot(q_t[half], ds))
            dvs.append(row_dot(d_t[half], p))
        dq = (jnp.concatenate(dqs, axis=0) * scale).T.astype(BF)
        dk = jnp.concatenate(dks, axis=0).T.astype(BF)
        dv = jnp.concatenate(dvs, axis=0).T.astype(BF)
        out_ref[0, 0] = dq
        out_ref[1, 0] = dk
        out_ref[2, 0] = dv
        bq_ref[...] += jnp.sum(dq.astype(F32), axis=0, keepdims=True)
        bv_ref[...] += jnp.sum(dv.astype(F32), axis=0, keepdims=True)

    def cols(base):
        return pl.BlockSpec((1, length, 128), lambda p, r: (lower + r, 0, base + p))

    vec = pl.BlockSpec((1, 128), lambda p, r: (0, p))
    out = jax.ShapeDtypeStruct((3, rows, length, width), BF)
    one = jax.ShapeDtypeStruct((1, width), F32)
    more = [] if partial_out is None else [partial_out]
    return pl.pallas_call(
        body,
        name="attention_grad",
        out_shape=[out, one, one],
        grid=(pairs, count),
        input_output_aliases={7: 0} if more else {},
        in_specs=[cols(0), cols(pairs), cols(2 * pairs), pl.BlockSpec((1, 1, 2, length, length), lambda p, r: (lower + r, p, 0, 0, 0)), cols(0), cols(0), cols(0)] + [ANY] * len(more),
        out_specs=[pl.BlockSpec((3, 1, length, 128), lambda p, r: (0, lower + r, 0, p)), vec, vec],
        compiler_params=params(32),
        cost_estimate=pl.CostEstimate(flops=8 * count * length * length * width, bytes_accessed=(15 * count) << 20, transcendentals=0),
    )(qkv, qkv, qkv, probs, mixed, dmixed, inverse, *more)


def input_grad_call(core, dproj, dpre, w_qkv, half):
    _, total, width = dproj.shape
    length = 2 * half
    group = total // length

    def body(core_ref, p_ref, d_ref, w_ref, own_hbm, other_hbm, acc_ref, out_ref, sem):
        step = pl.program_id(0)
        core = core_ref[0]
        value = row_dot_t(p_ref[0], w_ref[...])

        @pl.when(step == 0)
        def _():
            acc_ref[...] = value + d_ref[...].astype(F32)

        @pl.when(step == 1)
        def _():
            acc_ref[...] += value

        @pl.when(step == 2)
        def _():
            out_ref[...] = (acc_ref[...] + value).astype(BF)
            stores = []
            for r in range(group):
                other = pl.ds(pl.multiple_of(r * length + (1 - core) * half, half), half)
                own = pl.ds(pl.multiple_of(r * length + core * half, half), half)
                stores.append(pltpu.make_async_copy(out_ref.at[other], other_hbm.at[r], sem.at[r]))
                stores.append(pltpu.make_async_copy(out_ref.at[own], own_hbm.at[core * group + r], sem.at[group + r]))
            for store in stores:
                store.start()
            for store in stores:
                store.wait()

    return pl.pallas_call(
        body,
        name="input_grad",
        out_shape=[jax.ShapeDtypeStruct((2 * group, half, width), BF), jax.ShapeDtypeStruct((group, half, width), BF)],
        grid_spec=pltpu.PrefetchScalarGridSpec(
            num_scalar_prefetch=1,
            grid=(3,),
            in_specs=[
                pl.BlockSpec((1, total, width), lambda n, *_: (n, 0, 0)),
                whole((total, width)),
                pl.BlockSpec((width, width), lambda n, *_: (0, n)),
            ],
            out_specs=[HBM, HBM],
            scratch_shapes=[pltpu.VMEM((total, width), F32), pltpu.VMEM((total, width), BF), pltpu.SemaphoreType.DMA((2 * group,))],
        ),
        compiler_params=params(32),
        cost_estimate=pl.CostEstimate(flops=6 * total * width * width, bytes_accessed=10 << 20, transcendentals=0),
    )(core, dproj, dpre, w_qkv)


def vector_exchange(parts, devices):
    total = sum(p.shape[1] for p in parts)
    cut = total // devices
    stretch = cut
    while stretch % 128:
        stretch *= 2
    per = stretch // cut

    def body(*refs):
        *ins, out = refs
        joined = jnp.concatenate([ref[...] for ref in ins], axis=1)
        for d in range(devices // per):
            out[d * per : (d + 1) * per, :] = jnp.broadcast_to(joined[:, d * stretch : (d + 1) * stretch], (per, stretch))

    table = pl.pallas_call(
        body,
        name="vector_table",
        out_shape=jax.ShapeDtypeStruct((devices, stretch), F32),
        compiler_params=params(16),
    )(*parts)
    return jnp.sum(lax.all_to_all(table, ("dp", "seq"), 0, 0, tiled=True), axis=0)


def swap(value):
    return lax.ppermute(value, "seq", [(0, 1), (1, 0)])


def pick(value, index, axis):
    return lax.dynamic_index_in_dim(value, index, axis, keepdims=False)


def reduce_stages(part, order, dp_bits, dp):
    me = lax.axis_index("dp")
    n_halving = dp_bits - 2
    shape = part.shape[1:]
    current = part.reshape((2,) * dp_bits + shape)
    left = list(range(dp_bits - 1, -1, -1))
    for bit in order[:n_halving]:
        axis = left.index(bit)
        mine = (me >> bit) & 1
        pairs = [(i, i ^ (1 << bit)) for i in range(dp)]
        send = pick(current, 1 - mine, axis).astype(BF)
        got = lax.ppermute(send, "dp", pairs)
        keep = pick(current, mine, axis)
        current = (keep.astype(F32) + got.astype(F32)).astype(BF)
        left.remove(bit)
    high, low = left
    group = (((me >> high) & 1) << 1) | ((me >> low) & 1)
    current = current.reshape((4,) + shape)
    total = pick(current, group, 0).astype(F32)
    for other in (1, 2, 3):
        flip = ((other >> 1) << high) | ((other & 1) << low)
        pairs = [(i, i ^ flip) for i in range(dp)]
        send = pick(current, group ^ other, 0).astype(BF)
        total = total + lax.ppermute(send, "dp", pairs).astype(F32)
    return total


def reduce_scatter(grad, order, dp, dp_bits):
    core = lax.axis_index("seq")
    rows = grad.shape[0] // (2 * dp)
    blocks = grad.reshape(dp, 2, rows, grad.shape[1])
    send = pick(blocks, 1 - core, 1).astype(BF)
    keep = pick(blocks, core, 1)
    part = (keep.astype(F32) + swap(send).astype(F32)).astype(BF)
    return reduce_stages(part, order, dp_bits, dp)


LANES = 384


def split_store(acc_ref, keep_ref, send_ref, core, rows, parts):
    for d in range(acc_ref.shape[0] // (2 * rows)):
        for ref, side in ((keep_ref, core), (send_ref, 1 - core)):
            value = acc_ref[pl.ds(pl.multiple_of((2 * d + side) * rows, 8), rows), :].astype(BF)
            for c in range(parts):
                ref[c, d] = value[:, c * LANES : (c + 1) * LANES]


def grad_rows(core, left, right, dp, name):
    total, m = left.shape
    n = right.shape[1]
    rows = m // (2 * dp)
    group = 4
    block = group * 2 * rows

    def body(core_ref, l_ref, r_ref, keep_ref, send_ref, acc_ref):
        acc_ref[...] = col_dot(l_ref[...], r_ref[...])
        split_store(acc_ref, keep_ref, send_ref, core_ref[0], rows, n // LANES)

    out = jax.ShapeDtypeStruct((n // LANES, dp, rows, LANES), BF)
    out_spec = pl.BlockSpec((n // LANES, group, rows, LANES), lambda i, *_: (0, i, 0, 0))
    return pl.pallas_call(
        body,
        name=name,
        out_shape=[out, out],
        grid_spec=pltpu.PrefetchScalarGridSpec(
            num_scalar_prefetch=1,
            grid=(dp // group,),
            in_specs=[pl.BlockSpec((total, block), lambda i, *_: (0, i)), whole((total, n))],
            out_specs=[out_spec, out_spec],
            scratch_shapes=[pltpu.VMEM((block, n), F32)],
        ),
        compiler_params=params(60),
        cost_estimate=pl.CostEstimate(flops=2 * total * m * n, bytes_accessed=2 * (total * (m + n) + m * n), transcendentals=0),
    )(core, left, right)


def grad_columns(core, pairs, dp, name):
    counts = [(r.shape[0] if r.ndim == 3 else r.shape[1] // (2 * LANES)) for _, r in pairs]
    bases = [sum(counts[:i]) for i in range(len(counts))]
    blocks = sum(counts)
    total, m = pairs[0][0].shape
    rows = m // (2 * dp)
    n = 2 * LANES

    def body(core_ref, *refs):
        lefts = refs[: len(pairs)]
        rights = refs[len(pairs) : 2 * len(pairs)]
        keep_ref, send_ref, acc_ref = refs[2 * len(pairs) :]
        step = pl.program_id(0)
        for i, count in enumerate(counts):
            @pl.when(jnp.logical_and(step >= bases[i], step < bases[i] + count))
            def _():
                r = rights[i]
                value = r[0] if len(r.shape) == 3 else r[...]
                acc_ref[...] = col_dot(lefts[i][...], value)

        split_store(acc_ref, keep_ref, send_ref, core_ref[0], rows, 2)

    def right_spec(i, r):
        def at(j):
            return jnp.clip(j - bases[i], 0, counts[i] - 1)

        if r.ndim == 3:
            return pl.BlockSpec((1, total, n), lambda j, *_: (at(j), 0, 0))
        return pl.BlockSpec((total, n), lambda j, *_: (0, at(j)))

    out = jax.ShapeDtypeStruct((2 * blocks, dp, rows, LANES), BF)
    out_spec = pl.BlockSpec((2, dp, rows, LANES), lambda j, *_: (j, 0, 0, 0))
    return pl.pallas_call(
        body,
        name=name,
        out_shape=[out, out],
        grid_spec=pltpu.PrefetchScalarGridSpec(
            num_scalar_prefetch=1,
            grid=(blocks,),
            in_specs=[whole((total, m)) for _ in pairs] + [right_spec(i, r) for i, (_, r) in enumerate(pairs)],
            out_specs=[out_spec, out_spec],
            scratch_shapes=[pltpu.VMEM((m, n), F32)],
        ),
        compiler_params=params(32),
        cost_estimate=pl.CostEstimate(flops=2 * total * m * n * blocks, bytes_accessed=2 * blocks * n * (total + m), transcendentals=0),
    )(core, *[l for l, _ in pairs], *[r for _, r in pairs])


def add_pieces(where, inputs, outputs, pieces, piece_shape, name):
    count = len(pieces([jnp.int32(0)] * 3))

    def body(where_ref, *refs):
        ins = refs[: len(inputs)]
        outs = refs[len(inputs) : len(inputs) + len(outputs)]
        k_ref, g_ref, k_sem, g_sem, o_sem = refs[len(inputs) + len(outputs) :]
        table = pieces([where_ref[0], where_ref[1], where_ref[2]])
        loads, stores = [], []
        for i, (a, b, a_at, b_at, o, o_at) in enumerate(table):
            loads.append((pltpu.make_async_copy(ins[a].at[a_at], k_ref.at[i], k_sem.at[i]), pltpu.make_async_copy(ins[b].at[b_at], g_ref.at[i], g_sem.at[i])))
            stores.append(pltpu.make_async_copy(k_ref.at[i], outs[o].at[o_at], o_sem.at[i]))
        for pair in loads:
            pair[0].start()
            pair[1].start()
        for i in range(count):
            loads[i][0].wait()
            loads[i][1].wait()
            k_ref[i] = k_ref[i] + g_ref[i]
            stores[i].start()
        for store in stores:
            store.wait()

    return pl.pallas_call(
        body,
        name=name,
        out_shape=[jax.ShapeDtypeStruct(s, BF) for s in outputs],
        grid_spec=pltpu.PrefetchScalarGridSpec(
            num_scalar_prefetch=1,
            grid=(1,),
            in_specs=[ANY] * len(inputs),
            out_specs=[HBM] * len(outputs),
            scratch_shapes=[pltpu.VMEM((count,) + piece_shape, BF)] * 2 + [pltpu.SemaphoreType.DMA((count,))] * 3,
        ),
        compiler_params=params(16),
    )(where, *inputs)


def fold_first(where, keep, got, name):
    _, blocks, _, _, _, rows, lanes = keep.shape
    every = slice(None)

    def pieces(at):
        z_, y, x = at
        table = []
        for role in (1, 0):
            for z in range(4):
                ax = x if role == 0 else 1 - x
                ay = y if role == 0 else 1 - y
                for half, index in ((0, (0, every, z, every, ax)), (1, (1, every, z, ay))):
                    table.append((0, 1, index, index, 2 * half + (1 - role), (every, z)))
        return table

    shape = (blocks, 4, 2, rows, lanes)
    return add_pieces(where, (keep, got), [shape] * 4, pieces, (blocks, 2, rows, lanes), name)


def fold_second(where, keep_a, got_a, keep_b, got_b, name):
    blocks, _, _, rows, lanes = keep_a.shape
    every = slice(None)

    def pieces(at):
        z_, y, x = at
        table = []
        for role in (1, 0):
            for z in range(4):
                for half, own in ((0, y), (1, x)):
                    index = (every, z, own if role == 0 else 1 - own)
                    table.append((2 * half, 2 * half + 1, index, index, 2 * half + (1 - role), (every, z)))
        return table

    shape = (blocks, 4, rows, lanes)
    return add_pieces(where, (keep_a, got_a, keep_b, got_b), [shape] * 4, pieces, (blocks, rows, lanes), name)


def fold_third(where, keep_a, got_a, keep_b, got_b, name):
    blocks, _, rows, lanes = keep_a.shape
    every = slice(None)

    def pieces(at):
        z, y_, x_ = at
        table = []
        for flip in (1, 2, 3, 0):
            for half in range(2):
                index = (every, z ^ flip)
                table.append((2 * half, 2 * half + 1, index, index, flip, (half,)))
        return table

    shape = (2, blocks, rows, lanes)
    return add_pieces(where, (keep_a, got_a, keep_b, got_b), [shape] * 4, pieces, (blocks, rows, lanes), name)


def fold_last(parts, widths, name):
    _, blocks, rows, lanes = parts[0].shape

    def body(a_ref, b_ref, c_ref, d_ref, *outs):
        base = 0
        for out, width in zip(outs, widths):
            tiles = width // 128
            for t in range(tiles):
                column = base + t * 128
                chunk, at = column // lanes, column % lanes
                half, block = chunk // blocks, chunk % blocks
                total = None
                for ref in (a_ref, b_ref, c_ref, d_ref):
                    value = ref[half, block, :, at : at + 128].astype(F32)
                    total = value if total is None else total + value
                out[pl.ds(t, rows, stride=tiles), :] = total
            base += width

    return pl.pallas_call(
        body,
        name=name,
        out_shape=[jax.ShapeDtypeStruct((rows * w // 128, 128), F32) for w in widths],
        compiler_params=params(16),
    )(*parts)


def after(value, *earlier):
    return lax.optimization_barrier((value,) + earlier)[0]


def sync(*values):
    return lax.optimization_barrier(values)


def flip(value, bits):
    return lax.ppermute(value, "dp", [(i, i ^ bits) for i in range(16)])


def on_device(tokens, lengths, w_qkv, w_out, w_in, w_back, bias_q, value_bias, bias_out, gain1, shift1, bias_in, bias_back, gain2, shift2, cotangent):
    rows_local, half, width = tokens.shape
    dp = lax.axis_size("dp")
    dp_bits = dp.bit_length() - 1
    core = lax.axis_index("seq")
    rows = rows_local // 2
    length = 2 * half
    total = rows * length
    order_a = (0, 1) + tuple(range(2, dp_bits))
    order_b = (1, 0) + tuple(range(2, dp_bits))

    def send_rows(value):
        return swap(lax.dynamic_slice_in_dim(value, (1 - core) * rows, rows, 0))

    other = send_rows(tokens)
    cot_other = send_rows(cotangent)
    bq, bv, bo, g1, s1, bi, bb, g2, s2 = (bias_q, value_bias, bias_out, gain1, shift1, bias_in, bias_back, gain2, shift2)
    core_one = core.reshape(1).astype(jnp.int32)
    me = lax.axis_index("dp")
    fast = dp == 16 and width == 2 * LANES
    qkv, probs, full_tokens, mixed, low, hat1, inv1, inverse = attention_call(core_one, lengths, tokens, other, w_qkv, w_out, (bq, bv, bo, g1, s1))

    def flat(value):
        return value.reshape(total, value.shape[-1])

    full_tokens = flat(full_tokens)
    slope, output, output_other, cls_own, dfeed, g_gain2, g_shift2, g_bias_back, *rest = feed_forward_call(
        core_one, lengths, flat(low), w_in, w_back, (bi.reshape(1, -1), bb, g2, s2), cotangent, cot_other, dp, fast
    )
    pairs = width // 128
    output_got = swap(output_other)
    cls_own = cls_own[:, : lengths.shape[1]]
    cls_got = swap(cls_own)
    if fast:
        where = jnp.stack([me >> 2, (me >> 1) & 1, me & 1]).astype(jnp.int32)

        def view(value):
            return value.reshape((2, value.shape[0] // 2, 4, 2, 2) + value.shape[2:])

        def cross(parts, bit_a, bit_b):
            return flip(parts[0], bit_a), flip(parts[2], bit_b)

        def along_z(parts):
            return [parts[0]] + [flip(parts[f], 4 * f) for f in (1, 2, 3)]

        keep_b, send_b = rest
        got_b = swap(send_b)
        dpre1, dmixed, g_bias_in, g_gain1, g_shift1, g_bias_out, keep_i, send_i = branch_grad(
            core_one, dfeed, slope, flat(low), flat(mixed), flat(hat1), flat(inv1), w_in, w_back, w_out, g1, dp, True
        )
        send_i, keep_b, got_b, output_got, cls_got = sync(send_i, keep_b, got_b, output_got, cls_got)
        back = fold_first(where, view(keep_b), view(got_b), "back_1")
        dmixed, send_i, back = sync(dmixed, send_i, back)
        dmixed = dmixed.reshape(rows, length, width)
        got = cross(back, 1, 2)
        got_i = swap(send_i)
        dproj, *bias_a = attention_grad(qkv, probs, mixed, dmixed, inverse, 0, 1)
        dproj, got, got_i = sync(dproj, got, got_i)
        back = fold_second(where, back[1], got[0], back[3], got[1], "back_2")
        inner = fold_first(where, view(keep_i), view(got_i), "inner_1")
        dmixed, inner, back = sync(dmixed, inner, back)
        got = cross(back, 2, 1)
        got_i = cross(inner, 1, 2)
        dproj, *bias_b = attention_grad(qkv, probs, mixed, dmixed, inverse, 1, 1, dproj)
        dproj = dproj.reshape(3, total, width)
        keep_q, send_q = grad_columns(core_one, [(full_tokens, dproj)], dp, "grad_qkv")
        keep_q, send_q, got, got_i = sync(keep_q, send_q, got, got_i)
        got_q = swap(send_q)
        back = fold_third(where, back[1], got[0], back[3], got[1], "back_3")
        inner = fold_second(where, inner[1], got_i[0], inner[3], got_i[1], "inner_2")
        inner, back, got_q = sync(inner, back, got_q)
        proj = fold_first(where, view(keep_q), view(got_q), "proj_1")
        dproj, inner, proj, back = sync(dproj, inner, proj, back)
        got_q = cross(proj, 1, 2)
        got = cross(inner, 2, 1)
        back = along_z(back)
        dinput, dinput_other = input_grad_call(core_one, dproj, dpre1, w_qkv, half)
        dinput, dinput_other, got, got_q, back = sync(dinput, dinput_other, got, got_q, back)
        dinput_got = swap(dinput_other)
        proj = fold_second(where, proj[1], got_q[0], proj[3], got_q[1], "proj_2")
        inner = fold_third(where, inner[1], got[0], inner[3], got[1], "inner_3")
        proj, inner = sync(proj, inner)
        got_q = cross(proj, 2, 1)
        inner = along_z(inner)
        (r_back,) = fold_last(back, (width,), "back_4")
        g_bias_q, g_bias_v = bias_a[0] + bias_b[0], bias_a[1] + bias_b[1]
        vec_sum = vector_exchange((g_bias_q, g_bias_v, g_bias_out, g_gain1, g_shift1, g_bias_in, g_bias_back, g_gain2, g_shift2), 2 * dp)
        got_q, dinput_got = sync(got_q, dinput_got)
        proj = fold_third(where, proj[1], got_q[0], proj[3], got_q[1], "proj_3")
        proj, inner = sync(along_z(proj), inner)
        r_in, r_out = fold_last(inner, (w_in.shape[1], width), "inner_4")
        (r_qkv,) = fold_last(proj, (3 * width,), "proj_4")
    else:
        (act,) = rest
        g_back = weight_grad(act, dfeed, 512, width, "grad_back")
        r_back = reduce_scatter(g_back, order_a, dp, dp_bits)
        dpre1, dmixed, g_bias_in, g_gain1, g_shift1, g_bias_out, dinner = branch_grad(
            core_one, dfeed, slope, flat(low), flat(mixed), flat(hat1), flat(inv1), w_in, w_back, w_out, g1, dp, False
        )
        g_in = weight_grad(flat(low), dinner, width, 512, "grad_in")
        r_in = reduce_scatter(g_in, order_b, dp, dp_bits)
        g_out = weight_grad(flat(mixed), dpre1, width, width, "grad_out")
        r_out = reduce_scatter(g_out, order_a, dp, dp_bits)
        dproj, g_bias_q, g_bias_v = attention_grad(qkv, probs, mixed, dmixed.reshape(rows, length, width), inverse, 0, rows)
        dproj = dproj.reshape(3, total, width)
        g_qkv = jnp.concatenate([weight_grad(full_tokens, dproj[n], width, width, "grad_qkv") for n in range(3)], axis=1)
        r_qkv = reduce_scatter(g_qkv, order_b, dp, dp_bits)
        dinput, dinput_other = input_grad_call(core_one, dproj, dpre1, w_qkv, half)
        dinput_got = swap(dinput_other)
    if not fast:
        vec_sum = vector_exchange((g_bias_q, g_bias_v, g_bias_out, g_gain1, g_shift1, g_bias_in, g_bias_back, g_gain2, g_shift2), 2 * dp)
    n_vec = (8 * width + w_in.shape[1]) // (2 * dp)
    per = vec_sum.shape[0] // n_vec
    r_vec = lax.dynamic_slice_in_dim(vec_sum, lax.rem(2 * me + core, per) * n_vec, n_vec, 0)

    output = lax.dynamic_update_slice_in_dim(output, output_got, (1 - core) * rows, 0)
    cls = jnp.where(core == 0, jnp.concatenate([cls_own, cls_got], axis=0), jnp.concatenate([cls_got, cls_own], axis=0))
    input_grad = lax.dynamic_update_slice_in_dim(dinput, dinput_got, (1 - core) * rows, 0)
    return (
        output,
        cls,
        input_grad,
        r_qkv.reshape(-1),
        r_out.reshape(-1),
        r_in.reshape(-1),
        r_back.reshape(-1),
        r_vec,
    )


def solution(mesh):
    row = P("dp", "seq", None)
    both = P(("dp", "seq"))
    return jax.shard_map(
        on_device,
        mesh=mesh,
        in_specs=(row, P("dp", None)) + (P(),) * 13 + (row,),
        out_specs=(row, P("dp", None, None), row, both, both, both, both, both),
        check_vma=False,
    )
```

```python
from functools import partial

import jax
import jax.numpy as jnp
from jax import lax
from jax.experimental import pallas as pl
from jax.experimental.pallas import tpu as pltpu
from jax.sharding import PartitionSpec as P

HEADS = 12
EPS = 1e-12
BF = jnp.bfloat16
F32 = jnp.float32
VMEM_LIMIT = 60 << 20
RSQRT2 = 0.7071067811865476
RSQRT2PI = 0.3989422804014327


def row_dot(left, right):
    return lax.dot_general(left, right, (((1,), (0,)), ((), ())), preferred_element_type=F32)


def row_dot_t(left, right):
    return lax.dot_general(left, right, (((1,), (1,)), ((), ())), preferred_element_type=F32)


def col_dot(left, right):
    return lax.dot_general(left, right, (((0,), (0,)), ((), ())), preferred_element_type=F32)


def gelu_pair(value):
    expo = jnp.exp(value * value * -0.5)
    phi = 0.5 + 0.5 * lax.erf(value * RSQRT2)
    return value * phi, phi + value * expo * RSQRT2PI


def whole(shape):
    return pl.BlockSpec(shape, lambda *_: (0,) * len(shape))


ANY = pl.BlockSpec(memory_space=pl.ANY)
HBM = pl.BlockSpec(memory_space=pltpu.HBM)


def params(mib):
    return pltpu.CompilerParams(vmem_limit_bytes=mib << 20)


def row_starts(len_ref, row):
    starts = [jnp.int32(0)]
    for j in range(len_ref.shape[1] - 1):
        starts.append(starts[-1] + len_ref[row, j])
    return starts


def attention_kernel(
    core_ref, len_ref, own_ref, other_ref, wqkv_hbm, wout_hbm, bq_ref, bv_ref, bo_ref, g1_ref, s1_ref,
    qkv_hbm, probs_hbm, x_ref, mixed_ref, low_ref, hat1_ref, inv1_ref, scale_ref,
    bias_ref, ahead0_ref, ahead1_ref, qkv_ref, wqkv_ref, wout_ref, p_ref, w_sem, p_sem, q_sem,
):
    step = pl.program_id(0)
    core = core_ref[0]
    rows = pl.num_programs(0)
    half, width = own_ref.shape[1:]
    length = 2 * half
    pairs = width // 128
    parts = [slice(n * width, (n + 1) * width) for n in range(3)]
    copies = [pltpu.make_async_copy(wqkv_hbm.at[:, part], wqkv_ref.at[:, part], w_sem.at[n]) for n, part in enumerate(parts)]
    copies.append(pltpu.make_async_copy(wout_hbm, wout_ref, w_sem.at[3]))

    @pl.when(step == 0)
    def _():
        for copy in copies:
            copy.start()

    x_ref[0, pl.ds(pl.multiple_of(core * half, half), half), :] = own_ref[0]
    x_ref[0, pl.ds(pl.multiple_of((1 - core) * half, half), half), :] = other_ref[0]
    starts = row_starts(len_ref, core * rows + step)
    down = lax.broadcasted_iota(jnp.int32, (length, 1), 0)
    across = lax.broadcasted_iota(jnp.int32, (1, length), 1)
    seg_down = jnp.zeros((length, 1), jnp.int32)
    seg_across = jnp.zeros((1, length), jnp.int32)
    for start in starts[1:]:
        seg_down += (down >= start).astype(jnp.int32)
        seg_across += (across >= start).astype(jnp.int32)
    bias_ref[...] = jnp.where(seg_down == seg_across, 0.0, -1e30)

    for n, part in enumerate(parts):
        @pl.when(step == 0)
        def _():
            copies[n].wait()

        value = row_dot(x_ref[0], wqkv_ref[:, part])
        if n == 0:
            value = (value + bq_ref[...]) * (width // HEADS) ** -0.5
        if n == 2:
            value = value + bv_ref[...]
        qkv_ref[:, part] = value.astype(BF)
    save = pltpu.make_async_copy(qkv_ref, qkv_hbm.at[step], q_sem)
    save.start()

    first = lax.broadcasted_iota(jnp.int32, (1, 128), 1) < 64

    def columns(part, pair):
        return pl.ds(pl.multiple_of(part * width + pair * 128, 128), 128)

    def scores(pair, into):
        q_pair = qkv_ref[:, columns(0, pair)]
        k_pair = qkv_ref[:, columns(1, pair)]
        for h in range(2):
            on = first if h == 0 else jnp.logical_not(first)
            into[h] = row_dot_t(jnp.where(on, q_pair, jnp.zeros_like(q_pair)), k_pair)

    def finish(pair, held, slot):
        out_copy = pltpu.make_async_copy(p_ref.at[slot], probs_hbm.at[step, pair], p_sem.at[slot])

        @pl.when(pair >= 2)
        def _():
            out_copy.wait()

        v_pair = qkv_ref[:, columns(2, pair)]
        outs = []
        for h in range(2):
            on = first if h == 0 else jnp.logical_not(first)
            s = held[h] + bias_ref[...]
            e = jnp.exp(s - jnp.max(s, axis=-1, keepdims=True)).astype(BF)
            p_ref[slot, h] = e
            outs.append(row_dot(e, jnp.where(on, v_pair, jnp.ones_like(v_pair))))
        sums = pltpu.roll(jnp.where(first, outs[1], outs[0]), 64, 1)
        inverse = 1.0 / sums
        scale_ref[0, :, columns(0, pair)] = inverse
        mixed_ref[0, :, columns(0, pair)] = (jnp.where(first, outs[0], outs[1]) * inverse).astype(BF)
        out_copy.start()

    scores(0, ahead0_ref)

    def two_pairs(i, carry):
        scores(2 * i + 1, ahead1_ref)
        finish(2 * i, ahead0_ref, 0)
        scores(jnp.minimum(2 * i + 2, pairs - 1), ahead0_ref)
        finish(2 * i + 1, ahead1_ref, 1)
        return carry

    lax.fori_loop(0, pairs // 2, two_pairs, 0)
    for tail in (pairs - 2, pairs - 1):
        pltpu.make_async_copy(p_ref.at[tail % 2], probs_hbm.at[step, tail], p_sem.at[tail % 2]).wait()

    @pl.when(step == 0)
    def _():
        copies[3].wait()

    pre = x_ref[0].astype(F32) + row_dot(mixed_ref[0], wout_ref[...]) + bo_ref[...]
    center = pre - jnp.mean(pre, axis=-1, keepdims=True)
    inv = lax.rsqrt(jnp.mean(center * center, axis=-1, keepdims=True) + EPS)
    hat = center * inv
    hat1_ref[0] = hat.astype(BF)
    inv1_ref[0] = inv
    low_ref[0] = (hat * g1_ref[...] + s1_ref[...]).astype(BF)
    save.wait()


def attention_call(core, lengths, tokens, other, w_qkv, w_out, vectors):
    rows_local, half, width = tokens.shape
    rows = rows_local // 2
    length = 2 * half
    pairs = width // 128

    def full(n):
        return pl.BlockSpec((1, length, n), lambda r, *_: (r, 0, 0))

    def row(n, kind=BF):
        return jax.ShapeDtypeStruct((rows, length, n), kind)

    return pl.pallas_call(
        attention_kernel,
        name="attention_rows",
        out_shape=[
            row(3 * width), jax.ShapeDtypeStruct((rows, pairs, 2, length, length), BF), row(width), row(width), row(width), row(width),
            row(1, F32), row(width, F32),
        ],
        grid_spec=pltpu.PrefetchScalarGridSpec(
            num_scalar_prefetch=2,
            grid=(rows,),
            in_specs=[
                pl.BlockSpec((1, half, width), lambda r, core, lens: (core[0] * rows + r, 0, 0)),
                pl.BlockSpec((1, half, width), lambda r, *_: (r, 0, 0)),
                ANY,
                ANY,
            ]
            + [whole(v.shape) for v in vectors],
            out_specs=[HBM, HBM] + [full(width)] * 4 + [full(1), full(width)],
            scratch_shapes=[
                pltpu.VMEM((length, length), F32),
                pltpu.VMEM((2, length, length), F32),
                pltpu.VMEM((2, length, length), F32),
                pltpu.VMEM((length, 3 * width), BF),
                pltpu.VMEM(w_qkv.shape, BF),
                pltpu.VMEM(w_out.shape, BF),
                pltpu.VMEM((2, 2, length, length), BF),
                pltpu.SemaphoreType.DMA((4,)),
                pltpu.SemaphoreType.DMA((2,)),
                pltpu.SemaphoreType.DMA,
            ],
        ),
        compiler_params=params(60),
        cost_estimate=pl.CostEstimate(
            flops=8 * rows * length * width * width + 4 * rows * length * length * width,
            bytes_accessed=35 << 20,
            transcendentals=rows * HEADS * length * length,
        ),
    )(core, lengths, tokens, other, w_qkv, w_out, *vectors)


def feed_kernel(
    split, core_ref, len_ref, low_ref, win_hbm, wback_hbm, wout_hbm, mixed_hbm, hat1_hbm, inv1_hbm, scale_hbm, cot_hbm, cot_other_hbm,
    bi_ref, bb_ref, g1_ref, g2_ref, s2_ref,
    out_hbm, other_hbm, cls_ref, dpre_hbm, dmixed_hbm, gi_ref, gg2_ref, gs2_ref, gb2_ref, gg1_ref, gs1_ref, gb1_ref, *rest
):
    n_grads = 4 if split else 2
    grads = rest[:n_grads]
    (win_ref, wback_ref, wout_ref, mixed_ref, hat1_ref, inv1_ref, scale_ref, cot_ref, out_ref, act_ref, slope_ref, acc_ref, dfeed_ref,
     grad_ref, w_sem, v_sem, c_sem, o_sem, d_sem) = rest[n_grads:]
    step = pl.program_id(0)
    core = core_ref[0]
    total, width = low_ref.shape
    length = 2 * cot_other_hbm.shape[1]
    half = length // 2
    group = total // length
    hidden = act_ref.shape[1]
    chunk = width
    chunks = hidden // chunk
    piece = 768
    pieces = [slice(n * piece, (n + 1) * piece) for n in range(chunk // piece)]
    weights = []
    for c in range(chunks):
        part = slice(c * chunk, (c + 1) * chunk)
        weights.append(pltpu.make_async_copy(win_hbm.at[:, part], win_ref.at[:, part], w_sem.at[2 * c]))
        weights.append(pltpu.make_async_copy(wback_hbm.at[part], wback_ref.at[part], w_sem.at[2 * c + 1]))
    values = [
        pltpu.make_async_copy(src, dst, v_sem.at[i])
        for i, (src, dst) in enumerate(
            ((hat1_hbm, hat1_ref), (inv1_hbm, inv1_ref), (wout_hbm, wout_ref), (scale_hbm, scale_ref), (mixed_hbm, mixed_ref))
        )
    ]
    loads, stores = [], []
    for r in range(group):
        own = pl.ds(pl.multiple_of(r * length + core * half, half), half)
        other = pl.ds(pl.multiple_of(r * length + (1 - core) * half, half), half)
        loads.append(pltpu.make_async_copy(cot_hbm.at[core * group + r], cot_ref.at[own], c_sem.at[r]))
        loads.append(pltpu.make_async_copy(cot_other_hbm.at[r], cot_ref.at[other], c_sem.at[group + r]))
        stores.append(pltpu.make_async_copy(out_ref.at[other], other_hbm.at[r], o_sem.at[group + r]))
        stores.append(pltpu.make_async_copy(out_ref.at[own], out_hbm.at[core * group + r], o_sem.at[r]))
    dpre_store = pltpu.make_async_copy(out_ref, dpre_hbm, d_sem.at[0])
    dmixed_store = pltpu.make_async_copy(cot_ref, dmixed_hbm, d_sem.at[1])

    @pl.when(step == 0)
    def _():
        for copy in weights + loads + values:
            copy.start()

    for c in range(chunks):
        @pl.when(step == c)
        def _():
            weights[2 * c].wait()
            weights[2 * c + 1].wait()

    @pl.when(step < chunks)
    def _():
        base = pl.multiple_of(step * chunk, chunk)
        for n in range(len(pieces)):
            cols = pl.ds(base + n * piece, piece)
            act, slope = gelu_pair(row_dot(low_ref[...], win_ref[:, cols]) + bi_ref[:, cols])
            act_ref[:, cols] = act.astype(BF)
            slope_ref[:, cols] = slope.astype(BF)
        rows = pl.ds(base, chunk)

        @pl.when(step == 0)
        def _():
            for cols in pieces:
                acc_ref[:, cols] = row_dot(act_ref[:, rows], wback_ref[rows, cols])

        @pl.when(step > 0)
        def _():
            for cols in pieces:
                acc_ref[:, cols] += row_dot(act_ref[:, rows], wback_ref[rows, cols])

    block = 256

    @pl.when(step == chunks - 1)
    def _():
        for load in loads:
            load.wait()
        gg2_ref[...] = jnp.zeros_like(gg2_ref)
        gs2_ref[...] = jnp.zeros_like(gs2_ref)
        gb2_ref[...] = jnp.zeros_like(gb2_ref)

        def token_body(i, carry):
            at = pl.ds(pl.multiple_of(i * block, block), block)
            pre = low_ref[at, :].astype(F32) + acc_ref[at, :] + bb_ref[...]
            center = pre - jnp.mean(pre, axis=-1, keepdims=True)
            inv = lax.rsqrt(jnp.mean(center * center, axis=-1, keepdims=True) + EPS)
            hat = center * inv
            out_ref[at, :] = (hat * g2_ref[...] + s2_ref[...]).astype(BF)
            dy = cot_ref[at, :].astype(F32)
            gg2_ref[...] += jnp.sum(dy * hat, axis=0, keepdims=True)
            gs2_ref[...] += jnp.sum(dy, axis=0, keepdims=True)
            g = dy * g2_ref[...]
            dpre = inv * (g - jnp.mean(g, axis=-1, keepdims=True) - hat * jnp.mean(g * hat, axis=-1, keepdims=True))
            dfeed = dpre.astype(BF)
            dfeed_ref[at, :] = dfeed
            gb2_ref[...] += jnp.sum(dfeed.astype(F32), axis=0, keepdims=True)
            return carry

        lax.fori_loop(0, total // block, token_body, 0)
        for store in stores:
            store.start()
        which = lax.broadcasted_iota(jnp.int32, (8, 1), 0)
        across = lax.broadcasted_iota(jnp.int32, (1, length), 1)
        for r in range(group):
            down = jnp.full((8, 1), -1, jnp.int32)
            for j, start in enumerate(row_starts(len_ref, core * group + r)):
                down = jnp.where(which == j, start, down)
            choose = (down == across).astype(F32).astype(BF)
            cls_ref[r] = row_dot(choose, out_ref[r * length : (r + 1) * length]).astype(BF)

    def put_grad(value, kept, sent, stack):
        if split:
            grad_ref[...] = value
            split_store(grad_ref, kept, sent, core, 2, stack)
        else:
            kept[...] = value.astype(BF)

    keep_b, keep_i = grads[0], grads[n_grads // 2]
    send_b, send_i = (grads[1], grads[3]) if split else (None, None)

    @pl.when(jnp.logical_and(step >= chunks, step < 2 * chunks))
    def _():
        base = pl.multiple_of((step - chunks) * chunk, chunk)
        rows = pl.ds(base, chunk)
        put_grad(col_dot(act_ref[:, rows], dfeed_ref[...]), keep_b, send_b, chunks)
        for n in range(len(pieces)):
            cols = pl.ds(base + n * piece, piece)
            inner = (row_dot_t(dfeed_ref[...], wback_ref[cols, :]) * slope_ref[:, cols].astype(F32)).astype(BF)
            slope_ref[:, cols] = inner
            gi_ref[:, cols] = jnp.sum(inner.astype(F32), axis=0, keepdims=True)

        @pl.when(step == chunks)
        def _():
            for cols in pieces:
                acc_ref[:, cols] = row_dot_t(slope_ref[:, rows], win_ref[cols, rows])

        @pl.when(step > chunks)
        def _():
            for cols in pieces:
                acc_ref[:, cols] += row_dot_t(slope_ref[:, rows], win_ref[cols, rows])

        put_grad(col_dot(low_ref[...], slope_ref[:, rows]), keep_i, send_i, 1)

    @pl.when(step == 2 * chunks)
    def _():
        for store in stores:
            store.wait()
        for value in values:
            value.wait()
        gg1_ref[...] = jnp.zeros_like(gg1_ref)
        gs1_ref[...] = jnp.zeros_like(gs1_ref)
        gb1_ref[...] = jnp.zeros_like(gb1_ref)

        def token_body(i, carry):
            at = pl.ds(pl.multiple_of(i * block, block), block)
            dn = dfeed_ref[at, :].astype(F32) + acc_ref[at, :]
            hat = hat1_ref[at, :].astype(F32)
            gg1_ref[...] += jnp.sum(dn * hat, axis=0, keepdims=True)
            gs1_ref[...] += jnp.sum(dn, axis=0, keepdims=True)
            g = dn * g1_ref[...]
            dpre = inv1_ref[at, :] * (g - jnp.mean(g, axis=-1, keepdims=True) - hat * jnp.mean(g * hat, axis=-1, keepdims=True))
            branch = dpre.astype(BF)
            out_ref[at, :] = branch
            gb1_ref[...] += jnp.sum(branch.astype(F32), axis=0, keepdims=True)
            return carry

        lax.fori_loop(0, total // block, token_body, 0)
        dpre_store.start()
        for cols in pieces:
            cot_ref[:, cols] = (row_dot_t(out_ref[...], wout_ref[cols, :]) * scale_ref[:, cols]).astype(BF)
        dmixed_store.start()
        put_grad(col_dot(mixed_ref[...], out_ref[...]), keep_i, send_i, 1)
        dpre_store.wait()
        dmixed_store.wait()


def feed_call(core, lengths, low, w_in, w_back, w_out, mixed, hat1, inv1, scale, cot, cot_other, vectors, dp, split):
    total, width = low.shape
    half = cot.shape[1]
    group = cot.shape[0] // 2
    hidden = w_in.shape[1]
    chunks = hidden // width

    def in_back(j):
        return jnp.clip(j - chunks, 0, chunks - 1)

    def in_inner(j):
        return jnp.clip(j - chunks, 0, chunks)

    one = jax.ShapeDtypeStruct((1, width), F32)
    row = jax.ShapeDtypeStruct((total, width), BF)
    shapes = [
        jax.ShapeDtypeStruct(cot.shape, BF),
        jax.ShapeDtypeStruct(cot_other.shape, BF),
        jax.ShapeDtypeStruct((group, 8, width), BF),
        row,
        row,
        jax.ShapeDtypeStruct((1, hidden), F32),
    ] + [one] * 6
    specs = [HBM, HBM, whole((group, 8, width)), HBM, HBM, whole((1, hidden))] + [whole((1, width))] * 6
    if split:
        rows_i = width // (2 * dp)
        devices = dp // chunks
        shapes += [jax.ShapeDtypeStruct((2 * chunks, dp, rows_i, LANES), BF)] * 2
        specs += [pl.BlockSpec((2 * chunks, devices, rows_i, LANES), lambda j, *_: (0, in_back(j), 0, 0))] * 2
        shapes += [jax.ShapeDtypeStruct((2 * (chunks + 1), dp, rows_i, LANES), BF)] * 2
        specs += [pl.BlockSpec((2, dp, rows_i, LANES), lambda j, *_: (in_inner(j), 0, 0, 0))] * 2
    else:
        shapes += [jax.ShapeDtypeStruct((hidden, width), BF), jax.ShapeDtypeStruct((width, hidden + width), BF)]
        specs += [pl.BlockSpec((width, width), lambda j, *_: (in_back(j), 0)), pl.BlockSpec((width, width), lambda j, *_: (0, in_inner(j)))]
    return pl.pallas_call(
        partial(feed_kernel, split),
        name="feed_rows",
        out_shape=shapes,
        grid_spec=pltpu.PrefetchScalarGridSpec(
            num_scalar_prefetch=2,
            grid=(2 * chunks + 1,),
            in_specs=[pl.BlockSpec((total, width), lambda *_: (0, 0), pipeline_mode=pl.Buffered(1))]
            + [ANY] * 9
            + [whole((1, hidden))]
            + [whole((width,))] * 4,
            out_specs=specs,
            scratch_shapes=[
                pltpu.VMEM(w_in.shape, BF),
                pltpu.VMEM(w_back.shape, BF),
                pltpu.VMEM(w_out.shape, BF),
                pltpu.VMEM((total, width), BF),
                pltpu.VMEM((total, width), BF),
                pltpu.VMEM((total, 1), F32),
                pltpu.VMEM((total, width), F32),
                pltpu.VMEM((total, width), BF),
                pltpu.VMEM((total, width), BF),
                pltpu.VMEM((total, hidden), BF),
                pltpu.VMEM((total, hidden), BF),
                pltpu.VMEM((total, width), F32),
                pltpu.VMEM((total, width), BF),
                pltpu.VMEM((width, width), F32),
                pltpu.SemaphoreType.DMA((2 * chunks,)),
                pltpu.SemaphoreType.DMA((5,)),
                pltpu.SemaphoreType.DMA((2 * group,)),
                pltpu.SemaphoreType.DMA((2 * group,)),
                pltpu.SemaphoreType.DMA((2,)),
            ],
        ),
        compiler_params=params(60),
        cost_estimate=pl.CostEstimate(flops=2 * total * width * (6 * hidden + 2 * width), bytes_accessed=40 << 20, transcendentals=2 * total * hidden),
    )(core, lengths, low, w_in, w_back, w_out, mixed, hat1, inv1, scale, cot, cot_other, *vectors)


def weight_grad(left, right, block_m, block_n, name):
    total, m = left.shape
    n = right.shape[1]

    def body(l_ref, r_ref, o_ref, t_ref):
        @pl.when(pl.program_id(1) == 0)
        def _():
            t_ref[...] = l_ref[...].T

        o_ref[...] = row_dot(t_ref[...], r_ref[...]).astype(BF)

    return pl.pallas_call(
        body,
        name=name,
        out_shape=jax.ShapeDtypeStruct((m, n), BF),
        grid=(m // block_m, n // block_n),
        in_specs=[pl.BlockSpec((total, block_m), lambda i, j: (0, i)), pl.BlockSpec((total, block_n), lambda i, j: (0, j))],
        out_specs=pl.BlockSpec((block_m, block_n), lambda i, j: (i, j)),
        scratch_shapes=[pltpu.VMEM((block_m, total), BF)],
        compiler_params=params(63),
        cost_estimate=pl.CostEstimate(flops=2 * total * m * n, bytes_accessed=2 * (total * (m + n) + m * n), transcendentals=0),
    )(left, right)


def attention_grad_kernel(lower, qkv_ref, mixed_ref, d_ref, probs_hbm, *rest):
    out_ref, bq_ref, bv_ref, p_ref, p_sem = rest[-5:]
    step = pl.program_id(0)
    length, width = mixed_ref.shape[1:]
    pairs = width // 128
    scale = (width // HEADS) ** -0.5

    def fetch(pair, slot):
        return pltpu.make_async_copy(probs_hbm.at[lower + step, pair], p_ref.at[slot], p_sem.at[slot])

    fetch(0, 0).start()

    @pl.when(step == 0)
    def _():
        bq_ref[...] = jnp.zeros_like(bq_ref)
        bv_ref[...] = jnp.zeros_like(bv_ref)

    first = lax.broadcasted_iota(jnp.int32, (1, 128), 1) < 64

    def pair_body(pair, carry):
        slot = lax.rem(pair, 2)

        @pl.when(pair + 1 < pairs)
        def _():
            fetch(pair + 1, 1 - slot).start()

        at = pl.ds(pl.multiple_of(pair * 128, 128), 128)
        q = qkv_ref[0, :, at]
        k = qkv_ref[0, :, pl.ds(pl.multiple_of(width + pair * 128, 128), 128)]
        v = qkv_ref[0, :, pl.ds(pl.multiple_of(2 * width + pair * 128, 128), 128)]
        d = d_ref[0, :, at]
        product = d.astype(F32) * mixed_ref[0, :, at].astype(F32)
        q_t, d_t, k_t = q.T, d.T, k.T
        fetch(pair, slot).wait()
        dqs, dks, dvs = [], [], []
        for h in range(2):
            on = first if h == 0 else jnp.logical_not(first)
            part = slice(h * 64, (h + 1) * 64)
            delta = jnp.sum(jnp.where(on, product, 0.0), axis=-1, keepdims=True)
            dprobs = row_dot_t(jnp.where(on, d, jnp.zeros_like(d)), v)
            p = p_ref[slot, h]
            ds = (p.astype(F32) * (dprobs - delta)).astype(BF)
            dqs.append(row_dot_t(k_t[part], ds))
            dks.append(row_dot(q_t[part], ds))
            dvs.append(row_dot(d_t[part], p))
        dq = (jnp.concatenate(dqs, axis=0) * scale).T.astype(BF)
        dv = jnp.concatenate(dvs, axis=0).T.astype(BF)
        out_ref[0, 0, :, at] = dq
        out_ref[1, 0, :, at] = jnp.concatenate(dks, axis=0).T.astype(BF)
        out_ref[2, 0, :, at] = dv
        bq_ref[:, at] += jnp.sum(dq.astype(F32), axis=0, keepdims=True)
        bv_ref[:, at] += jnp.sum(dv.astype(F32), axis=0, keepdims=True)
        return carry

    lax.fori_loop(0, pairs, pair_body, 0)


def attention_grad(qkv, probs, mixed, d, lower, count, partial_out=None):
    rows, length, width = mixed.shape
    more = [] if partial_out is None else [partial_out]

    def full(n):
        return pl.BlockSpec((1, length, n), lambda r: (lower + r, 0, 0))

    one = jax.ShapeDtypeStruct((1, width), F32)
    return pl.pallas_call(
        partial(attention_grad_kernel, lower),
        name="attention_grad",
        out_shape=[jax.ShapeDtypeStruct((3, rows, length, width), BF), one, one],
        grid=(count,),
        input_output_aliases={4: 0} if more else {},
        in_specs=[full(3 * width), full(width), full(width), ANY] + [ANY] * len(more),
        out_specs=[pl.BlockSpec((3, 1, length, width), lambda r: (0, lower + r, 0, 0)), whole((1, width)), whole((1, width))],
        scratch_shapes=[pltpu.VMEM((2, 2, length, length), BF), pltpu.SemaphoreType.DMA((2,))],
        compiler_params=params(63),
        cost_estimate=pl.CostEstimate(flops=8 * count * length * length * width, bytes_accessed=(15 * count) << 20, transcendentals=0),
    )(qkv, mixed, d, probs, *more)


def input_grad_call(core, dproj, dpre, w_qkv, half):
    _, total, width = dproj.shape
    length = 2 * half
    group = total // length

    def body(core_ref, p_ref, d_ref, w_ref, own_hbm, other_hbm, acc_ref, out_ref, sem):
        step = pl.program_id(0)
        core = core_ref[0]
        value = row_dot_t(p_ref[0], w_ref[...])

        @pl.when(step == 0)
        def _():
            acc_ref[...] = value + d_ref[...].astype(F32)

        @pl.when(step == 1)
        def _():
            acc_ref[...] += value

        @pl.when(step == 2)
        def _():
            out_ref[...] = (acc_ref[...] + value).astype(BF)
            stores = []
            for r in range(group):
                other = pl.ds(pl.multiple_of(r * length + (1 - core) * half, half), half)
                own = pl.ds(pl.multiple_of(r * length + core * half, half), half)
                stores.append(pltpu.make_async_copy(out_ref.at[other], other_hbm.at[r], sem.at[r]))
                stores.append(pltpu.make_async_copy(out_ref.at[own], own_hbm.at[core * group + r], sem.at[group + r]))
            for store in stores:
                store.start()
            for store in stores:
                store.wait()

    return pl.pallas_call(
        body,
        name="input_grad",
        out_shape=[jax.ShapeDtypeStruct((2 * group, half, width), BF), jax.ShapeDtypeStruct((group, half, width), BF)],
        grid_spec=pltpu.PrefetchScalarGridSpec(
            num_scalar_prefetch=1,
            grid=(3,),
            in_specs=[
                pl.BlockSpec((1, total, width), lambda n, *_: (n, 0, 0)),
                whole((total, width)),
                pl.BlockSpec((width, width), lambda n, *_: (0, n)),
            ],
            out_specs=[HBM, HBM],
            scratch_shapes=[pltpu.VMEM((total, width), F32), pltpu.VMEM((total, width), BF), pltpu.SemaphoreType.DMA((2 * group,))],
        ),
        compiler_params=params(63),
        cost_estimate=pl.CostEstimate(flops=6 * total * width * width, bytes_accessed=10 << 20, transcendentals=0),
    )(core, dproj, dpre, w_qkv)


def vector_table(parts, devices, more=()):
    cut = sum(p.shape[1] for p in parts) // devices

    def body(*refs):
        *ins, out = refs
        values = [ref[...] for ref in ins[: len(parts)]]
        for i, ref in enumerate(ins[len(parts) :]):
            values[i] = values[i] + ref[...]
        joined = jnp.concatenate(values, axis=1)
        out[...] = jnp.zeros_like(out)
        for d in range(devices):
            out[d : d + 1, :cut] = joined[:, d * cut : (d + 1) * cut]

    return pl.pallas_call(
        body,
        name="vector_table",
        out_shape=jax.ShapeDtypeStruct((devices, LANES), F32),
        compiler_params=params(63),
    )(*parts, *more)


def swap(value):
    return lax.ppermute(value, "seq", [(0, 1), (1, 0)])


def pick(value, index, axis):
    return lax.dynamic_index_in_dim(value, index, axis, keepdims=False)


def reduce_stages(part, order, dp_bits, dp):
    me = lax.axis_index("dp")
    n_halving = dp_bits - 2
    shape = part.shape[1:]
    current = part.reshape((2,) * dp_bits + shape)
    left = list(range(dp_bits - 1, -1, -1))
    for bit in order[:n_halving]:
        axis = left.index(bit)
        mine = (me >> bit) & 1
        pairs = [(i, i ^ (1 << bit)) for i in range(dp)]
        send = pick(current, 1 - mine, axis).astype(BF)
        got = lax.ppermute(send, "dp", pairs)
        keep = pick(current, mine, axis)
        current = (keep.astype(F32) + got.astype(F32)).astype(BF)
        left.remove(bit)
    high, low = left
    group = (((me >> high) & 1) << 1) | ((me >> low) & 1)
    current = current.reshape((4,) + shape)
    total = pick(current, group, 0).astype(F32)
    for other in (1, 2, 3):
        flip = ((other >> 1) << high) | ((other & 1) << low)
        pairs = [(i, i ^ flip) for i in range(dp)]
        send = pick(current, group ^ other, 0).astype(BF)
        total = total + lax.ppermute(send, "dp", pairs).astype(F32)
    return total


def reduce_scatter(grad, order, dp, dp_bits):
    core = lax.axis_index("seq")
    rows = grad.shape[0] // (2 * dp)
    blocks = grad.reshape(dp, 2, rows, grad.shape[1])
    send = pick(blocks, 1 - core, 1).astype(BF)
    keep = pick(blocks, core, 1)
    part = (keep.astype(F32) + swap(send).astype(F32)).astype(BF)
    return reduce_stages(part, order, dp_bits, dp)


LANES = 384


def split_store(acc_ref, keep_ref, send_ref, core, parts, stack):
    rows = keep_ref.shape[2]
    for d in range(acc_ref.shape[0] // (2 * stack * rows)):
        for ref, side in ((keep_ref, core), (send_ref, 1 - core)):
            for r in range(stack):
                value = acc_ref[pl.ds(pl.multiple_of(((2 * d + side) * stack + r) * rows, 8), rows), :].astype(BF)
                for c in range(parts):
                    ref[c * stack + r, d] = value[:, c * LANES : (c + 1) * LANES]


def grad_proj(core, left, right, vectors, more, dp):
    total, m = left.shape
    n = 2 * LANES
    rows = m // (2 * dp)
    deep = rows // 8
    blocks = 3 * deep + 1
    cut = sum(v.shape[1] for v in vectors) // (2 * dp)

    def body(core_ref, l_ref, r_ref, *refs):
        ins = refs[: len(vectors) + len(more)]
        keep_ref, send_ref, acc_ref, table_ref = refs[len(ins) :]
        acc_ref[...] = col_dot(l_ref[...], r_ref[0])
        core = core_ref[0]
        step = pl.program_id(0)
        for ref, side in ((keep_ref, core), (send_ref, 1 - core)):
            for d in range(dp):
                value = acc_ref[pl.ds(pl.multiple_of((2 * d + side) * rows, 8), rows), :].astype(BF)
                for c in range(2):
                    chunk = 2 * step + c
                    first = lax.div(chunk, 3) * blocks + lax.rem(chunk, 3) * deep
                    for r in range(deep):
                        ref[first + r, d] = value[8 * r : 8 * r + 8, c * LANES : (c + 1) * LANES]

        @pl.when(step == 0)
        def _():
            values = [ref[...] for ref in ins[: len(vectors)]]
            for i, ref in enumerate(ins[len(vectors) :]):
                values[i] = values[i] + ref[...]
            joined = jnp.concatenate(values, axis=1)
            table_ref[...] = jnp.zeros_like(table_ref)
            for d in range(2 * dp):
                table_ref[d : d + 1, :cut] = joined[:, d * cut : (d + 1) * cut]
            for ref, side in ((keep_ref, core), (send_ref, 1 - core)):
                for d in range(dp):
                    line = table_ref[pl.ds(2 * d + side, 1), :].astype(BF)
                    ref[blocks - 1, d] = jnp.broadcast_to(line, (8, LANES))
                    ref[2 * blocks - 1, d] = jnp.zeros((8, LANES), BF)

    out = jax.ShapeDtypeStruct((2 * blocks, dp, 8, LANES), BF)
    return pl.pallas_call(
        body,
        name="grad_qkv",
        out_shape=[out, out],
        grid_spec=pltpu.PrefetchScalarGridSpec(
            num_scalar_prefetch=1,
            grid=(3,),
            in_specs=[whole((total, m)), pl.BlockSpec((1, total, n), lambda j, *_: (j, 0, 0))] + [whole(v.shape) for v in (*vectors, *more)],
            out_specs=[whole(out.shape)] * 2,
            scratch_shapes=[pltpu.VMEM((m, n), F32), pltpu.VMEM((2 * dp, LANES), F32)],
        ),
        compiler_params=params(63),
        cost_estimate=pl.CostEstimate(flops=6 * total * m * n, bytes_accessed=6 * n * (total + m), transcendentals=0),
    )(core, left, right, *vectors, *more)


def add_pieces(where, groups, name):
    counts = [len(pieces([jnp.int32(0)] * 3)) for _, _, pieces, _ in groups]
    inputs = [i for g in groups for i in g[0]]
    outputs = [o for g in groups for o in g[1]]

    def body(where_ref, *refs):
        ins = refs[: len(inputs)]
        outs = refs[len(inputs) : len(inputs) + len(outputs)]
        scratch = refs[len(inputs) + len(outputs) :]
        loads, stores, sums = [], [], []
        for n, (group_in, group_out, pieces, _) in enumerate(groups):
            k_ref, g_ref, k_sem, g_sem, o_sem = scratch[5 * n : 5 * n + 5]
            for i, (a, a_at, b, b_at, o, o_at) in enumerate(pieces([where_ref[0], where_ref[1], where_ref[2]])):
                loads.append(pltpu.make_async_copy(ins[a].at[a_at], k_ref.at[i], k_sem.at[i]))
                loads.append(pltpu.make_async_copy(ins[b].at[b_at], g_ref.at[i], g_sem.at[i]))
                stores.append(pltpu.make_async_copy(k_ref.at[i], outs[o].at[o_at], o_sem.at[i]))
                sums.append((k_ref, g_ref, i))
            ins, outs = ins[len(group_in) :], outs[len(group_out) :]
        for load in loads:
            load.start()
        for i, (k_ref, g_ref, at) in enumerate(sums):
            loads[2 * i].wait()
            loads[2 * i + 1].wait()
            k_ref[at] = k_ref[at] + g_ref[at]
            stores[i].start()
        for store in stores:
            store.wait()

    scratch_shapes = []
    for (_, _, _, shape), count in zip(groups, counts):
        scratch_shapes += [pltpu.VMEM((count,) + shape, BF)] * 2 + [pltpu.SemaphoreType.DMA((count,))] * 3
    result = pl.pallas_call(
        body,
        name=name,
        out_shape=[jax.ShapeDtypeStruct(s, BF) for s in outputs],
        grid_spec=pltpu.PrefetchScalarGridSpec(
            num_scalar_prefetch=1,
            grid=(1,),
            in_specs=[ANY] * len(inputs),
            out_specs=[HBM] * len(outputs),
            scratch_shapes=scratch_shapes,
        ),
        compiler_params=params(63),
    )(where, *inputs)
    split = []
    for _, group_out, _, _ in groups:
        split.append(result[: len(group_out)])
        result = result[len(group_out) :]
    return split


def fold_first(keep, got):
    _, blocks, _, _, _, rows, lanes = keep.shape
    every = slice(None)

    def pieces(at):
        _, y, x = at
        table = []
        for role in (1, 0):
            for z in range(4):
                ax = x if role == 0 else 1 - x
                ay = y if role == 0 else 1 - y
                for half, index in ((0, (0, every, z, every, ax)), (1, (1, every, z, ay))):
                    table.append((0, index, 1, index, 2 * half + (1 - role), (every, z)))
        return table

    return (keep, got), [(blocks, 4, 2, rows, lanes)] * 4, pieces, (blocks, 2, rows, lanes)


def fold_second(parts, got):
    blocks, _, _, rows, lanes = parts[1].shape
    every = slice(None)

    def pieces(at):
        _, y, x = at
        table = []
        for role in (1, 0):
            for z in range(4):
                for half, own in ((0, y), (1, x)):
                    index = (every, z, own if role == 0 else 1 - own)
                    table.append((2 * half, index, 2 * half + 1, index, 2 * half + (1 - role), (every, z)))
        return table

    return (parts[1], got[0], parts[3], got[1]), [(blocks, 4, rows, lanes)] * 4, pieces, (blocks, rows, lanes)


def fold_third(parts, got):
    blocks, _, rows, lanes = parts[1].shape
    every = slice(None)

    def pieces(at):
        table = []
        for z in range(4):
            for half in range(2):
                table.append((2 * half, (every, z), 2 * half + 1, (every, z), 0, (z, half)))
        return table

    return (parts[1], got[0], parts[3], got[1]), [(4, 2, blocks, rows, lanes)], pieces, (blocks, rows, lanes)


def fold_last(parts, widths, name, stack=1, extra=0):
    _, _, blocks, deep, lanes = parts.shape
    chunks = sum(widths) // (2 * lanes)
    rows = (blocks * deep - extra) // (chunks * stack)

    def body(part_ref, *outs):
        def take(half, line, count, at, size):
            step = min(deep, count)
            pieces = []
            for start in range(line, line + count, step):
                total = None
                for z in range(4):
                    value = part_ref[z, half, start // deep, start % deep : start % deep + step, at : at + size].astype(F32)
                    total = value if total is None else total + value
                pieces.append(total)
            return pieces[0] if len(pieces) == 1 else jnp.concatenate(pieces, axis=0)

        base = 0
        for out, width in zip(outs, widths):
            tiles = width // 128
            for r in range(stack):
                for t in range(tiles):
                    chunk, at = (base + t * 128) // lanes, (base + t * 128) % lanes
                    line = (chunk % chunks * stack + r) * rows
                    out[pl.ds(r * rows * tiles + t, rows, stride=tiles), :] = take(chunk // chunks, line, rows, at, 128)
            base += width
        if extra:
            outs[-1][...] = take(0, blocks * deep - extra, extra, 0, lanes)

    shapes = [jax.ShapeDtypeStruct((stack * rows * w // 128, 128), F32) for w in widths]
    if extra:
        shapes.append(jax.ShapeDtypeStruct((extra, lanes), F32))
    return pl.pallas_call(body, name=name, out_shape=shapes, compiler_params=params(63))(parts)


def sync(*values):
    return lax.optimization_barrier(values)


def flip(value, bits):
    return lax.ppermute(value, "dp", [(i, i ^ bits) for i in range(16)])


def on_device(tokens, lengths, w_qkv, w_out, w_in, w_back, bias_q, value_bias, bias_out, gain1, shift1, bias_in, bias_back, gain2, shift2, cotangent):
    rows_local, half, width = tokens.shape
    dp = lax.axis_size("dp")
    dp_bits = dp.bit_length() - 1
    core = lax.axis_index("seq")
    rows = rows_local // 2
    length = 2 * half
    total = rows * length
    order_a = (0, 1) + tuple(range(2, dp_bits))
    order_b = (1, 0) + tuple(range(2, dp_bits))

    def send_rows(value):
        return swap(lax.dynamic_slice_in_dim(value, (1 - core) * rows, rows, 0))

    other = send_rows(tokens)
    cot_other = send_rows(cotangent)
    bq, bv, bo, g1, s1, bi, bb, g2, s2 = (bias_q, value_bias, bias_out, gain1, shift1, bias_in, bias_back, gain2, shift2)
    core_one = core.reshape(1).astype(jnp.int32)
    me = lax.axis_index("dp")
    fast = dp == 16 and width == 2 * LANES
    qkv, probs, full_tokens, mixed, low, hat1, inv1, inverse = attention_call(core_one, lengths, tokens, other, w_qkv, w_out, (bq, bv, bo, g1, s1))

    def flat(value):
        return value.reshape(total, value.shape[-1])

    full_tokens = flat(full_tokens)
    output, output_other, cls_own, dpre1, dmixed, g_bias_in, g_gain2, g_shift2, g_bias_back, g_gain1, g_shift1, g_bias_out, *grads = feed_call(
        core_one, lengths, flat(low), w_in, w_back, w_out, flat(mixed), flat(hat1), flat(inv1), flat(inverse), cotangent, cot_other,
        (bi.reshape(1, -1), bb, g1, g2, s2), dp, fast,
    )
    dmixed = dmixed.reshape(rows, length, width)
    cls_own = cls_own[:, : lengths.shape[1]]
    if fast:
        where = jnp.stack([me >> 2, (me >> 1) & 1, me & 1]).astype(jnp.int32)

        def view(value):
            return value.reshape((2, value.shape[0] // 2, 4, 2, 2) + value.shape[2:])

        def cross(parts, bit_a, bit_b):
            return flip(parts[0], bit_a), flip(parts[2], bit_b)

        def along_z(parts):
            return lax.all_to_all(parts, "dp", 0, 0, axis_index_groups=[[i, i + 4, i + 8, i + 12] for i in range(4)], tiled=True)

        keep_b, send_b, keep_i, send_i = grads
        got_b = swap(send_b)
        (back,) = add_pieces(where, [fold_first(view(keep_b), view(got_b))], "fold_a")
        dmixed, back, send_i, output_other = sync(dmixed, back, send_i, output_other)
        got_b = cross(back, 1, 2)
        got_i = swap(send_i)
        output_got = swap(output_other)
        dproj, *bias_a = attention_grad(qkv, probs, mixed, dmixed, 0, 1)
        dproj, got_b, got_i, keep_i, output_got = sync(dproj, got_b, got_i, keep_i, output_got)
        inner, back = add_pieces(where, [fold_first(view(keep_i), view(got_i)), fold_second(back, got_b)], "fold_b")
        dmixed, inner, back = sync(dmixed, inner, back)
        got_i = cross(inner, 1, 2)
        got_b = cross(back, 2, 1)
        dproj, *bias_b = attention_grad(qkv, probs, mixed, dmixed, 1, 1, dproj)
        keep_q, send_q = grad_proj(
            core_one, full_tokens, dproj.reshape(3, total, width),
            (bias_a[0], bias_a[1], g_bias_out, g_gain1, g_shift1, g_bias_in, g_bias_back, g_gain2, g_shift2), bias_b, dp,
        )
        send_q, keep_q, got_b, got_i = sync(send_q, keep_q, got_b, got_i)
        got_q = swap(send_q)
        inner, back = add_pieces(where, [fold_second(inner, got_i), fold_third(back, got_b)], "fold_c")
        inner, back, got_q, keep_q = sync(inner, back, got_q, keep_q)
        got_i = cross(inner, 2, 1)
        got_b = along_z(back[0])
        (proj,) = add_pieces(where, [fold_first(view(keep_q), view(got_q))], "fold_d")
        dproj, proj = sync(dproj, proj)
        got_q = cross(proj, 1, 2)
        dinput, dinput_other = input_grad_call(core_one, dproj.reshape(3, total, width), dpre1, w_qkv, half)
        output, dinput = sync(output, dinput)
        output = lax.dynamic_update_slice_in_dim(output, output_got, (1 - core) * rows, 0)
        output, dinput, dinput_other, got_i, got_q, got_b, cls_own = sync(output, dinput, dinput_other, got_i, got_q, got_b, cls_own)
        inner, proj = add_pieces(where, [fold_third(inner, got_i), fold_second(proj, got_q)], "fold_e")
        inner, proj, dinput_other, cls_own = sync(inner, proj, dinput_other, cls_own)
        got_q = cross(proj, 2, 1)
        got_i = along_z(inner[0])
        cls_got = swap(cls_own)
        dinput_got = swap(dinput_other)
        proj, got_b = sync(proj, got_b)
        (r_back,) = fold_last(got_b, (width,), "back_sum", w_back.shape[0] // width)
        r_back, got_q, cls_got, dinput_got = sync(r_back, got_q, cls_got, dinput_got)
        (proj,) = add_pieces(where, [fold_third(proj, got_q)], "fold_f")
        proj, got_i, dinput = sync(proj, got_i, dinput)
        got_q = along_z(proj[0])
        r_in, r_out = fold_last(got_i, (w_in.shape[1], width), "inner_sum")
        dinput = lax.dynamic_update_slice_in_dim(dinput, dinput_got, (1 - core) * rows, 0)
        r_in, got_q, dinput = sync(r_in, got_q, dinput)
        r_qkv, r_vec = fold_last(got_q, (3 * width,), "proj_sum", 1, 8)
        r_vec = r_vec[0, : (8 * width + w_in.shape[1]) // (2 * dp)]
    else:
        g_back, g_inner = grads
        r_back = reduce_scatter(g_back, order_a, dp, dp_bits)
        r_inner = reduce_scatter(g_inner, order_b, dp, dp_bits)
        r_in, r_out = r_inner[:, :-width], r_inner[:, -width:]
        output_got, cls_got = swap(output_other), swap(cls_own)
        dproj, g_bias_q, g_bias_v = attention_grad(qkv, probs, mixed, dmixed, 0, rows)
        dproj = dproj.reshape(3, total, width)
        g_qkv = jnp.concatenate([weight_grad(full_tokens, dproj[n], width, width, "grad_qkv") for n in range(3)], axis=1)
        r_qkv = reduce_scatter(g_qkv, order_b, dp, dp_bits)
        dinput, dinput_other = input_grad_call(core_one, dproj, dpre1, w_qkv, half)
        dinput_got = swap(dinput_other)
    if not fast:
        table = vector_table((g_bias_q, g_bias_v, g_bias_out, g_gain1, g_shift1, g_bias_in, g_bias_back, g_gain2, g_shift2), 2 * dp)
        r_vec = jnp.sum(lax.all_to_all(table, ("dp", "seq"), 0, 0, tiled=True), axis=0)[: (8 * width + w_in.shape[1]) // (2 * dp)]
        output = lax.dynamic_update_slice_in_dim(output, output_got, (1 - core) * rows, 0)
        dinput = lax.dynamic_update_slice_in_dim(dinput, dinput_got, (1 - core) * rows, 0)
    cls = jnp.where(core == 0, jnp.concatenate([cls_own, cls_got], axis=0), jnp.concatenate([cls_got, cls_own], axis=0))
    return (
        output,
        cls,
        dinput,
        r_qkv.reshape(-1),
        r_out.reshape(-1),
        r_in.reshape(-1),
        r_back.reshape(-1),
        r_vec,
    )


def solution(mesh):
    row = P("dp", "seq", None)
    both = P(("dp", "seq"))
    return jax.shard_map(
        on_device,
        mesh=mesh,
        in_specs=(row, P("dp", None)) + (P(),) * 13 + (row,),
        out_specs=(row, P("dp", None, None), row, both, both, both, both, both),
        check_vma=False,
    )
```

```python
from functools import partial

import jax
import jax.numpy as jnp
from jax import lax
from jax.experimental import pallas as pl
from jax.experimental.pallas import tpu as pltpu
from jax.sharding import PartitionSpec as P

HEADS = 12
EPS = 1e-12
BF = jnp.bfloat16
F32 = jnp.float32
VMEM_LIMIT = 60 << 20
RSQRT2 = 0.7071067811865476
RSQRT2PI = 0.3989422804014327


def row_dot(left, right):
    return lax.dot_general(left, right, (((1,), (0,)), ((), ())), preferred_element_type=F32)


def row_dot_t(left, right):
    return lax.dot_general(left, right, (((1,), (1,)), ((), ())), preferred_element_type=F32)


def col_dot(left, right):
    return lax.dot_general(left, right, (((0,), (0,)), ((), ())), preferred_element_type=F32)


def gelu_pair(value):
    expo = jnp.exp(value * value * -0.5)
    phi = 0.5 + 0.5 * lax.erf(value * RSQRT2)
    return value * phi, phi + value * expo * RSQRT2PI


def whole(shape):
    return pl.BlockSpec(shape, lambda *_: (0,) * len(shape))


ANY = pl.BlockSpec(memory_space=pl.ANY)
HBM = pl.BlockSpec(memory_space=pltpu.HBM)


def params(mib):
    return pltpu.CompilerParams(vmem_limit_bytes=mib << 20)


def row_starts(len_ref, row):
    starts = [jnp.int32(0)]
    for j in range(len_ref.shape[1] - 1):
        starts.append(starts[-1] + len_ref[row, j])
    return starts


def attention_kernel(
    core_ref, len_ref, own_ref, other_ref, wqkv_hbm, wout_hbm, bq_ref, bv_ref, bo_ref, g1_ref, s1_ref,
    qkv_hbm, probs_hbm, x_ref, mixed_ref, low_ref, hat1_ref, inv1_ref, scale_ref,
    bias_ref, ahead0_ref, ahead1_ref, qkv_ref, wqkv_ref, wout_ref, p_ref, w_sem, p_sem, q_sem,
):
    step = pl.program_id(0)
    core = core_ref[0]
    rows = pl.num_programs(0)
    half, width = own_ref.shape[1:]
    length = 2 * half
    pairs = width // 128
    parts = [slice(n * width, (n + 1) * width) for n in range(3)]
    copies = [pltpu.make_async_copy(wqkv_hbm.at[:, part], wqkv_ref.at[:, part], w_sem.at[n]) for n, part in enumerate(parts)]
    copies.append(pltpu.make_async_copy(wout_hbm, wout_ref, w_sem.at[3]))

    @pl.when(step == 0)
    def _():
        for copy in copies:
            copy.start()

    x_ref[0, pl.ds(pl.multiple_of(core * half, half), half), :] = own_ref[0]
    x_ref[0, pl.ds(pl.multiple_of((1 - core) * half, half), half), :] = other_ref[0]
    starts = row_starts(len_ref, core * rows + step)
    down = lax.broadcasted_iota(jnp.int32, (length, 1), 0)
    across = lax.broadcasted_iota(jnp.int32, (1, length), 1)
    seg_down = jnp.zeros((length, 1), jnp.int32)
    seg_across = jnp.zeros((1, length), jnp.int32)
    for start in starts[1:]:
        seg_down += (down >= start).astype(jnp.int32)
        seg_across += (across >= start).astype(jnp.int32)
    bias_ref[...] = jnp.where(seg_down == seg_across, 0.0, -1e30)

    for n, part in enumerate(parts):
        @pl.when(step == 0)
        def _():
            copies[n].wait()

        value = row_dot(x_ref[0], wqkv_ref[:, part])
        if n == 0:
            value = (value + bq_ref[...]) * (width // HEADS) ** -0.5
        if n == 2:
            value = value + bv_ref[...]
        qkv_ref[:, part] = value.astype(BF)
    save = pltpu.make_async_copy(qkv_ref, qkv_hbm.at[step], q_sem)
    save.start()

    first = lax.broadcasted_iota(jnp.int32, (1, 128), 1) < 64

    def columns(part, pair):
        return pl.ds(pl.multiple_of(part * width + pair * 128, 128), 128)

    def scores(pair, into):
        q_pair = qkv_ref[:, columns(0, pair)]
        k_pair = qkv_ref[:, columns(1, pair)]
        for h in range(2):
            on = first if h == 0 else jnp.logical_not(first)
            into[h] = row_dot_t(jnp.where(on, q_pair, jnp.zeros_like(q_pair)), k_pair)

    def finish(pair, held, slot):
        out_copy = pltpu.make_async_copy(p_ref.at[slot], probs_hbm.at[step, pair], p_sem.at[slot])

        @pl.when(pair >= 2)
        def _():
            out_copy.wait()

        v_pair = qkv_ref[:, columns(2, pair)]
        outs = []
        for h in range(2):
            on = first if h == 0 else jnp.logical_not(first)
            s = held[h] + bias_ref[...]
            e = jnp.exp(s - jnp.max(s, axis=-1, keepdims=True)).astype(BF)
            p_ref[slot, h] = e
            outs.append(row_dot(e, jnp.where(on, v_pair, jnp.ones_like(v_pair))))
        sums = pltpu.roll(jnp.where(first, outs[1], outs[0]), 64, 1)
        inverse = 1.0 / sums
        scale_ref[0, :, columns(0, pair)] = inverse
        mixed_ref[0, :, columns(0, pair)] = (jnp.where(first, outs[0], outs[1]) * inverse).astype(BF)
        out_copy.start()

    scores(0, ahead0_ref)

    def two_pairs(i, carry):
        scores(2 * i + 1, ahead1_ref)
        finish(2 * i, ahead0_ref, 0)
        scores(jnp.minimum(2 * i + 2, pairs - 1), ahead0_ref)
        finish(2 * i + 1, ahead1_ref, 1)
        return carry

    lax.fori_loop(0, pairs // 2, two_pairs, 0, unroll=True)
    for tail in (pairs - 2, pairs - 1):
        pltpu.make_async_copy(p_ref.at[tail % 2], probs_hbm.at[step, tail], p_sem.at[tail % 2]).wait()

    @pl.when(step == 0)
    def _():
        copies[3].wait()

    pre = x_ref[0].astype(F32) + row_dot(mixed_ref[0], wout_ref[...]) + bo_ref[...]
    center = pre - jnp.mean(pre, axis=-1, keepdims=True)
    inv = lax.rsqrt(jnp.mean(center * center, axis=-1, keepdims=True) + EPS)
    hat = center * inv
    hat1_ref[0] = hat.astype(BF)
    inv1_ref[0] = inv
    low_ref[0] = (hat * g1_ref[...] + s1_ref[...]).astype(BF)
    save.wait()


def attention_call(core, lengths, tokens, other, w_qkv, w_out, vectors):
    rows_local, half, width = tokens.shape
    rows = rows_local // 2
    length = 2 * half
    pairs = width // 128

    def full(n):
        return pl.BlockSpec((1, length, n), lambda r, *_: (r, 0, 0))

    def row(n, kind=BF):
        return jax.ShapeDtypeStruct((rows, length, n), kind)

    return pl.pallas_call(
        attention_kernel,
        name="attention_rows",
        out_shape=[
            row(3 * width), jax.ShapeDtypeStruct((rows, pairs, 2, length, length), BF), row(width), row(width), row(width), row(width),
            row(1, F32), row(width, F32),
        ],
        grid_spec=pltpu.PrefetchScalarGridSpec(
            num_scalar_prefetch=2,
            grid=(rows,),
            in_specs=[
                pl.BlockSpec((1, half, width), lambda r, core, lens: (core[0] * rows + r, 0, 0)),
                pl.BlockSpec((1, half, width), lambda r, *_: (r, 0, 0)),
                ANY,
                ANY,
            ]
            + [whole(v.shape) for v in vectors],
            out_specs=[HBM, HBM] + [full(width)] * 4 + [full(1), full(width)],
            scratch_shapes=[
                pltpu.VMEM((length, length), F32),
                pltpu.VMEM((2, length, length), F32),
                pltpu.VMEM((2, length, length), F32),
                pltpu.VMEM((length, 3 * width), BF),
                pltpu.VMEM(w_qkv.shape, BF),
                pltpu.VMEM(w_out.shape, BF),
                pltpu.VMEM((2, 2, length, length), BF),
                pltpu.SemaphoreType.DMA((4,)),
                pltpu.SemaphoreType.DMA((2,)),
                pltpu.SemaphoreType.DMA,
            ],
        ),
        compiler_params=params(60),
        cost_estimate=pl.CostEstimate(
            flops=8 * rows * length * width * width + 4 * rows * length * length * width,
            bytes_accessed=35 << 20,
            transcendentals=rows * HEADS * length * length,
        ),
    )(core, lengths, tokens, other, w_qkv, w_out, *vectors)


def feed_kernel(
    split, core_ref, len_ref, low_ref, win_hbm, wback_hbm, wout_hbm, mixed_hbm, hat1_hbm, inv1_hbm, scale_hbm, cot_hbm, cot_other_hbm,
    bi_ref, bb_ref, g1_ref, g2_ref, s2_ref,
    out_hbm, other_hbm, cls_ref, dpre_hbm, dmixed_hbm, gi_ref, gg2_ref, gs2_ref, gb2_ref, gg1_ref, gs1_ref, gb1_ref, *rest
):
    n_grads = 4 if split else 2
    grads = rest[:n_grads]
    (win_ref, wback_ref, wout_ref, mixed_ref, hat1_ref, inv1_ref, scale_ref, cot_ref, out_ref, act_ref, slope_ref, acc_ref, dfeed_ref,
     grad_ref, w_sem, v_sem, c_sem, o_sem, d_sem) = rest[n_grads:]
    step = pl.program_id(0)
    core = core_ref[0]
    total, width = low_ref.shape
    length = 2 * cot_other_hbm.shape[1]
    half = length // 2
    group = total // length
    hidden = act_ref.shape[1]
    chunk = width
    chunks = hidden // chunk
    piece = 768
    pieces = [slice(n * piece, (n + 1) * piece) for n in range(chunk // piece)]
    weights = []
    for c in range(chunks):
        part = slice(c * chunk, (c + 1) * chunk)
        weights.append(pltpu.make_async_copy(win_hbm.at[:, part], win_ref.at[:, part], w_sem.at[2 * c]))
        weights.append(pltpu.make_async_copy(wback_hbm.at[part], wback_ref.at[part], w_sem.at[2 * c + 1]))
    values = [
        pltpu.make_async_copy(src, dst, v_sem.at[i])
        for i, (src, dst) in enumerate(
            ((hat1_hbm, hat1_ref), (inv1_hbm, inv1_ref), (wout_hbm, wout_ref), (scale_hbm, scale_ref), (mixed_hbm, mixed_ref))
        )
    ]
    loads, stores = [], []
    for r in range(group):
        own = pl.ds(pl.multiple_of(r * length + core * half, half), half)
        other = pl.ds(pl.multiple_of(r * length + (1 - core) * half, half), half)
        loads.append(pltpu.make_async_copy(cot_hbm.at[core * group + r], cot_ref.at[own], c_sem.at[r]))
        loads.append(pltpu.make_async_copy(cot_other_hbm.at[r], cot_ref.at[other], c_sem.at[group + r]))
        stores.append(pltpu.make_async_copy(out_ref.at[other], other_hbm.at[r], o_sem.at[group + r]))
        stores.append(pltpu.make_async_copy(out_ref.at[own], out_hbm.at[core * group + r], o_sem.at[r]))
    dpre_store = pltpu.make_async_copy(out_ref, dpre_hbm, d_sem.at[0])
    dmixed_store = pltpu.make_async_copy(cot_ref, dmixed_hbm, d_sem.at[1])

    @pl.when(step == 0)
    def _():
        for copy in weights + loads + values:
            copy.start()

    for c in range(chunks):
        @pl.when(step == c)
        def _():
            weights[2 * c].wait()
            weights[2 * c + 1].wait()

    @pl.when(step < chunks)
    def _():
        base = pl.multiple_of(step * chunk, chunk)
        for n in range(len(pieces)):
            cols = pl.ds(base + n * piece, piece)
            act, slope = gelu_pair(row_dot(low_ref[...], win_ref[:, cols]) + bi_ref[:, cols])
            act_ref[:, cols] = act.astype(BF)
            slope_ref[:, cols] = slope.astype(BF)
        rows = pl.ds(base, chunk)

        @pl.when(step == 0)
        def _():
            for cols in pieces:
                acc_ref[:, cols] = row_dot(act_ref[:, rows], wback_ref[rows, cols])

        @pl.when(step > 0)
        def _():
            for cols in pieces:
                acc_ref[:, cols] += row_dot(act_ref[:, rows], wback_ref[rows, cols])

    block = 256

    @pl.when(step == chunks - 1)
    def _():
        for load in loads:
            load.wait()
        gg2_ref[...] = jnp.zeros_like(gg2_ref)
        gs2_ref[...] = jnp.zeros_like(gs2_ref)
        gb2_ref[...] = jnp.zeros_like(gb2_ref)

        def token_body(i, carry):
            at = pl.ds(pl.multiple_of(i * block, block), block)
            pre = low_ref[at, :].astype(F32) + acc_ref[at, :] + bb_ref[...]
            center = pre - jnp.mean(pre, axis=-1, keepdims=True)
            inv = lax.rsqrt(jnp.mean(center * center, axis=-1, keepdims=True) + EPS)
            hat = center * inv
            out_ref[at, :] = (hat * g2_ref[...] + s2_ref[...]).astype(BF)
            dy = cot_ref[at, :].astype(F32)
            gg2_ref[...] += jnp.sum(dy * hat, axis=0, keepdims=True)
            gs2_ref[...] += jnp.sum(dy, axis=0, keepdims=True)
            g = dy * g2_ref[...]
            dpre = inv * (g - jnp.mean(g, axis=-1, keepdims=True) - hat * jnp.mean(g * hat, axis=-1, keepdims=True))
            dfeed = dpre.astype(BF)
            dfeed_ref[at, :] = dfeed
            gb2_ref[...] += jnp.sum(dfeed.astype(F32), axis=0, keepdims=True)
            return carry

        lax.fori_loop(0, total // block, token_body, 0)
        for store in stores:
            store.start()
        which = lax.broadcasted_iota(jnp.int32, (8, 1), 0)
        across = lax.broadcasted_iota(jnp.int32, (1, length), 1)
        for r in range(group):
            down = jnp.full((8, 1), -1, jnp.int32)
            for j, start in enumerate(row_starts(len_ref, core * group + r)):
                down = jnp.where(which == j, start, down)
            choose = (down == across).astype(F32).astype(BF)
            cls_ref[r] = row_dot(choose, out_ref[r * length : (r + 1) * length]).astype(BF)

    def put_grad(value, kept, sent, stack):
        if split:
            grad_ref[...] = value
            split_store(grad_ref, kept, sent, core, 2, stack)
        else:
            kept[...] = value.astype(BF)

    keep_b, keep_i = grads[0], grads[n_grads // 2]
    send_b, send_i = (grads[1], grads[3]) if split else (None, None)

    @pl.when(jnp.logical_and(step >= chunks, step < 2 * chunks))
    def _():
        base = pl.multiple_of((step - chunks) * chunk, chunk)
        rows = pl.ds(base, chunk)
        put_grad(col_dot(act_ref[:, rows], dfeed_ref[...]), keep_b, send_b, chunks)
        for n in range(len(pieces)):
            cols = pl.ds(base + n * piece, piece)
            inner = (row_dot_t(dfeed_ref[...], wback_ref[cols, :]) * slope_ref[:, cols].astype(F32)).astype(BF)
            slope_ref[:, cols] = inner
            gi_ref[:, cols] = jnp.sum(inner.astype(F32), axis=0, keepdims=True)

        @pl.when(step == chunks)
        def _():
            for cols in pieces:
                acc_ref[:, cols] = row_dot_t(slope_ref[:, rows], win_ref[cols, rows])

        @pl.when(step > chunks)
        def _():
            for cols in pieces:
                acc_ref[:, cols] += row_dot_t(slope_ref[:, rows], win_ref[cols, rows])

        put_grad(col_dot(low_ref[...], slope_ref[:, rows]), keep_i, send_i, 1)

    @pl.when(step == 2 * chunks)
    def _():
        for store in stores:
            store.wait()
        for value in values:
            value.wait()
        gg1_ref[...] = jnp.zeros_like(gg1_ref)
        gs1_ref[...] = jnp.zeros_like(gs1_ref)
        gb1_ref[...] = jnp.zeros_like(gb1_ref)

        def token_body(i, carry):
            at = pl.ds(pl.multiple_of(i * block, block), block)
            dn = dfeed_ref[at, :].astype(F32) + acc_ref[at, :]
            hat = hat1_ref[at, :].astype(F32)
            gg1_ref[...] += jnp.sum(dn * hat, axis=0, keepdims=True)
            gs1_ref[...] += jnp.sum(dn, axis=0, keepdims=True)
            g = dn * g1_ref[...]
            dpre = inv1_ref[at, :] * (g - jnp.mean(g, axis=-1, keepdims=True) - hat * jnp.mean(g * hat, axis=-1, keepdims=True))
            branch = dpre.astype(BF)
            out_ref[at, :] = branch
            gb1_ref[...] += jnp.sum(branch.astype(F32), axis=0, keepdims=True)
            return carry

        lax.fori_loop(0, total // block, token_body, 0)
        dpre_store.start()
        for cols in pieces:
            cot_ref[:, cols] = (row_dot_t(out_ref[...], wout_ref[cols, :]) * scale_ref[:, cols]).astype(BF)
        dmixed_store.start()
        put_grad(col_dot(mixed_ref[...], out_ref[...]), keep_i, send_i, 1)
        dpre_store.wait()
        dmixed_store.wait()


def feed_call(core, lengths, low, w_in, w_back, w_out, mixed, hat1, inv1, scale, cot, cot_other, vectors, dp, split):
    total, width = low.shape
    half = cot.shape[1]
    group = cot.shape[0] // 2
    hidden = w_in.shape[1]
    chunks = hidden // width

    def in_back(j):
        return jnp.clip(j - chunks, 0, chunks - 1)

    def in_inner(j):
        return jnp.clip(j - chunks, 0, chunks)

    one = jax.ShapeDtypeStruct((1, width), F32)
    row = jax.ShapeDtypeStruct((total, width), BF)
    shapes = [
        jax.ShapeDtypeStruct(cot.shape, BF),
        jax.ShapeDtypeStruct(cot_other.shape, BF),
        jax.ShapeDtypeStruct((group, 8, width), BF),
        row,
        row,
        jax.ShapeDtypeStruct((1, hidden), F32),
    ] + [one] * 6
    specs = [HBM, HBM, whole((group, 8, width)), HBM, HBM, whole((1, hidden))] + [whole((1, width))] * 6
    if split:
        rows_i = width // (2 * dp)
        devices = dp // chunks
        shapes += [jax.ShapeDtypeStruct((2 * chunks, dp, rows_i, LANES), BF)] * 2
        specs += [pl.BlockSpec((2 * chunks, devices, rows_i, LANES), lambda j, *_: (0, in_back(j), 0, 0))] * 2
        shapes += [jax.ShapeDtypeStruct((2 * (chunks + 1), dp, rows_i, LANES), BF)] * 2
        specs += [pl.BlockSpec((2, dp, rows_i, LANES), lambda j, *_: (in_inner(j), 0, 0, 0))] * 2
    else:
        shapes += [jax.ShapeDtypeStruct((hidden, width), BF), jax.ShapeDtypeStruct((width, hidden + width), BF)]
        specs += [pl.BlockSpec((width, width), lambda j, *_: (in_back(j), 0)), pl.BlockSpec((width, width), lambda j, *_: (0, in_inner(j)))]
    return pl.pallas_call(
        partial(feed_kernel, split),
        name="feed_rows",
        out_shape=shapes,
        grid_spec=pltpu.PrefetchScalarGridSpec(
            num_scalar_prefetch=2,
            grid=(2 * chunks + 1,),
            in_specs=[pl.BlockSpec((total, width), lambda *_: (0, 0), pipeline_mode=pl.Buffered(1))]
            + [ANY] * 9
            + [whole((1, hidden))]
            + [whole((width,))] * 4,
            out_specs=specs,
            scratch_shapes=[
                pltpu.VMEM(w_in.shape, BF),
                pltpu.VMEM(w_back.shape, BF),
                pltpu.VMEM(w_out.shape, BF),
                pltpu.VMEM((total, width), BF),
                pltpu.VMEM((total, width), BF),
                pltpu.VMEM((total, 1), F32),
                pltpu.VMEM((total, width), F32),
                pltpu.VMEM((total, width), BF),
                pltpu.VMEM((total, width), BF),
                pltpu.VMEM((total, hidden), BF),
                pltpu.VMEM((total, hidden), BF),
                pltpu.VMEM((total, width), F32),
                pltpu.VMEM((total, width), BF),
                pltpu.VMEM((width, width), F32),
                pltpu.SemaphoreType.DMA((2 * chunks,)),
                pltpu.SemaphoreType.DMA((5,)),
                pltpu.SemaphoreType.DMA((2 * group,)),
                pltpu.SemaphoreType.DMA((2 * group,)),
                pltpu.SemaphoreType.DMA((2,)),
            ],
        ),
        compiler_params=params(60),
        cost_estimate=pl.CostEstimate(flops=2 * total * width * (6 * hidden + 2 * width), bytes_accessed=40 << 20, transcendentals=2 * total * hidden),
    )(core, lengths, low, w_in, w_back, w_out, mixed, hat1, inv1, scale, cot, cot_other, *vectors)


def weight_grad(left, right, block_m, block_n, name):
    total, m = left.shape
    n = right.shape[1]

    def body(l_ref, r_ref, o_ref, t_ref):
        @pl.when(pl.program_id(1) == 0)
        def _():
            t_ref[...] = l_ref[...].T

        o_ref[...] = row_dot(t_ref[...], r_ref[...]).astype(BF)

    return pl.pallas_call(
        body,
        name=name,
        out_shape=jax.ShapeDtypeStruct((m, n), BF),
        grid=(m // block_m, n // block_n),
        in_specs=[pl.BlockSpec((total, block_m), lambda i, j: (0, i)), pl.BlockSpec((total, block_n), lambda i, j: (0, j))],
        out_specs=pl.BlockSpec((block_m, block_n), lambda i, j: (i, j)),
        scratch_shapes=[pltpu.VMEM((block_m, total), BF)],
        compiler_params=params(63),
        cost_estimate=pl.CostEstimate(flops=2 * total * m * n, bytes_accessed=2 * (total * (m + n) + m * n), transcendentals=0),
    )(left, right)


def attention_grad(qkv, probs, mixed, d, lower, count, partial_out=None):
    rows, length, width = mixed.shape
    pairs = width // 128
    scale = (width // HEADS) ** -0.5
    more = [] if partial_out is None else [partial_out]

    def body(q_ref, k_ref, v_ref, p_ref, m_ref, d_ref, *rest):
        out_ref, bq_ref, bv_ref = rest[-3:]

        @pl.when(pl.program_id(1) == 0)
        def _():
            bq_ref[...] = jnp.zeros_like(bq_ref)
            bv_ref[...] = jnp.zeros_like(bv_ref)

        first = lax.broadcasted_iota(jnp.int32, (1, 128), 1) < 64
        q, k, v, d = q_ref[0], k_ref[0], v_ref[0], d_ref[0]
        product = d.astype(F32) * m_ref[0].astype(F32)
        q_t, d_t, k_t = q.T, d.T, k.T
        dqs, dks, dvs = [], [], []
        for h in range(2):
            on = first if h == 0 else jnp.logical_not(first)
            part = slice(h * 64, (h + 1) * 64)
            delta = jnp.sum(jnp.where(on, product, 0.0), axis=-1, keepdims=True)
            dprobs = row_dot_t(jnp.where(on, d, jnp.zeros_like(d)), v)
            p = p_ref[0, 0, h]
            ds = (p.astype(F32) * (dprobs - delta)).astype(BF)
            dqs.append(row_dot_t(k_t[part], ds))
            dks.append(row_dot(q_t[part], ds))
            dvs.append(row_dot(d_t[part], p))
        dq = (jnp.concatenate(dqs, axis=0) * scale).T.astype(BF)
        dv = jnp.concatenate(dvs, axis=0).T.astype(BF)
        out_ref[0, 0] = dq
        out_ref[1, 0] = jnp.concatenate(dks, axis=0).T.astype(BF)
        out_ref[2, 0] = dv
        bq_ref[...] += jnp.sum(dq.astype(F32), axis=0, keepdims=True)
        bv_ref[...] += jnp.sum(dv.astype(F32), axis=0, keepdims=True)

    def cols(base):
        return pl.BlockSpec((1, length, 128), lambda p, r: (lower + r, 0, base + p))

    vec = pl.BlockSpec((1, 128), lambda p, r: (0, p))
    one = jax.ShapeDtypeStruct((1, width), F32)
    return pl.pallas_call(
        body,
        name="attention_grad",
        out_shape=[jax.ShapeDtypeStruct((3, rows, length, width), BF), one, one],
        grid=(pairs, count),
        input_output_aliases={6: 0} if more else {},
        in_specs=[cols(0), cols(pairs), cols(2 * pairs), pl.BlockSpec((1, 1, 2, length, length), lambda p, r: (lower + r, p, 0, 0, 0)), cols(0), cols(0)]
        + [ANY] * len(more),
        out_specs=[pl.BlockSpec((3, 1, length, 128), lambda p, r: (0, lower + r, 0, p)), vec, vec],
        compiler_params=params(63),
        cost_estimate=pl.CostEstimate(flops=8 * count * length * length * width, bytes_accessed=(15 * count) << 20, transcendentals=0),
    )(qkv, qkv, qkv, probs, mixed, d, *more)


def input_grad_call(core, dproj, dpre, w_qkv, half):
    _, total, width = dproj.shape
    length = 2 * half
    group = total // length

    def body(core_ref, p_ref, d_hbm, w_ref, own_hbm, other_hbm, acc_ref, out_ref, d_ref, sem, d_sem):
        step = pl.program_id(0)
        load = pltpu.make_async_copy(d_hbm, d_ref, d_sem)
        core = core_ref[0]

        @pl.when(step == 0)
        def _():
            load.start()

        value = row_dot_t(p_ref[0], w_ref[...])

        @pl.when(step == 0)
        def _():
            acc_ref[...] = value

        @pl.when(step == 1)
        def _():
            acc_ref[...] += value

        @pl.when(step == 2)
        def _():
            load.wait()
            out_ref[...] = (acc_ref[...] + value + d_ref[...].astype(F32)).astype(BF)
            stores = []
            for r in range(group):
                other = pl.ds(pl.multiple_of(r * length + (1 - core) * half, half), half)
                own = pl.ds(pl.multiple_of(r * length + core * half, half), half)
                stores.append(pltpu.make_async_copy(out_ref.at[other], other_hbm.at[r], sem.at[r]))
                stores.append(pltpu.make_async_copy(out_ref.at[own], own_hbm.at[core * group + r], sem.at[group + r]))
            for store in stores:
                store.start()
            for store in stores:
                store.wait()

    return pl.pallas_call(
        body,
        name="input_grad",
        out_shape=[jax.ShapeDtypeStruct((2 * group, half, width), BF), jax.ShapeDtypeStruct((group, half, width), BF)],
        grid_spec=pltpu.PrefetchScalarGridSpec(
            num_scalar_prefetch=1,
            grid=(3,),
            in_specs=[
                pl.BlockSpec((1, total, width), lambda n, *_: (n, 0, 0)),
                ANY,
                pl.BlockSpec((width, width), lambda n, *_: (0, n)),
            ],
            out_specs=[HBM, HBM],
            scratch_shapes=[pltpu.VMEM((total, width), F32), pltpu.VMEM((total, width), BF), pltpu.VMEM((total, width), BF), pltpu.SemaphoreType.DMA((2 * group,)), pltpu.SemaphoreType.DMA],
        ),
        compiler_params=params(63),
        cost_estimate=pl.CostEstimate(flops=6 * total * width * width, bytes_accessed=10 << 20, transcendentals=0),
    )(core, dproj, dpre, w_qkv)


def vector_table(parts, devices, more=()):
    cut = sum(p.shape[1] for p in parts) // devices

    def body(*refs):
        *ins, out = refs
        values = [ref[...] for ref in ins[: len(parts)]]
        for i, ref in enumerate(ins[len(parts) :]):
            values[i] = values[i] + ref[...]
        joined = jnp.concatenate(values, axis=1)
        out[...] = jnp.zeros_like(out)
        for d in range(devices):
            out[d : d + 1, :cut] = joined[:, d * cut : (d + 1) * cut]

    return pl.pallas_call(
        body,
        name="vector_table",
        out_shape=jax.ShapeDtypeStruct((devices, LANES), F32),
        compiler_params=params(63),
    )(*parts, *more)


def swap(value):
    return lax.ppermute(value, "seq", [(0, 1), (1, 0)])


def pick(value, index, axis):
    return lax.dynamic_index_in_dim(value, index, axis, keepdims=False)


def reduce_stages(part, order, dp_bits, dp):
    me = lax.axis_index("dp")
    n_halving = dp_bits - 2
    shape = part.shape[1:]
    current = part.reshape((2,) * dp_bits + shape)
    left = list(range(dp_bits - 1, -1, -1))
    for bit in order[:n_halving]:
        axis = left.index(bit)
        mine = (me >> bit) & 1
        pairs = [(i, i ^ (1 << bit)) for i in range(dp)]
        send = pick(current, 1 - mine, axis).astype(BF)
        got = lax.ppermute(send, "dp", pairs)
        keep = pick(current, mine, axis)
        current = (keep.astype(F32) + got.astype(F32)).astype(BF)
        left.remove(bit)
    high, low = left
    group = (((me >> high) & 1) << 1) | ((me >> low) & 1)
    current = current.reshape((4,) + shape)
    total = pick(current, group, 0).astype(F32)
    for other in (1, 2, 3):
        flip = ((other >> 1) << high) | ((other & 1) << low)
        pairs = [(i, i ^ flip) for i in range(dp)]
        send = pick(current, group ^ other, 0).astype(BF)
        total = total + lax.ppermute(send, "dp", pairs).astype(F32)
    return total


def reduce_scatter(grad, order, dp, dp_bits):
    core = lax.axis_index("seq")
    rows = grad.shape[0] // (2 * dp)
    blocks = grad.reshape(dp, 2, rows, grad.shape[1])
    send = pick(blocks, 1 - core, 1).astype(BF)
    keep = pick(blocks, core, 1)
    part = (keep.astype(F32) + swap(send).astype(F32)).astype(BF)
    return reduce_stages(part, order, dp_bits, dp)


LANES = 384


def split_store(acc_ref, keep_ref, send_ref, core, parts, stack):
    rows = keep_ref.shape[2]
    for d in range(acc_ref.shape[0] // (2 * stack * rows)):
        for ref, side in ((keep_ref, core), (send_ref, 1 - core)):
            for r in range(stack):
                value = acc_ref[pl.ds(pl.multiple_of(((2 * d + side) * stack + r) * rows, 8), rows), :].astype(BF)
                for c in range(parts):
                    ref[c * stack + r, d] = value[:, c * LANES : (c + 1) * LANES]


def grad_proj(core, left, right, vectors, more, dp):
    total, m = left.shape
    n = 2 * LANES
    rows = m // (2 * dp)
    deep = rows // 8
    blocks = 3 * deep + 1
    cut = sum(v.shape[1] for v in vectors) // (2 * dp)

    def body(core_ref, l_ref, r_ref, *refs):
        ins = refs[: len(vectors) + len(more)]
        keep_hbm, send_hbm, keep_ref, send_ref, acc_ref, table_ref, o_sem = refs[len(ins) :]
        acc_ref[...] = col_dot(l_ref[...], r_ref[0])
        core = core_ref[0]
        step = pl.program_id(0)
        for ref, side in ((keep_ref, core), (send_ref, 1 - core)):
            for d in range(dp):
                value = acc_ref[pl.ds(pl.multiple_of((2 * d + side) * rows, 8), rows), :].astype(BF)
                for c in range(2):
                    chunk = 2 * step + c
                    first = lax.div(chunk, 3) * blocks + lax.rem(chunk, 3) * deep
                    for r in range(deep):
                        ref[first + r, d] = value[8 * r : 8 * r + 8, c * LANES : (c + 1) * LANES]

        @pl.when(step == 0)
        def _():
            values = [ref[...] for ref in ins[: len(vectors)]]
            for i, ref in enumerate(ins[len(vectors) :]):
                values[i] = values[i] + ref[...]
            joined = jnp.concatenate(values, axis=1)
            table_ref[...] = jnp.zeros_like(table_ref)
            for d in range(2 * dp):
                table_ref[d : d + 1, :cut] = joined[:, d * cut : (d + 1) * cut]
            for ref, side in ((keep_ref, core), (send_ref, 1 - core)):
                for d in range(dp):
                    line = table_ref[pl.ds(2 * d + side, 1), :].astype(BF)
                    ref[blocks - 1, d] = jnp.broadcast_to(line, (8, LANES))
                    ref[2 * blocks - 1, d] = jnp.zeros((8, LANES), BF)

        stretches = [
            [(0, 2 * deep), (blocks - 1, blocks), (2 * blocks - 1, 2 * blocks)],
            [(2 * deep, 3 * deep), (blocks, blocks + deep)],
            [(blocks + deep, blocks + 3 * deep)],
        ]
        stores, count = [], 0
        for group in stretches:
            copies = []
            for start, stop in group:
                for src, dst in ((keep_ref, keep_hbm), (send_ref, send_hbm)):
                    copies.append(pltpu.make_async_copy(src.at[start:stop], dst.at[start:stop], o_sem.at[count]))
                    count += 1
            stores.append(copies)
        for n, copies in enumerate(stores):
            @pl.when(step == n)
            def _():
                for copy in copies:
                    copy.start()

        @pl.when(step == 2)
        def _():
            for copies in stores:
                for copy in copies:
                    copy.wait()

    out = jax.ShapeDtypeStruct((2 * blocks, dp, 8, LANES), BF)
    return pl.pallas_call(
        body,
        name="grad_qkv",
        out_shape=[out, out],
        grid_spec=pltpu.PrefetchScalarGridSpec(
            num_scalar_prefetch=1,
            grid=(3,),
            in_specs=[whole((total, m)), pl.BlockSpec((1, total, n), lambda j, *_: (j, 0, 0))] + [whole(v.shape) for v in (*vectors, *more)],
            out_specs=[HBM] * 2,
            scratch_shapes=[pltpu.VMEM(out.shape, BF)] * 2 + [pltpu.VMEM((m, n), F32), pltpu.VMEM((2 * dp, LANES), F32), pltpu.SemaphoreType.DMA((12,))],
        ),
        compiler_params=params(63),
        cost_estimate=pl.CostEstimate(flops=6 * total * m * n, bytes_accessed=6 * n * (total + m), transcendentals=0),
    )(core, left, right, *vectors, *more)


def add_pieces(where, groups, name):
    counts = [len(pieces([jnp.int32(0)] * 3)) for _, _, pieces, _ in groups]
    inputs = [i for g in groups for i in g[0]]
    outputs = [o for g in groups for o in g[1]]

    def body(where_ref, *refs):
        ins = refs[: len(inputs)]
        outs = refs[len(inputs) : len(inputs) + len(outputs)]
        scratch = refs[len(inputs) + len(outputs) :]
        loads, stores, sums = [], [], []
        for n, (group_in, group_out, pieces, _) in enumerate(groups):
            k_ref, g_ref, k_sem, g_sem, o_sem = scratch[5 * n : 5 * n + 5]
            for i, (a, a_at, b, b_at, o, o_at) in enumerate(pieces([where_ref[0], where_ref[1], where_ref[2]])):
                loads.append(pltpu.make_async_copy(ins[a].at[a_at], k_ref.at[i], k_sem.at[i]))
                loads.append(pltpu.make_async_copy(ins[b].at[b_at], g_ref.at[i], g_sem.at[i]))
                stores.append(pltpu.make_async_copy(k_ref.at[i], outs[o].at[o_at], o_sem.at[i]))
                sums.append((k_ref, g_ref, i))
            ins = ins[len(group_in) :]
            if n + 1 < len(groups) and groups[n + 1][1]:
                outs = outs[len(group_out) :]
        for load in loads:
            load.start()
        for i, (k_ref, g_ref, at) in enumerate(sums):
            loads[2 * i].wait()
            loads[2 * i + 1].wait()
            k_ref[at] = k_ref[at] + g_ref[at]
            stores[i].start()
        for store in stores:
            store.wait()

    scratch_shapes = []
    for (_, _, _, shape), count in zip(groups, counts):
        scratch_shapes += [pltpu.VMEM((count,) + shape, BF)] * 2 + [pltpu.SemaphoreType.DMA((count,))] * 3
    result = pl.pallas_call(
        body,
        name=name,
        out_shape=[jax.ShapeDtypeStruct(s, BF) for s in outputs],
        grid_spec=pltpu.PrefetchScalarGridSpec(
            num_scalar_prefetch=1,
            grid=(1,),
            in_specs=[ANY] * len(inputs),
            out_specs=[HBM] * len(outputs),
            scratch_shapes=scratch_shapes,
        ),
        compiler_params=params(63),
    )(where, *inputs)
    split = []
    for _, group_out, _, _ in groups:
        split.append(result[: len(group_out)])
        result = result[len(group_out) :]
    return split


def fold_first(keep, got):
    _, blocks, _, _, _, rows, lanes = keep.shape
    every = slice(None)

    def pieces(at):
        _, y, x = at
        table = []
        for role in (1, 0):
            for z in range(4):
                ax = x if role == 0 else 1 - x
                ay = y if role == 0 else 1 - y
                for half, index in ((0, (0, every, z, every, ax)), (1, (1, every, z, ay))):
                    table.append((0, index, 1, index, 2 * half + (1 - role), (every, z)))
        return table

    return (keep, got), [(blocks, 4, 2, rows, lanes)] * 4, pieces, (blocks, 2, rows, lanes)


def fold_second(parts, got):
    blocks, _, _, rows, lanes = parts[1].shape
    every = slice(None)

    def pieces(at):
        _, y, x = at
        table = []
        for role in (1, 0):
            for z in range(4):
                for half, own in ((0, y), (1, x)):
                    index = (every, z, own if role == 0 else 1 - own)
                    table.append((2 * half, index, 2 * half + 1, index, 2 * half + (1 - role), (every, z)))
        return table

    return (parts[1], got[0], parts[3], got[1]), [(blocks, 4, rows, lanes)] * 4, pieces, (blocks, rows, lanes)


def fold_third(parts, got, joined=True):
    blocks, _, rows, lanes = parts[1].shape
    every = slice(None)

    def pieces(at):
        table = []
        for n in (0, 1, 2, 3) if joined else (1, 2, 3, 0):
            for half in range(2):
                index = (every, n if joined else at[0] ^ n)
                table.append((2 * half, index, 2 * half + 1, index, 0 if joined else n, (n, half) if joined else (half,)))
        return table

    shape = (2, blocks, rows, lanes)
    return (parts[1], got[0], parts[3], got[1]), [(4,) + shape] if joined else [shape] * 4, pieces, (blocks, rows, lanes)


def fold_third_pair(first, second):
    def moved(group, lower, shapes):
        inputs, _, pieces, shape = group

        def at(where):
            return [(a, a_at, b, b_at, 0, o_at + (slice(lower, lower + shape[0]),)) for a, a_at, b, b_at, _, o_at in pieces(where)]

        return inputs, shapes, at, shape

    split = first[3][0]
    joined = (4, 2, split + second[3][0]) + first[3][1:]
    return [moved(first, 0, [joined]), moved(second, split, [])]


def fold_last(parts, widths, name, stack=1, extra=0, lower=0, upper=None):
    parts = parts if isinstance(parts, list) else [parts]
    blocks, deep, lanes = parts[0].shape[-3:]
    blocks = (blocks if upper is None else upper) - lower
    chunks = sum(widths) // (2 * lanes)
    rows = (blocks * deep - extra) // (chunks * stack)

    def body(*refs):
        ins, outs = refs[: len(parts)], refs[len(parts) :]
        if len(ins) == 1:
            ins = [ins[0].at[z] for z in range(4)]

        def take(half, line, count, at, size):
            step = min(deep, count)
            pieces = []
            for start in range(line, line + count, step):
                total = None
                for ref in ins:
                    value = ref[half, lower + start // deep, start % deep : start % deep + step, at : at + size].astype(F32)
                    total = value if total is None else total + value
                pieces.append(total)
            return pieces[0] if len(pieces) == 1 else jnp.concatenate(pieces, axis=0)

        base = 0
        for out, width in zip(outs, widths):
            tiles = width // 128
            for r in range(stack):
                for t in range(tiles):
                    chunk, at = (base + t * 128) // lanes, (base + t * 128) % lanes
                    line = (chunk % chunks * stack + r) * rows
                    out[pl.ds(r * rows * tiles + t, rows, stride=tiles), :] = take(chunk // chunks, line, rows, at, 128)
            base += width
        if extra:
            outs[-1][...] = take(0, blocks * deep - extra, extra, 0, lanes)[0]

    shapes = [jax.ShapeDtypeStruct((stack * rows * w // 128, 128), F32) for w in widths]
    if extra:
        shapes.append(jax.ShapeDtypeStruct((lanes,), F32))
    return pl.pallas_call(body, name=name, out_shape=shapes, compiler_params=params(63))(*parts)


def sync(*values):
    return lax.optimization_barrier(values)


def flip(value, bits):
    return lax.ppermute(value, "dp", [(i, i ^ bits) for i in range(16)])


def on_device(tokens, lengths, w_qkv, w_out, w_in, w_back, bias_q, value_bias, bias_out, gain1, shift1, bias_in, bias_back, gain2, shift2, cotangent):
    rows_local, half, width = tokens.shape
    dp = lax.axis_size("dp")
    dp_bits = dp.bit_length() - 1
    core = lax.axis_index("seq")
    rows = rows_local // 2
    length = 2 * half
    total = rows * length
    order_a = (0, 1) + tuple(range(2, dp_bits))
    order_b = (1, 0) + tuple(range(2, dp_bits))

    def send_rows(value):
        return swap(lax.dynamic_slice_in_dim(value, (1 - core) * rows, rows, 0))

    other = send_rows(tokens)
    cot_other = send_rows(cotangent)
    bq, bv, bo, g1, s1, bi, bb, g2, s2 = (bias_q, value_bias, bias_out, gain1, shift1, bias_in, bias_back, gain2, shift2)
    core_one = core.reshape(1).astype(jnp.int32)
    me = lax.axis_index("dp")
    fast = dp == 16 and width == 2 * LANES
    qkv, probs, full_tokens, mixed, low, hat1, inv1, inverse = attention_call(core_one, lengths, tokens, other, w_qkv, w_out, (bq, bv, bo, g1, s1))

    def flat(value):
        return value.reshape(total, value.shape[-1])

    full_tokens = flat(full_tokens)
    output, output_other, cls_own, dpre1, dmixed, g_bias_in, g_gain2, g_shift2, g_bias_back, g_gain1, g_shift1, g_bias_out, *grads = feed_call(
        core_one, lengths, flat(low), w_in, w_back, w_out, flat(mixed), flat(hat1), flat(inv1), flat(inverse), cotangent, cot_other,
        (bi.reshape(1, -1), bb, g1, g2, s2), dp, fast,
    )
    dmixed = dmixed.reshape(rows, length, width)
    cls_own = cls_own[:, : lengths.shape[1]]
    if fast:
        where = jnp.stack([me >> 2, (me >> 1) & 1, me & 1]).astype(jnp.int32)

        def view(value):
            return value.reshape((2, value.shape[0] // 2, 4, 2, 2) + value.shape[2:])

        def cross(parts, bit_a, bit_b):
            return flip(parts[0], bit_a), flip(parts[2], bit_b)

        def along_z(parts):
            return lax.all_to_all(parts, "dp", 0, 0, axis_index_groups=[[i, i + 4, i + 8, i + 12] for i in range(4)], tiled=True)

        keep_b, send_b, keep_i, send_i = grads
        got_b = swap(send_b)
        (back,) = add_pieces(where, [fold_first(view(keep_b), view(got_b))], "fold_a")
        dmixed, back, send_i, output_other = sync(dmixed, back, send_i, output_other)
        got_b = cross(back, 1, 2)
        got_i = swap(send_i)
        output_got = swap(output_other)
        dproj, *bias_a = attention_grad(qkv, probs, mixed, dmixed, 0, 1)
        dproj, got_b, got_i, keep_i, output_got = sync(dproj, got_b, got_i, keep_i, output_got)
        inner, back = add_pieces(where, [fold_first(view(keep_i), view(got_i)), fold_second(back, got_b)], "fold_b")
        dmixed, inner, back = sync(dmixed, inner, back)
        got_i = cross(inner, 1, 2)
        got_b = cross(back, 2, 1)
        dproj, *bias_b = attention_grad(qkv, probs, mixed, dmixed, 1, 1, dproj)
        keep_q, send_q = grad_proj(
            core_one, full_tokens, dproj.reshape(3, total, width),
            (bias_a[0], bias_a[1], g_bias_out, g_gain1, g_shift1, g_bias_in, g_bias_back, g_gain2, g_shift2), bias_b, dp,
        )
        send_q, keep_q, got_b, got_i = sync(send_q, keep_q, got_b, got_i)
        got_q = swap(send_q)
        (inner,) = add_pieces(where, [fold_second(inner, got_i)], "fold_c")
        inner, got_q, keep_q, cls_own = sync(inner, got_q, keep_q, cls_own)
        got_i = cross(inner, 2, 1)
        cls_got = swap(cls_own)
        (proj,) = add_pieces(where, [fold_first(view(keep_q), view(got_q))], "fold_d")
        proj, got_i, cls_got = sync(proj, got_i, cls_got)
        got_q = cross(proj, 1, 2)
        split = back[1].shape[0]
        joint = add_pieces(where, fold_third_pair(fold_third(back, got_b), fold_third(inner, got_i)), "fold_e")[0][0]
        dproj, joint = sync(dproj, joint)
        got_i = along_z(joint)
        dinput, dinput_other = input_grad_call(core_one, dproj.reshape(3, total, width), dpre1, w_qkv, half)
        dinput, dinput_other, got_q, output = sync(dinput, dinput_other, got_q, output)
        (proj,) = add_pieces(where, [fold_second(proj, got_q)], "fold_f")
        proj, dinput_other, output = sync(proj, dinput_other, output)
        got_q = cross(proj, 2, 1)
        dinput_got = swap(dinput_other)
        output = lax.dynamic_update_slice_in_dim(output, output_got, (1 - core) * rows, 0)
        output, got_q, dinput_got = sync(output, got_q, dinput_got)
        (proj,) = add_pieces(where, [fold_third(proj, got_q, False)], "fold_g")
        got_q = [proj[0]] + [flip(proj[n], 4 * n) for n in (1, 2, 3)]
        dinput, proj = sync(dinput, proj)
        dinput = lax.dynamic_update_slice_in_dim(dinput, dinput_got, (1 - core) * rows, 0)
        (r_back,) = fold_last(got_i, (width,), "back_sum", w_back.shape[0] // width, 0, 0, split)
        r_in, r_out = fold_last(got_i, (w_in.shape[1], width), "inner_sum", 1, 0, split)
        r_in, r_back, got_q, dinput = sync(r_in, r_back, got_q, dinput)
        r_qkv, r_vec = fold_last(got_q, (3 * width,), "proj_sum", 1, 8)
        r_vec = r_vec[: (8 * width + w_in.shape[1]) // (2 * dp)]
    else:
        g_back, g_inner = grads
        r_back = reduce_scatter(g_back, order_a, dp, dp_bits)
        r_inner = reduce_scatter(g_inner, order_b, dp, dp_bits)
        r_in, r_out = r_inner[:, :-width], r_inner[:, -width:]
        output_got, cls_got = swap(output_other), swap(cls_own)
        dproj, g_bias_q, g_bias_v = attention_grad(qkv, probs, mixed, dmixed, 0, rows)
        dproj = dproj.reshape(3, total, width)
        g_qkv = jnp.concatenate([weight_grad(full_tokens, dproj[n], width, width, "grad_qkv") for n in range(3)], axis=1)
        r_qkv = reduce_scatter(g_qkv, order_b, dp, dp_bits)
        dinput, dinput_other = input_grad_call(core_one, dproj, dpre1, w_qkv, half)
        dinput_got = swap(dinput_other)
    if not fast:
        table = vector_table((g_bias_q, g_bias_v, g_bias_out, g_gain1, g_shift1, g_bias_in, g_bias_back, g_gain2, g_shift2), 2 * dp)
        r_vec = jnp.sum(lax.all_to_all(table, ("dp", "seq"), 0, 0, tiled=True), axis=0)[: (8 * width + w_in.shape[1]) // (2 * dp)]
        output = lax.dynamic_update_slice_in_dim(output, output_got, (1 - core) * rows, 0)
        dinput = lax.dynamic_update_slice_in_dim(dinput, dinput_got, (1 - core) * rows, 0)
    cls = jnp.where(core == 0, jnp.concatenate([cls_own, cls_got], axis=0), jnp.concatenate([cls_got, cls_own], axis=0))
    return (
        output,
        cls,
        dinput,
        r_qkv.reshape(-1),
        r_out.reshape(-1),
        r_in.reshape(-1),
        r_back.reshape(-1),
        r_vec,
    )


def solution(mesh):
    row = P("dp", "seq", None)
    both = P(("dp", "seq"))
    return jax.shard_map(
        on_device,
        mesh=mesh,
        in_specs=(row, P("dp", None)) + (P(),) * 13 + (row,),
        out_specs=(row, P("dp", None, None), row, both, both, both, both, both),
        check_vma=False,
    )
```

```python
from functools import partial

import jax
import jax.numpy as jnp
from jax import lax
from jax.experimental import pallas as pl
from jax.experimental.pallas import tpu as pltpu
from jax.sharding import PartitionSpec as P

HEADS = 12
EPS = 1e-12
BF = jnp.bfloat16
F32 = jnp.float32
VMEM_LIMIT = 60 << 20
RSQRT2 = 0.7071067811865476
RSQRT2PI = 0.3989422804014327


def row_dot(left, right):
    return lax.dot_general(left, right, (((1,), (0,)), ((), ())), preferred_element_type=F32)


def row_dot_t(left, right):
    return lax.dot_general(left, right, (((1,), (1,)), ((), ())), preferred_element_type=F32)


def col_dot(left, right):
    return lax.dot_general(left, right, (((0,), (0,)), ((), ())), preferred_element_type=F32)


def gelu_pair(value):
    expo = jnp.exp(value * value * -0.5)
    phi = 0.5 + 0.5 * lax.erf(value * RSQRT2)
    return value * phi, phi + value * expo * RSQRT2PI


def whole(shape):
    return pl.BlockSpec(shape, lambda *_: (0,) * len(shape))


ANY = pl.BlockSpec(memory_space=pl.ANY)
HBM = pl.BlockSpec(memory_space=pltpu.HBM)


def params(mib):
    return pltpu.CompilerParams(vmem_limit_bytes=(mib << 20) + (896 << 10))


def row_starts(len_ref, row):
    starts = [jnp.int32(0)]
    for j in range(len_ref.shape[1] - 1):
        starts.append(starts[-1] + len_ref[row, j])
    return starts


def attention_kernel(
    core_ref, len_ref, own_ref, other_ref, wqkv_hbm, wout_hbm, bq_ref, bv_ref, bo_ref, g1_ref, s1_ref,
    qkv_hbm, probs_hbm, x_ref, mixed_ref, low_ref, hat1_ref, inv1_ref, scale_ref,
    bias_ref, ahead0_ref, ahead1_ref, qkv_ref, wqkv_ref, wout_ref, p_ref, w_sem, p_sem, q_sem,
):
    step = pl.program_id(0)
    core = core_ref[0]
    rows = pl.num_programs(0)
    half, width = own_ref.shape[1:]
    length = 2 * half
    pairs = width // 128
    parts = [slice(n * width, (n + 1) * width) for n in range(3)]
    copies = [pltpu.make_async_copy(wqkv_hbm.at[:, part], wqkv_ref.at[:, part], w_sem.at[n]) for n, part in enumerate(parts)]
    copies.append(pltpu.make_async_copy(wout_hbm, wout_ref, w_sem.at[3]))

    @pl.when(step == 0)
    def _():
        for copy in copies:
            copy.start()

    x_ref[0, pl.ds(pl.multiple_of(core * half, half), half), :] = own_ref[0]
    x_ref[0, pl.ds(pl.multiple_of((1 - core) * half, half), half), :] = other_ref[0]
    starts = row_starts(len_ref, core * rows + step)
    down = lax.broadcasted_iota(jnp.int32, (length, 1), 0)
    across = lax.broadcasted_iota(jnp.int32, (1, length), 1)
    seg_down = jnp.zeros((length, 1), jnp.int32)
    seg_across = jnp.zeros((1, length), jnp.int32)
    for start in starts[1:]:
        seg_down += (down >= start).astype(jnp.int32)
        seg_across += (across >= start).astype(jnp.int32)
    bias_ref[...] = jnp.where(seg_down == seg_across, 0.0, -1e30)

    for n, part in enumerate(parts):
        @pl.when(step == 0)
        def _():
            copies[n].wait()

        value = row_dot(x_ref[0], wqkv_ref[:, part])
        if n == 0:
            value = (value + bq_ref[...]) * (width // HEADS) ** -0.5
        if n == 2:
            value = value + bv_ref[...]
        qkv_ref[:, part] = value.astype(BF)
    save = pltpu.make_async_copy(qkv_ref, qkv_hbm.at[step], q_sem)
    save.start()

    first = lax.broadcasted_iota(jnp.int32, (1, 128), 1) < 64

    def columns(part, pair):
        return pl.ds(pl.multiple_of(part * width + pair * 128, 128), 128)

    def scores(pair, into):
        q_pair = qkv_ref[:, columns(0, pair)]
        k_pair = qkv_ref[:, columns(1, pair)]
        for h in range(2):
            on = first if h == 0 else jnp.logical_not(first)
            into[h] = row_dot_t(jnp.where(on, q_pair, jnp.zeros_like(q_pair)), k_pair)

    def finish(pair, held, slot):
        out_copy = pltpu.make_async_copy(p_ref.at[slot], probs_hbm.at[step, pair], p_sem.at[slot])

        @pl.when(pair >= 2)
        def _():
            out_copy.wait()

        v_pair = qkv_ref[:, columns(2, pair)]
        outs = []
        for h in range(2):
            on = first if h == 0 else jnp.logical_not(first)
            s = held[h] + bias_ref[...]
            e = jnp.exp(s - jnp.max(s, axis=-1, keepdims=True)).astype(BF)
            p_ref[slot, h] = e
            outs.append(row_dot(e, jnp.where(on, v_pair, jnp.ones_like(v_pair))))
        sums = pltpu.roll(jnp.where(first, outs[1], outs[0]), 64, 1)
        inverse = 1.0 / sums
        scale_ref[0, :, columns(0, pair)] = inverse
        mixed_ref[0, :, columns(0, pair)] = (jnp.where(first, outs[0], outs[1]) * inverse).astype(BF)
        out_copy.start()

    scores(0, ahead0_ref)

    def two_pairs(i, carry):
        scores(2 * i + 1, ahead1_ref)
        finish(2 * i, ahead0_ref, 0)
        scores(jnp.minimum(2 * i + 2, pairs - 1), ahead0_ref)
        finish(2 * i + 1, ahead1_ref, 1)
        return carry

    lax.fori_loop(0, pairs // 2, two_pairs, 0, unroll=True)
    for tail in (pairs - 2, pairs - 1):
        pltpu.make_async_copy(p_ref.at[tail % 2], probs_hbm.at[step, tail], p_sem.at[tail % 2]).wait()

    @pl.when(step == 0)
    def _():
        copies[3].wait()

    pre = x_ref[0].astype(F32) + row_dot(mixed_ref[0], wout_ref[...]) + bo_ref[...]
    center = pre - jnp.mean(pre, axis=-1, keepdims=True)
    inv = lax.rsqrt(jnp.mean(center * center, axis=-1, keepdims=True) + EPS)
    hat = center * inv
    hat1_ref[0] = hat.astype(BF)
    inv1_ref[0] = inv
    low_ref[0] = (hat * g1_ref[...] + s1_ref[...]).astype(BF)
    save.wait()


def attention_call(core, lengths, tokens, other, w_qkv, w_out, vectors):
    rows_local, half, width = tokens.shape
    rows = rows_local // 2
    length = 2 * half
    pairs = width // 128

    def full(n):
        return pl.BlockSpec((1, length, n), lambda r, *_: (r, 0, 0))

    def row(n, kind=BF):
        return jax.ShapeDtypeStruct((rows, length, n), kind)

    return pl.pallas_call(
        attention_kernel,
        name="attention_rows",
        out_shape=[
            row(3 * width), jax.ShapeDtypeStruct((rows, pairs, 2, length, length), BF), row(width), row(width), row(width), row(width),
            row(1, F32), row(width, F32),
        ],
        grid_spec=pltpu.PrefetchScalarGridSpec(
            num_scalar_prefetch=2,
            grid=(rows,),
            in_specs=[
                pl.BlockSpec((1, half, width), lambda r, core, lens: (core[0] * rows + r, 0, 0)),
                pl.BlockSpec((1, half, width), lambda r, *_: (r, 0, 0)),
                ANY,
                ANY,
            ]
            + [whole(v.shape) for v in vectors],
            out_specs=[HBM, HBM] + [full(width)] * 4 + [full(1), full(width)],
            scratch_shapes=[
                pltpu.VMEM((length, length), F32),
                pltpu.VMEM((2, length, length), F32),
                pltpu.VMEM((2, length, length), F32),
                pltpu.VMEM((length, 3 * width), BF),
                pltpu.VMEM(w_qkv.shape, BF),
                pltpu.VMEM(w_out.shape, BF),
                pltpu.VMEM((2, 2, length, length), BF),
                pltpu.SemaphoreType.DMA((4,)),
                pltpu.SemaphoreType.DMA((2,)),
                pltpu.SemaphoreType.DMA,
            ],
        ),
        compiler_params=params(60),
        cost_estimate=pl.CostEstimate(
            flops=8 * rows * length * width * width + 4 * rows * length * length * width,
            bytes_accessed=35 << 20,
            transcendentals=rows * HEADS * length * length,
        ),
    )(core, lengths, tokens, other, w_qkv, w_out, *vectors)


def feed_kernel(
    split, core_ref, len_ref, low_ref, win_hbm, wback_hbm, wout_hbm, mixed_hbm, hat1_hbm, inv1_hbm, scale_hbm, cot_hbm, cot_other_hbm,
    bi_ref, bb_ref, g1_ref, g2_ref, s2_ref,
    out_hbm, other_hbm, cls_ref, dpre_hbm, dmixed_hbm, gi_ref, gg2_ref, gs2_ref, gb2_ref, gg1_ref, gs1_ref, gb1_ref, *rest
):
    n_grads = 4 if split else 2
    grads = rest[:n_grads]
    (win_ref, wback_ref, wout_ref, mixed_ref, hat1_ref, inv1_ref, scale_ref, cot_ref, out_ref, act_ref, slope_ref, acc_ref, dfeed_ref,
     grad_ref, w_sem, v_sem, c_sem, o_sem, d_sem) = rest[n_grads:]
    step = pl.program_id(0)
    core = core_ref[0]
    total, width = low_ref.shape
    length = 2 * cot_other_hbm.shape[1]
    half = length // 2
    group = total // length
    hidden = act_ref.shape[1]
    chunk = width
    chunks = hidden // chunk
    piece = 768
    pieces = [slice(n * piece, (n + 1) * piece) for n in range(chunk // piece)]
    weights = []
    for c in range(chunks):
        part = slice(c * chunk, (c + 1) * chunk)
        weights.append(pltpu.make_async_copy(win_hbm.at[:, part], win_ref.at[:, part], w_sem.at[2 * c]))
        weights.append(pltpu.make_async_copy(wback_hbm.at[part], wback_ref.at[part], w_sem.at[2 * c + 1]))
    values = [
        pltpu.make_async_copy(src, dst, v_sem.at[i])
        for i, (src, dst) in enumerate(
            ((hat1_hbm, hat1_ref), (inv1_hbm, inv1_ref), (wout_hbm, wout_ref), (scale_hbm, scale_ref), (mixed_hbm, mixed_ref))
        )
    ]
    loads, stores = [], []
    for r in range(group):
        own = pl.ds(pl.multiple_of(r * length + core * half, half), half)
        other = pl.ds(pl.multiple_of(r * length + (1 - core) * half, half), half)
        loads.append(pltpu.make_async_copy(cot_hbm.at[core * group + r], cot_ref.at[own], c_sem.at[r]))
        loads.append(pltpu.make_async_copy(cot_other_hbm.at[r], cot_ref.at[other], c_sem.at[group + r]))
        stores.append(pltpu.make_async_copy(out_ref.at[other], other_hbm.at[r], o_sem.at[group + r]))
        stores.append(pltpu.make_async_copy(out_ref.at[own], out_hbm.at[core * group + r], o_sem.at[r]))
    dpre_store = pltpu.make_async_copy(out_ref, dpre_hbm, d_sem.at[0])
    dmixed_store = pltpu.make_async_copy(cot_ref, dmixed_hbm, d_sem.at[1])

    @pl.when(step == 0)
    def _():
        for copy in weights + loads + values:
            copy.start()

    for c in range(chunks):
        @pl.when(step == c)
        def _():
            weights[2 * c].wait()
            weights[2 * c + 1].wait()

    @pl.when(step < chunks)
    def _():
        base = pl.multiple_of(step * chunk, chunk)
        for n in range(len(pieces)):
            cols = pl.ds(base + n * piece, piece)
            act, slope = gelu_pair(row_dot(low_ref[...], win_ref[:, cols]) + bi_ref[:, cols])
            act_ref[:, cols] = act.astype(BF)
            slope_ref[:, cols] = slope.astype(BF)
        rows = pl.ds(base, chunk)

        @pl.when(step == 0)
        def _():
            for cols in pieces:
                acc_ref[:, cols] = row_dot(act_ref[:, rows], wback_ref[rows, cols])

        @pl.when(step > 0)
        def _():
            for cols in pieces:
                acc_ref[:, cols] += row_dot(act_ref[:, rows], wback_ref[rows, cols])

    block = 256

    @pl.when(step == chunks - 1)
    def _():
        for load in loads:
            load.wait()
        gg2_ref[...] = jnp.zeros_like(gg2_ref)
        gs2_ref[...] = jnp.zeros_like(gs2_ref)
        gb2_ref[...] = jnp.zeros_like(gb2_ref)

        def token_body(i, carry):
            at = pl.ds(pl.multiple_of(i * block, block), block)
            pre = low_ref[at, :].astype(F32) + acc_ref[at, :] + bb_ref[...]
            center = pre - jnp.mean(pre, axis=-1, keepdims=True)
            inv = lax.rsqrt(jnp.mean(center * center, axis=-1, keepdims=True) + EPS)
            hat = center * inv
            out_ref[at, :] = (hat * g2_ref[...] + s2_ref[...]).astype(BF)
            dy = cot_ref[at, :].astype(F32)
            gg2_ref[...] += jnp.sum(dy * hat, axis=0, keepdims=True)
            gs2_ref[...] += jnp.sum(dy, axis=0, keepdims=True)
            g = dy * g2_ref[...]
            dpre = inv * (g - jnp.mean(g, axis=-1, keepdims=True) - hat * jnp.mean(g * hat, axis=-1, keepdims=True))
            dfeed = dpre.astype(BF)
            dfeed_ref[at, :] = dfeed
            gb2_ref[...] += jnp.sum(dfeed.astype(F32), axis=0, keepdims=True)
            return carry

        lax.fori_loop(0, total // block, token_body, 0)
        for store in stores:
            store.start()
        which = lax.broadcasted_iota(jnp.int32, (8, 1), 0)
        across = lax.broadcasted_iota(jnp.int32, (1, length), 1)
        for r in range(group):
            down = jnp.full((8, 1), -1, jnp.int32)
            for j, start in enumerate(row_starts(len_ref, core * group + r)):
                down = jnp.where(which == j, start, down)
            choose = (down == across).astype(F32).astype(BF)
            cls_ref[r] = row_dot(choose, out_ref[r * length : (r + 1) * length]).astype(BF)

    def put_grad(value, kept, sent, stack):
        if split:
            grad_ref[...] = value
            split_store(grad_ref, kept, sent, core, 2, stack)
        else:
            kept[...] = value.astype(BF)

    keep_b, keep_i = grads[0], grads[n_grads // 2]
    send_b, send_i = (grads[1], grads[3]) if split else (None, None)

    @pl.when(jnp.logical_and(step >= chunks, step < 2 * chunks))
    def _():
        base = pl.multiple_of((step - chunks) * chunk, chunk)
        rows = pl.ds(base, chunk)
        put_grad(col_dot(act_ref[:, rows], dfeed_ref[...]), keep_b, send_b, chunks)
        for n in range(len(pieces)):
            cols = pl.ds(base + n * piece, piece)
            inner = (row_dot_t(dfeed_ref[...], wback_ref[cols, :]) * slope_ref[:, cols].astype(F32)).astype(BF)
            slope_ref[:, cols] = inner
            gi_ref[:, cols] = jnp.sum(inner.astype(F32), axis=0, keepdims=True)

        @pl.when(step == chunks)
        def _():
            for cols in pieces:
                acc_ref[:, cols] = row_dot_t(slope_ref[:, rows], win_ref[cols, rows])

        @pl.when(step > chunks)
        def _():
            for cols in pieces:
                acc_ref[:, cols] += row_dot_t(slope_ref[:, rows], win_ref[cols, rows])

        put_grad(col_dot(low_ref[...], slope_ref[:, rows]), keep_i, send_i, 1)

    @pl.when(step == 2 * chunks)
    def _():
        for store in stores:
            store.wait()
        for value in values:
            value.wait()
        gg1_ref[...] = jnp.zeros_like(gg1_ref)
        gs1_ref[...] = jnp.zeros_like(gs1_ref)
        gb1_ref[...] = jnp.zeros_like(gb1_ref)

        def token_body(i, carry):
            at = pl.ds(pl.multiple_of(i * block, block), block)
            dn = dfeed_ref[at, :].astype(F32) + acc_ref[at, :]
            hat = hat1_ref[at, :].astype(F32)
            gg1_ref[...] += jnp.sum(dn * hat, axis=0, keepdims=True)
            gs1_ref[...] += jnp.sum(dn, axis=0, keepdims=True)
            g = dn * g1_ref[...]
            dpre = inv1_ref[at, :] * (g - jnp.mean(g, axis=-1, keepdims=True) - hat * jnp.mean(g * hat, axis=-1, keepdims=True))
            branch = dpre.astype(BF)
            out_ref[at, :] = branch
            gb1_ref[...] += jnp.sum(branch.astype(F32), axis=0, keepdims=True)
            return carry

        lax.fori_loop(0, total // block, token_body, 0)
        dpre_store.start()
        for cols in pieces:
            cot_ref[:, cols] = (row_dot_t(out_ref[...], wout_ref[cols, :]) * scale_ref[:, cols]).astype(BF)
        dmixed_store.start()
        put_grad(col_dot(mixed_ref[...], out_ref[...]), keep_i, send_i, 1)
        dpre_store.wait()
        dmixed_store.wait()


def feed_call(core, lengths, low, w_in, w_back, w_out, mixed, hat1, inv1, scale, cot, cot_other, vectors, dp, split):
    total, width = low.shape
    half = cot.shape[1]
    group = cot.shape[0] // 2
    hidden = w_in.shape[1]
    chunks = hidden // width

    def in_back(j):
        return jnp.clip(j - chunks, 0, chunks - 1)

    def in_inner(j):
        return jnp.clip(j - chunks, 0, chunks)

    one = jax.ShapeDtypeStruct((1, width), F32)
    row = jax.ShapeDtypeStruct((total, width), BF)
    shapes = [
        jax.ShapeDtypeStruct(cot.shape, BF),
        jax.ShapeDtypeStruct(cot_other.shape, BF),
        jax.ShapeDtypeStruct((group, 8, width), BF),
        row,
        row,
        jax.ShapeDtypeStruct((1, hidden), F32),
    ] + [one] * 6
    specs = [HBM, HBM, whole((group, 8, width)), HBM, HBM, whole((1, hidden))] + [whole((1, width))] * 6
    if split:
        rows_i = width // (2 * dp)
        devices = dp // chunks
        shapes += [jax.ShapeDtypeStruct((2 * chunks, dp, rows_i, LANES), BF)] * 2
        specs += [pl.BlockSpec((2 * chunks, devices, rows_i, LANES), lambda j, *_: (0, in_back(j), 0, 0))] * 2
        shapes += [jax.ShapeDtypeStruct((2 * (chunks + 1), dp, rows_i, LANES), BF)] * 2
        specs += [pl.BlockSpec((2, dp, rows_i, LANES), lambda j, *_: (in_inner(j), 0, 0, 0))] * 2
    else:
        shapes += [jax.ShapeDtypeStruct((hidden, width), BF), jax.ShapeDtypeStruct((width, hidden + width), BF)]
        specs += [pl.BlockSpec((width, width), lambda j, *_: (in_back(j), 0)), pl.BlockSpec((width, width), lambda j, *_: (0, in_inner(j)))]
    return pl.pallas_call(
        partial(feed_kernel, split),
        name="feed_rows",
        out_shape=shapes,
        grid_spec=pltpu.PrefetchScalarGridSpec(
            num_scalar_prefetch=2,
            grid=(2 * chunks + 1,),
            in_specs=[pl.BlockSpec((total, width), lambda *_: (0, 0), pipeline_mode=pl.Buffered(1))]
            + [ANY] * 9
            + [whole((1, hidden))]
            + [whole((width,))] * 4,
            out_specs=specs,
            scratch_shapes=[
                pltpu.VMEM(w_in.shape, BF),
                pltpu.VMEM(w_back.shape, BF),
                pltpu.VMEM(w_out.shape, BF),
                pltpu.VMEM((total, width), BF),
                pltpu.VMEM((total, width), BF),
                pltpu.VMEM((total, 1), F32),
                pltpu.VMEM((total, width), F32),
                pltpu.VMEM((total, width), BF),
                pltpu.VMEM((total, width), BF),
                pltpu.VMEM((total, hidden), BF),
                pltpu.VMEM((total, hidden), BF),
                pltpu.VMEM((total, width), F32),
                pltpu.VMEM((total, width), BF),
                pltpu.VMEM((width, width), F32),
                pltpu.SemaphoreType.DMA((2 * chunks,)),
                pltpu.SemaphoreType.DMA((5,)),
                pltpu.SemaphoreType.DMA((2 * group,)),
                pltpu.SemaphoreType.DMA((2 * group,)),
                pltpu.SemaphoreType.DMA((2,)),
            ],
        ),
        compiler_params=params(60),
        cost_estimate=pl.CostEstimate(flops=2 * total * width * (6 * hidden + 2 * width), bytes_accessed=40 << 20, transcendentals=2 * total * hidden),
    )(core, lengths, low, w_in, w_back, w_out, mixed, hat1, inv1, scale, cot, cot_other, *vectors)


def weight_grad(left, right, block_m, block_n, name):
    total, m = left.shape
    n = right.shape[1]

    def body(l_ref, r_ref, o_ref, t_ref):
        @pl.when(pl.program_id(1) == 0)
        def _():
            t_ref[...] = l_ref[...].T

        o_ref[...] = row_dot(t_ref[...], r_ref[...]).astype(BF)

    return pl.pallas_call(
        body,
        name=name,
        out_shape=jax.ShapeDtypeStruct((m, n), BF),
        grid=(m // block_m, n // block_n),
        in_specs=[pl.BlockSpec((total, block_m), lambda i, j: (0, i)), pl.BlockSpec((total, block_n), lambda i, j: (0, j))],
        out_specs=pl.BlockSpec((block_m, block_n), lambda i, j: (i, j)),
        scratch_shapes=[pltpu.VMEM((block_m, total), BF)],
        compiler_params=params(63),
        cost_estimate=pl.CostEstimate(flops=2 * total * m * n, bytes_accessed=2 * (total * (m + n) + m * n), transcendentals=0),
    )(left, right)


def attention_grad(qkv, probs, mixed, d, lower, count, partial_out=None):
    rows, length, width = mixed.shape
    pairs = width // 128
    scale = (width // HEADS) ** -0.5
    more = [] if partial_out is None else [partial_out]

    def body(q_ref, k_ref, v_ref, p_ref, m_ref, d_ref, *rest):
        out_ref, bq_ref, bv_ref = rest[-3:]

        @pl.when(pl.program_id(1) == 0)
        def _():
            bq_ref[...] = jnp.zeros_like(bq_ref)
            bv_ref[...] = jnp.zeros_like(bv_ref)

        first = lax.broadcasted_iota(jnp.int32, (1, 128), 1) < 64
        q, k, v, d = q_ref[0], k_ref[0], v_ref[0], d_ref[0]
        product = d.astype(F32) * m_ref[0].astype(F32)
        q_t, d_t, k_t = q.T, d.T, k.T
        dqs, dks, dvs = [], [], []
        for h in range(2):
            on = first if h == 0 else jnp.logical_not(first)
            part = slice(h * 64, (h + 1) * 64)
            delta = jnp.sum(jnp.where(on, product, 0.0), axis=-1, keepdims=True)
            dprobs = row_dot_t(jnp.where(on, d, jnp.zeros_like(d)), v)
            p = p_ref[0, 0, h]
            ds = (p.astype(F32) * (dprobs - delta)).astype(BF)
            dqs.append(row_dot_t(k_t[part], ds))
            dks.append(row_dot(q_t[part], ds))
            dvs.append(row_dot(d_t[part], p))
        dq = (jnp.concatenate(dqs, axis=0) * scale).T.astype(BF)
        dv = jnp.concatenate(dvs, axis=0).T.astype(BF)
        out_ref[0, 0] = dq
        out_ref[1, 0] = jnp.concatenate(dks, axis=0).T.astype(BF)
        out_ref[2, 0] = dv
        bq_ref[...] += jnp.sum(dq.astype(F32), axis=0, keepdims=True)
        bv_ref[...] += jnp.sum(dv.astype(F32), axis=0, keepdims=True)

    def cols(base):
        return pl.BlockSpec((1, length, 128), lambda p, r: (lower + r, 0, base + p))

    vec = pl.BlockSpec((1, 128), lambda p, r: (0, p))
    one = jax.ShapeDtypeStruct((1, width), F32)
    return pl.pallas_call(
        body,
        name="attention_grad",
        out_shape=[jax.ShapeDtypeStruct((3, rows, length, width), BF), one, one],
        grid=(pairs, count),
        input_output_aliases={6: 0} if more else {},
        in_specs=[cols(0), cols(pairs), cols(2 * pairs), pl.BlockSpec((1, 1, 2, length, length), lambda p, r: (lower + r, p, 0, 0, 0)), cols(0), cols(0)]
        + [ANY] * len(more),
        out_specs=[pl.BlockSpec((3, 1, length, 128), lambda p, r: (0, lower + r, 0, p)), vec, vec],
        compiler_params=params(63),
        cost_estimate=pl.CostEstimate(flops=8 * count * length * length * width, bytes_accessed=(15 * count) << 20, transcendentals=0),
    )(qkv, qkv, qkv, probs, mixed, d, *more)


def input_grad_call(core, dproj, dpre, w_qkv, half):
    _, total, width = dproj.shape
    length = 2 * half
    group = total // length

    def body(core_ref, p_ref, d_hbm, w_ref, own_hbm, other_hbm, acc_ref, out_ref, d_ref, sem, d_sem):
        step = pl.program_id(0)
        load = pltpu.make_async_copy(d_hbm, d_ref, d_sem)
        core = core_ref[0]

        @pl.when(step == 0)
        def _():
            load.start()

        value = row_dot_t(p_ref[0], w_ref[...])

        @pl.when(step == 0)
        def _():
            acc_ref[...] = value

        @pl.when(step == 1)
        def _():
            acc_ref[...] += value

        @pl.when(step == 2)
        def _():
            load.wait()
            out_ref[...] = (acc_ref[...] + value + d_ref[...].astype(F32)).astype(BF)
            stores = []
            for r in range(group):
                other = pl.ds(pl.multiple_of(r * length + (1 - core) * half, half), half)
                own = pl.ds(pl.multiple_of(r * length + core * half, half), half)
                stores.append(pltpu.make_async_copy(out_ref.at[other], other_hbm.at[r], sem.at[r]))
                stores.append(pltpu.make_async_copy(out_ref.at[own], own_hbm.at[core * group + r], sem.at[group + r]))
            for store in stores:
                store.start()
            for store in stores:
                store.wait()

    return pl.pallas_call(
        body,
        name="input_grad",
        out_shape=[jax.ShapeDtypeStruct((2 * group, half, width), BF), jax.ShapeDtypeStruct((group, half, width), BF)],
        grid_spec=pltpu.PrefetchScalarGridSpec(
            num_scalar_prefetch=1,
            grid=(3,),
            in_specs=[
                pl.BlockSpec((1, total, width), lambda n, *_: (n, 0, 0)),
                ANY,
                pl.BlockSpec((width, width), lambda n, *_: (0, n)),
            ],
            out_specs=[HBM, HBM],
            scratch_shapes=[pltpu.VMEM((total, width), F32), pltpu.VMEM((total, width), BF), pltpu.VMEM((total, width), BF), pltpu.SemaphoreType.DMA((2 * group,)), pltpu.SemaphoreType.DMA],
        ),
        compiler_params=params(63),
        cost_estimate=pl.CostEstimate(flops=6 * total * width * width, bytes_accessed=10 << 20, transcendentals=0),
    )(core, dproj, dpre, w_qkv)


def vector_table(parts, devices, more=()):
    cut = sum(p.shape[1] for p in parts) // devices

    def body(*refs):
        *ins, out = refs
        values = [ref[...] for ref in ins[: len(parts)]]
        for i, ref in enumerate(ins[len(parts) :]):
            values[i] = values[i] + ref[...]
        joined = jnp.concatenate(values, axis=1)
        out[...] = jnp.zeros_like(out)
        for d in range(devices):
            out[d : d + 1, :cut] = joined[:, d * cut : (d + 1) * cut]

    return pl.pallas_call(
        body,
        name="vector_table",
        out_shape=jax.ShapeDtypeStruct((devices, LANES), F32),
        compiler_params=params(63),
    )(*parts, *more)


def swap(value):
    return lax.ppermute(value, "seq", [(0, 1), (1, 0)])


def pick(value, index, axis):
    return lax.dynamic_index_in_dim(value, index, axis, keepdims=False)


def reduce_stages(part, order, dp_bits, dp):
    me = lax.axis_index("dp")
    n_halving = dp_bits - 2
    shape = part.shape[1:]
    current = part.reshape((2,) * dp_bits + shape)
    left = list(range(dp_bits - 1, -1, -1))
    for bit in order[:n_halving]:
        axis = left.index(bit)
        mine = (me >> bit) & 1
        pairs = [(i, i ^ (1 << bit)) for i in range(dp)]
        send = pick(current, 1 - mine, axis).astype(BF)
        got = lax.ppermute(send, "dp", pairs)
        keep = pick(current, mine, axis)
        current = (keep.astype(F32) + got.astype(F32)).astype(BF)
        left.remove(bit)
    high, low = left
    group = (((me >> high) & 1) << 1) | ((me >> low) & 1)
    current = current.reshape((4,) + shape)
    total = pick(current, group, 0).astype(F32)
    for other in (1, 2, 3):
        flip = ((other >> 1) << high) | ((other & 1) << low)
        pairs = [(i, i ^ flip) for i in range(dp)]
        send = pick(current, group ^ other, 0).astype(BF)
        total = total + lax.ppermute(send, "dp", pairs).astype(F32)
    return total


def reduce_scatter(grad, order, dp, dp_bits):
    core = lax.axis_index("seq")
    rows = grad.shape[0] // (2 * dp)
    blocks = grad.reshape(dp, 2, rows, grad.shape[1])
    send = pick(blocks, 1 - core, 1).astype(BF)
    keep = pick(blocks, core, 1)
    part = (keep.astype(F32) + swap(send).astype(F32)).astype(BF)
    return reduce_stages(part, order, dp_bits, dp)


LANES = 384


def split_store(acc_ref, keep_ref, send_ref, core, parts, stack):
    rows = keep_ref.shape[2]
    for d in range(acc_ref.shape[0] // (2 * stack * rows)):
        for ref, side in ((keep_ref, core), (send_ref, 1 - core)):
            for r in range(stack):
                value = acc_ref[pl.ds(pl.multiple_of(((2 * d + side) * stack + r) * rows, 8), rows), :].astype(BF)
                for c in range(parts):
                    ref[c * stack + r, d] = value[:, c * LANES : (c + 1) * LANES]


def grad_proj(core, left, right, vectors, more, dp):
    total, m = left.shape
    n = 2 * LANES
    rows = m // (2 * dp)
    deep = rows // 8
    blocks = 3 * deep + 1
    cut = sum(v.shape[1] for v in vectors) // (2 * dp)

    def body(core_ref, l_ref, r_ref, *refs):
        ins = refs[: len(vectors) + len(more)]
        keep_hbm, send_hbm, keep_ref, send_ref, acc_ref, table_ref, o_sem = refs[len(ins) :]
        acc_ref[...] = col_dot(l_ref[...], r_ref[0])
        core = core_ref[0]
        step = pl.program_id(0)
        for ref, side in ((keep_ref, core), (send_ref, 1 - core)):
            for d in range(dp):
                value = acc_ref[pl.ds(pl.multiple_of((2 * d + side) * rows, 8), rows), :].astype(BF)
                for c in range(2):
                    chunk = 2 * step + c
                    first = lax.div(chunk, 3) * blocks + lax.rem(chunk, 3) * deep
                    for r in range(deep):
                        ref[first + r, d] = value[8 * r : 8 * r + 8, c * LANES : (c + 1) * LANES]

        @pl.when(step == 0)
        def _():
            values = [ref[...] for ref in ins[: len(vectors)]]
            for i, ref in enumerate(ins[len(vectors) :]):
                values[i] = values[i] + ref[...]
            joined = jnp.concatenate(values, axis=1)
            table_ref[...] = jnp.zeros_like(table_ref)
            for d in range(2 * dp):
                table_ref[d : d + 1, :cut] = joined[:, d * cut : (d + 1) * cut]
            for ref, side in ((keep_ref, core), (send_ref, 1 - core)):
                for d in range(dp):
                    line = table_ref[pl.ds(2 * d + side, 1), :].astype(BF)
                    ref[blocks - 1, d] = jnp.broadcast_to(line, (8, LANES))
                    ref[2 * blocks - 1, d] = jnp.zeros((8, LANES), BF)

        stretches = [
            [(0, 2 * deep), (blocks - 1, blocks), (2 * blocks - 1, 2 * blocks)],
            [(2 * deep, 3 * deep), (blocks, blocks + deep)],
            [(blocks + deep, blocks + 3 * deep)],
        ]
        stores, count = [], 0
        for group in stretches:
            copies = []
            for start, stop in group:
                for src, dst in ((keep_ref, keep_hbm), (send_ref, send_hbm)):
                    copies.append(pltpu.make_async_copy(src.at[start:stop], dst.at[start:stop], o_sem.at[count]))
                    count += 1
            stores.append(copies)
        for n, copies in enumerate(stores):
            @pl.when(step == n)
            def _():
                for copy in copies:
                    copy.start()

        @pl.when(step == 2)
        def _():
            for copies in stores:
                for copy in copies:
                    copy.wait()

    out = jax.ShapeDtypeStruct((2 * blocks, dp, 8, LANES), BF)
    return pl.pallas_call(
        body,
        name="grad_qkv",
        out_shape=[out, out],
        grid_spec=pltpu.PrefetchScalarGridSpec(
            num_scalar_prefetch=1,
            grid=(3,),
            in_specs=[whole((total, m)), pl.BlockSpec((1, total, n), lambda j, *_: (j, 0, 0))] + [whole(v.shape) for v in (*vectors, *more)],
            out_specs=[HBM] * 2,
            scratch_shapes=[pltpu.VMEM(out.shape, BF)] * 2 + [pltpu.VMEM((m, n), F32), pltpu.VMEM((2 * dp, LANES), F32), pltpu.SemaphoreType.DMA((12,))],
        ),
        compiler_params=params(63),
        cost_estimate=pl.CostEstimate(flops=6 * total * m * n, bytes_accessed=6 * n * (total + m), transcendentals=0),
    )(core, left, right, *vectors, *more)


def add_pieces(where, groups, name):
    counts = [len(pieces([jnp.int32(0)] * 3)) for _, _, pieces, _ in groups]
    inputs = [i for g in groups for i in g[0]]
    outputs = [o for g in groups for o in g[1]]

    def body(where_ref, *refs):
        ins = refs[: len(inputs)]
        outs = refs[len(inputs) : len(inputs) + len(outputs)]
        scratch = refs[len(inputs) + len(outputs) :]
        loads, stores, sums = [], [], []
        for n, (group_in, group_out, pieces, _) in enumerate(groups):
            k_ref, g_ref, k_sem, g_sem, o_sem = scratch[5 * n : 5 * n + 5]
            for i, (a, a_at, b, b_at, o, o_at) in enumerate(pieces([where_ref[0], where_ref[1], where_ref[2]])):
                loads.append(pltpu.make_async_copy(ins[a].at[a_at], k_ref.at[i], k_sem.at[i]))
                loads.append(pltpu.make_async_copy(ins[b].at[b_at], g_ref.at[i], g_sem.at[i]))
                stores.append(pltpu.make_async_copy(k_ref.at[i], outs[o].at[o_at], o_sem.at[i]))
                sums.append((k_ref, g_ref, i))
            ins = ins[len(group_in) :]
            if n + 1 < len(groups) and groups[n + 1][1]:
                outs = outs[len(group_out) :]
        for load in loads:
            load.start()
        for i, (k_ref, g_ref, at) in enumerate(sums):
            loads[2 * i].wait()
            loads[2 * i + 1].wait()
            k_ref[at] = k_ref[at] + g_ref[at]
            stores[i].start()
        for store in stores:
            store.wait()

    scratch_shapes = []
    for (_, _, _, shape), count in zip(groups, counts):
        scratch_shapes += [pltpu.VMEM((count,) + shape, BF)] * 2 + [pltpu.SemaphoreType.DMA((count,))] * 3
    result = pl.pallas_call(
        body,
        name=name,
        out_shape=[jax.ShapeDtypeStruct(s, BF) for s in outputs],
        grid_spec=pltpu.PrefetchScalarGridSpec(
            num_scalar_prefetch=1,
            grid=(1,),
            in_specs=[ANY] * len(inputs),
            out_specs=[HBM] * len(outputs),
            scratch_shapes=scratch_shapes,
        ),
        compiler_params=params(63),
    )(where, *inputs)
    split = []
    for _, group_out, _, _ in groups:
        split.append(result[: len(group_out)])
        result = result[len(group_out) :]
    return split


def fold_first(keep, got):
    _, blocks, _, _, _, rows, lanes = keep.shape
    every = slice(None)

    def pieces(at):
        _, y, x = at
        table = []
        for role in (1, 0):
            for z in range(4):
                ax = x if role == 0 else 1 - x
                ay = y if role == 0 else 1 - y
                for half, index in ((0, (0, every, z, every, ax)), (1, (1, every, z, ay))):
                    table.append((0, index, 1, index, 2 * half + (1 - role), (every, z)))
        return table

    return (keep, got), [(blocks, 4, 2, rows, lanes)] * 4, pieces, (blocks, 2, rows, lanes)


def fold_second(parts, got):
    blocks, _, _, rows, lanes = parts[1].shape
    every = slice(None)

    def pieces(at):
        _, y, x = at
        table = []
        for role in (1, 0):
            for z in range(4):
                for half, own in ((0, y), (1, x)):
                    index = (every, z, own if role == 0 else 1 - own)
                    table.append((2 * half, index, 2 * half + 1, index, 2 * half + (1 - role), (every, z)))
        return table

    return (parts[1], got[0], parts[3], got[1]), [(blocks, 4, rows, lanes)] * 4, pieces, (blocks, rows, lanes)


def fold_third(parts, got, joined=True):
    blocks, _, rows, lanes = parts[1].shape
    every = slice(None)

    def pieces(at):
        table = []
        for n in (0, 1, 2, 3) if joined else (1, 2, 3, 0):
            for half in range(2):
                index = (every, n if joined else at[0] ^ n)
                table.append((2 * half, index, 2 * half + 1, index, 0 if joined else n, (n, half) if joined else (half,)))
        return table

    shape = (2, blocks, rows, lanes)
    return (parts[1], got[0], parts[3], got[1]), [(4,) + shape] if joined else [shape] * 4, pieces, (blocks, rows, lanes)


def fold_third_pair(first, second):
    def moved(group, lower, shapes):
        inputs, _, pieces, shape = group

        def at(where):
            return [(a, a_at, b, b_at, 0, o_at + (slice(lower, lower + shape[0]),)) for a, a_at, b, b_at, _, o_at in pieces(where)]

        return inputs, shapes, at, shape

    split = first[3][0]
    joined = (4, 2, split + second[3][0]) + first[3][1:]
    return [moved(first, 0, [joined]), moved(second, split, [])]


def fold_last(parts, widths, name, stack=1, extra=0, lower=0, upper=None):
    parts = parts if isinstance(parts, list) else [parts]
    blocks, deep, lanes = parts[0].shape[-3:]
    blocks = (blocks if upper is None else upper) - lower
    chunks = sum(widths) // (2 * lanes)
    rows = (blocks * deep - extra) // (chunks * stack)

    def body(*refs):
        ins, outs = refs[: len(parts)], refs[len(parts) :]
        if len(ins) == 1:
            ins = [ins[0].at[z] for z in range(4)]

        def take(half, line, count, at, size):
            step = min(deep, count)
            pieces = []
            for start in range(line, line + count, step):
                total = None
                for ref in ins:
                    value = ref[half, lower + start // deep, start % deep : start % deep + step, at : at + size].astype(F32)
                    total = value if total is None else total + value
                pieces.append(total)
            return pieces[0] if len(pieces) == 1 else jnp.concatenate(pieces, axis=0)

        base = 0
        for out, width in zip(outs, widths):
            tiles = width // 128
            for r in range(stack):
                for t in range(tiles):
                    chunk, at = (base + t * 128) // lanes, (base + t * 128) % lanes
                    line = (chunk % chunks * stack + r) * rows
                    out[pl.ds(r * rows * tiles + t, rows, stride=tiles), :] = take(chunk // chunks, line, rows, at, 128)
            base += width
        if extra:
            outs[-1][...] = take(0, blocks * deep - extra, extra, 0, lanes)[0]

    shapes = [jax.ShapeDtypeStruct((stack * rows * w // 128, 128), F32) for w in widths]
    if extra:
        shapes.append(jax.ShapeDtypeStruct((lanes,), F32))
    return pl.pallas_call(body, name=name, out_shape=shapes, compiler_params=params(63))(*parts)


def sync(*values):
    return lax.optimization_barrier(values)


def flip(value, bits):
    return lax.ppermute(value, "dp", [(i, i ^ bits) for i in range(16)])


def on_device(tokens, lengths, w_qkv, w_out, w_in, w_back, bias_q, value_bias, bias_out, gain1, shift1, bias_in, bias_back, gain2, shift2, cotangent):
    rows_local, half, width = tokens.shape
    dp = lax.axis_size("dp")
    dp_bits = dp.bit_length() - 1
    core = lax.axis_index("seq")
    rows = rows_local // 2
    length = 2 * half
    total = rows * length
    order_a = (0, 1) + tuple(range(2, dp_bits))
    order_b = (1, 0) + tuple(range(2, dp_bits))

    def send_rows(value):
        return swap(lax.dynamic_slice_in_dim(value, (1 - core) * rows, rows, 0))

    other = send_rows(tokens)
    cot_other = send_rows(cotangent)
    bq, bv, bo, g1, s1, bi, bb, g2, s2 = (bias_q, value_bias, bias_out, gain1, shift1, bias_in, bias_back, gain2, shift2)
    core_one = core.reshape(1).astype(jnp.int32)
    me = lax.axis_index("dp")
    fast = dp == 16 and width == 2 * LANES
    qkv, probs, full_tokens, mixed, low, hat1, inv1, inverse = attention_call(core_one, lengths, tokens, other, w_qkv, w_out, (bq, bv, bo, g1, s1))

    def flat(value):
        return value.reshape(total, value.shape[-1])

    full_tokens = flat(full_tokens)
    output, output_other, cls_own, dpre1, dmixed, g_bias_in, g_gain2, g_shift2, g_bias_back, g_gain1, g_shift1, g_bias_out, *grads = feed_call(
        core_one, lengths, flat(low), w_in, w_back, w_out, flat(mixed), flat(hat1), flat(inv1), flat(inverse), cotangent, cot_other,
        (bi.reshape(1, -1), bb, g1, g2, s2), dp, fast,
    )
    dmixed = dmixed.reshape(rows, length, width)
    cls_own = cls_own[:, : lengths.shape[1]]
    if fast:
        where = jnp.stack([me >> 2, (me >> 1) & 1, me & 1]).astype(jnp.int32)

        def view(value):
            return value.reshape((2, value.shape[0] // 2, 4, 2, 2) + value.shape[2:])

        def cross(parts, bit_a, bit_b):
            return flip(parts[0], bit_a), flip(parts[2], bit_b)

        def along_z(parts):
            return lax.all_to_all(parts, "dp", 0, 0, axis_index_groups=[[i, i + 4, i + 8, i + 12] for i in range(4)], tiled=True)

        keep_b, send_b, keep_i, send_i = grads
        got_b = swap(send_b)
        (back,) = add_pieces(where, [fold_first(view(keep_b), view(got_b))], "fold_a")
        dmixed, back, send_i, output_other = sync(dmixed, back, send_i, output_other)
        got_b = cross(back, 1, 2)
        got_i = swap(send_i)
        output_got = swap(output_other)
        dproj, *bias_a = attention_grad(qkv, probs, mixed, dmixed, 0, 1)
        dproj, got_i, keep_i, output_got = sync(dproj, got_i, keep_i, output_got)
        (inner,) = add_pieces(where, [fold_first(view(keep_i), view(got_i))], "fold_b")
        inner, got_b = sync(inner, got_b)
        got_i = cross(inner, 1, 2)
        (back,) = add_pieces(where, [fold_second(back, got_b)], "fold_b2")
        dmixed, back = sync(dmixed, back)
        got_b = cross(back, 2, 1)
        dproj, *bias_b = attention_grad(qkv, probs, mixed, dmixed, 1, 1, dproj)
        keep_q, send_q = grad_proj(
            core_one, full_tokens, dproj.reshape(3, total, width),
            (bias_a[0], bias_a[1], g_bias_out, g_gain1, g_shift1, g_bias_in, g_bias_back, g_gain2, g_shift2), bias_b, dp,
        )
        send_q, keep_q, got_b, got_i = sync(send_q, keep_q, got_b, got_i)
        got_q = swap(send_q)
        (inner,) = add_pieces(where, [fold_second(inner, got_i)], "fold_c")
        inner, got_q, keep_q, cls_own = sync(inner, got_q, keep_q, cls_own)
        got_i = cross(inner, 2, 1)
        cls_got = swap(cls_own)
        (proj,) = add_pieces(where, [fold_first(view(keep_q), view(got_q))], "fold_d")
        proj, got_i, cls_got = sync(proj, got_i, cls_got)
        got_q = cross(proj, 1, 2)
        split = back[1].shape[0]
        joint = add_pieces(where, fold_third_pair(fold_third(back, got_b), fold_third(inner, got_i)), "fold_e")[0][0]
        dproj, joint = sync(dproj, joint)
        got_i = along_z(joint)
        dinput, dinput_other = input_grad_call(core_one, dproj.reshape(3, total, width), dpre1, w_qkv, half)
        dinput, dinput_other, got_q, output = sync(dinput, dinput_other, got_q, output)
        (proj,) = add_pieces(where, [fold_second(proj, got_q)], "fold_f")
        proj, dinput_other, output = sync(proj, dinput_other, output)
        got_q = cross(proj, 2, 1)
        dinput_got = swap(dinput_other)
        output = lax.dynamic_update_slice_in_dim(output, output_got, (1 - core) * rows, 0)
        output, got_q, dinput_got = sync(output, got_q, dinput_got)
        (proj,) = add_pieces(where, [fold_third(proj, got_q, False)], "fold_g")
        got_q = [proj[0]] + [flip(proj[n], 4 * n) for n in (1, 2, 3)]
        dinput, proj = sync(dinput, proj)
        dinput = lax.dynamic_update_slice_in_dim(dinput, dinput_got, (1 - core) * rows, 0)
        (r_back,) = fold_last(got_i, (width,), "back_sum", w_back.shape[0] // width, 0, 0, split)
        r_in, r_out = fold_last(got_i, (w_in.shape[1], width), "inner_sum", 1, 0, split)
        r_in, r_back, got_q, dinput = sync(r_in, r_back, got_q, dinput)
        r_qkv, r_vec = fold_last(got_q, (3 * width,), "proj_sum", 1, 8)
        r_vec = r_vec[: (8 * width + w_in.shape[1]) // (2 * dp)]
    else:
        g_back, g_inner = grads
        r_back = reduce_scatter(g_back, order_a, dp, dp_bits)
        r_inner = reduce_scatter(g_inner, order_b, dp, dp_bits)
        r_in, r_out = r_inner[:, :-width], r_inner[:, -width:]
        output_got, cls_got = swap(output_other), swap(cls_own)
        dproj, g_bias_q, g_bias_v = attention_grad(qkv, probs, mixed, dmixed, 0, rows)
        dproj = dproj.reshape(3, total, width)
        g_qkv = jnp.concatenate([weight_grad(full_tokens, dproj[n], width, width, "grad_qkv") for n in range(3)], axis=1)
        r_qkv = reduce_scatter(g_qkv, order_b, dp, dp_bits)
        dinput, dinput_other = input_grad_call(core_one, dproj, dpre1, w_qkv, half)
        dinput_got = swap(dinput_other)
    if not fast:
        table = vector_table((g_bias_q, g_bias_v, g_bias_out, g_gain1, g_shift1, g_bias_in, g_bias_back, g_gain2, g_shift2), 2 * dp)
        r_vec = jnp.sum(lax.all_to_all(table, ("dp", "seq"), 0, 0, tiled=True), axis=0)[: (8 * width + w_in.shape[1]) // (2 * dp)]
        output = lax.dynamic_update_slice_in_dim(output, output_got, (1 - core) * rows, 0)
        dinput = lax.dynamic_update_slice_in_dim(dinput, dinput_got, (1 - core) * rows, 0)
    cls = jnp.where(core == 0, jnp.concatenate([cls_own, cls_got], axis=0), jnp.concatenate([cls_got, cls_own], axis=0))
    return (
        output,
        cls,
        dinput,
        r_qkv.reshape(-1),
        r_out.reshape(-1),
        r_in.reshape(-1),
        r_back.reshape(-1),
        r_vec,
    )


def solution(mesh):
    row = P("dp", "seq", None)
    both = P(("dp", "seq"))
    return jax.shard_map(
        on_device,
        mesh=mesh,
        in_specs=(row, P("dp", None)) + (P(),) * 13 + (row,),
        out_specs=(row, P("dp", None, None), row, both, both, both, both, both),
        check_vma=False,
    )
```

```python
from functools import partial

import jax
import jax.numpy as jnp
from jax import lax
from jax.experimental import pallas as pl
from jax.experimental.pallas import tpu as pltpu
from jax.sharding import PartitionSpec as P

HEADS = 12
EPS = 1e-12
BF = jnp.bfloat16
F32 = jnp.float32
VMEM_LIMIT = 60 << 20
RSQRT2 = 0.7071067811865476
RSQRT2PI = 0.3989422804014327


def row_dot(left, right):
    return lax.dot_general(left, right, (((1,), (0,)), ((), ())), preferred_element_type=F32)


def row_dot_t(left, right):
    return lax.dot_general(left, right, (((1,), (1,)), ((), ())), preferred_element_type=F32)


def col_dot(left, right):
    return lax.dot_general(left, right, (((0,), (0,)), ((), ())), preferred_element_type=F32)


def gelu_pair(value):
    expo = jnp.exp(value * value * -0.5)
    phi = 0.5 + 0.5 * lax.erf(value * RSQRT2)
    return value * phi, phi + value * expo * RSQRT2PI


def whole(shape):
    return pl.BlockSpec(shape, lambda *_: (0,) * len(shape))


ANY = pl.BlockSpec(memory_space=pl.ANY)
HBM = pl.BlockSpec(memory_space=pltpu.HBM)


def params(mib):
    return pltpu.CompilerParams(vmem_limit_bytes=(mib << 20) + (896 << 10))


def row_starts(len_ref, row):
    starts = [jnp.int32(0)]
    for j in range(len_ref.shape[1] - 1):
        starts.append(starts[-1] + len_ref[row, j])
    return starts


def attention_kernel(
    core_ref, len_ref, own_ref, other_ref, wqkv_hbm, wout_hbm, bq_ref, bv_ref, bo_ref, g1_ref, s1_ref,
    qkv_hbm, probs_hbm, x_ref, mixed_ref, low_ref, hat1_ref, inv1_ref, scale_ref,
    bias_ref, ahead0_ref, ahead1_ref, qkv_ref, wqkv_ref, wout_ref, p_ref, w_sem, p_sem, q_sem,
):
    step = pl.program_id(0)
    core = core_ref[0]
    rows = pl.num_programs(0)
    half, width = own_ref.shape[1:]
    length = 2 * half
    pairs = width // 128
    parts = [slice(n * width, (n + 1) * width) for n in range(3)]
    copies = [pltpu.make_async_copy(wqkv_hbm.at[:, part], wqkv_ref.at[:, part], w_sem.at[n]) for n, part in enumerate(parts)]
    copies.append(pltpu.make_async_copy(wout_hbm, wout_ref, w_sem.at[3]))

    @pl.when(step == 0)
    def _():
        for copy in copies:
            copy.start()

    x_ref[0, pl.ds(pl.multiple_of(core * half, half), half), :] = own_ref[0]
    x_ref[0, pl.ds(pl.multiple_of((1 - core) * half, half), half), :] = other_ref[0]
    starts = row_starts(len_ref, core * rows + step)
    down = lax.broadcasted_iota(jnp.int32, (length, 1), 0)
    across = lax.broadcasted_iota(jnp.int32, (1, length), 1)
    seg_down = jnp.zeros((length, 1), jnp.int32)
    seg_across = jnp.zeros((1, length), jnp.int32)
    for start in starts[1:]:
        seg_down += (down >= start).astype(jnp.int32)
        seg_across += (across >= start).astype(jnp.int32)
    bias_ref[...] = jnp.where(seg_down == seg_across, 0.0, -1e30)

    for n, part in enumerate(parts):
        @pl.when(step == 0)
        def _():
            copies[n].wait()

        value = row_dot(x_ref[0], wqkv_ref[:, part])
        if n == 0:
            value = (value + bq_ref[...]) * (width // HEADS) ** -0.5
        if n == 2:
            value = value + bv_ref[...]
        qkv_ref[:, part] = value.astype(BF)
    save = pltpu.make_async_copy(qkv_ref, qkv_hbm.at[step], q_sem)
    save.start()

    first = lax.broadcasted_iota(jnp.int32, (1, 128), 1) < 64

    def columns(part, pair):
        return pl.ds(pl.multiple_of(part * width + pair * 128, 128), 128)

    def scores(pair, into):
        q_pair = qkv_ref[:, columns(0, pair)]
        k_pair = qkv_ref[:, columns(1, pair)]
        for h in range(2):
            on = first if h == 0 else jnp.logical_not(first)
            into[h] = row_dot_t(jnp.where(on, q_pair, jnp.zeros_like(q_pair)), k_pair)

    def finish(pair, held, slot):
        out_copy = pltpu.make_async_copy(p_ref.at[slot], probs_hbm.at[step, pair], p_sem.at[slot])

        @pl.when(pair >= 2)
        def _():
            out_copy.wait()

        v_pair = qkv_ref[:, columns(2, pair)]
        outs = []
        for h in range(2):
            on = first if h == 0 else jnp.logical_not(first)
            s = held[h] + bias_ref[...]
            e = jnp.exp(s - jnp.max(s, axis=-1, keepdims=True)).astype(BF)
            p_ref[slot, h] = e
            outs.append(row_dot(e, jnp.where(on, v_pair, jnp.ones_like(v_pair))))
        sums = pltpu.roll(jnp.where(first, outs[1], outs[0]), 64, 1)
        inverse = 1.0 / sums
        scale_ref[0, :, columns(0, pair)] = inverse
        mixed_ref[0, :, columns(0, pair)] = (jnp.where(first, outs[0], outs[1]) * inverse).astype(BF)
        out_copy.start()

    scores(0, ahead0_ref)

    def two_pairs(i, carry):
        scores(2 * i + 1, ahead1_ref)
        finish(2 * i, ahead0_ref, 0)
        scores(jnp.minimum(2 * i + 2, pairs - 1), ahead0_ref)
        finish(2 * i + 1, ahead1_ref, 1)
        return carry

    lax.fori_loop(0, pairs // 2, two_pairs, 0, unroll=True)
    for tail in (pairs - 2, pairs - 1):
        pltpu.make_async_copy(p_ref.at[tail % 2], probs_hbm.at[step, tail], p_sem.at[tail % 2]).wait()

    @pl.when(step == 0)
    def _():
        copies[3].wait()

    pre = x_ref[0].astype(F32) + row_dot(mixed_ref[0], wout_ref[...]) + bo_ref[...]
    center = pre - jnp.mean(pre, axis=-1, keepdims=True)
    inv = lax.rsqrt(jnp.mean(center * center, axis=-1, keepdims=True) + EPS)
    hat = center * inv
    hat1_ref[0] = hat.astype(BF)
    inv1_ref[0] = inv
    low_ref[0] = (hat * g1_ref[...] + s1_ref[...]).astype(BF)
    save.wait()


def attention_call(core, lengths, tokens, other, w_qkv, w_out, vectors):
    rows_local, half, width = tokens.shape
    rows = rows_local // 2
    length = 2 * half
    pairs = width // 128

    def full(n):
        return pl.BlockSpec((1, length, n), lambda r, *_: (r, 0, 0))

    def row(n, kind=BF):
        return jax.ShapeDtypeStruct((rows, length, n), kind)

    return pl.pallas_call(
        attention_kernel,
        name="attention_rows",
        out_shape=[
            row(3 * width), jax.ShapeDtypeStruct((rows, pairs, 2, length, length), BF), row(width), row(width), row(width), row(width),
            row(1, F32), row(width, F32),
        ],
        grid_spec=pltpu.PrefetchScalarGridSpec(
            num_scalar_prefetch=2,
            grid=(rows,),
            in_specs=[
                pl.BlockSpec((1, half, width), lambda r, core, lens: (core[0] * rows + r, 0, 0)),
                pl.BlockSpec((1, half, width), lambda r, *_: (r, 0, 0)),
                ANY,
                ANY,
            ]
            + [whole(v.shape) for v in vectors],
            out_specs=[HBM, HBM] + [full(width)] * 4 + [full(1), full(width)],
            scratch_shapes=[
                pltpu.VMEM((length, length), F32),
                pltpu.VMEM((2, length, length), F32),
                pltpu.VMEM((2, length, length), F32),
                pltpu.VMEM((length, 3 * width), BF),
                pltpu.VMEM(w_qkv.shape, BF),
                pltpu.VMEM(w_out.shape, BF),
                pltpu.VMEM((2, 2, length, length), BF),
                pltpu.SemaphoreType.DMA((4,)),
                pltpu.SemaphoreType.DMA((2,)),
                pltpu.SemaphoreType.DMA,
            ],
        ),
        compiler_params=params(60),
        cost_estimate=pl.CostEstimate(
            flops=8 * rows * length * width * width + 4 * rows * length * length * width,
            bytes_accessed=35 << 20,
            transcendentals=rows * HEADS * length * length,
        ),
    )(core, lengths, tokens, other, w_qkv, w_out, *vectors)


def feed_kernel(
    split, core_ref, len_ref, low_ref, win_hbm, wback_hbm, wout_hbm, mixed_hbm, hat1_hbm, inv1_hbm, scale_hbm, cot_hbm, cot_other_hbm,
    bi_ref, bb_ref, g1_ref, g2_ref, s2_ref,
    out_hbm, other_hbm, cls_ref, dpre_hbm, dmixed_hbm, gi_ref, gg2_ref, gs2_ref, gb2_ref, gg1_ref, gs1_ref, gb1_ref, *rest
):
    n_grads = 4 if split else 2
    grads = rest[:n_grads]
    (win_ref, wback_ref, wout_ref, mixed_ref, hat1_ref, inv1_ref, scale_ref, cot_ref, out_ref, act_ref, slope_ref, acc_ref, dfeed_ref,
     grad_ref, w_sem, v_sem, c_sem, o_sem, d_sem) = rest[n_grads:]
    step = pl.program_id(0)
    core = core_ref[0]
    total, width = low_ref.shape
    length = 2 * cot_other_hbm.shape[1]
    half = length // 2
    group = total // length
    hidden = act_ref.shape[1]
    chunk = width
    chunks = hidden // chunk
    piece = 768
    pieces = [slice(n * piece, (n + 1) * piece) for n in range(chunk // piece)]
    weights = []
    for c in range(chunks):
        part = slice(c * chunk, (c + 1) * chunk)
        weights.append(pltpu.make_async_copy(win_hbm.at[:, part], win_ref.at[:, part], w_sem.at[2 * c]))
        weights.append(pltpu.make_async_copy(wback_hbm.at[part], wback_ref.at[part], w_sem.at[2 * c + 1]))
    values = [
        pltpu.make_async_copy(src, dst, v_sem.at[i])
        for i, (src, dst) in enumerate(
            ((hat1_hbm, hat1_ref), (inv1_hbm, inv1_ref), (wout_hbm, wout_ref), (scale_hbm, scale_ref), (mixed_hbm, mixed_ref))
        )
    ]
    loads, stores = [], []
    for r in range(group):
        own = pl.ds(pl.multiple_of(r * length + core * half, half), half)
        other = pl.ds(pl.multiple_of(r * length + (1 - core) * half, half), half)
        loads.append(pltpu.make_async_copy(cot_hbm.at[core * group + r], cot_ref.at[own], c_sem.at[r]))
        loads.append(pltpu.make_async_copy(cot_other_hbm.at[r], cot_ref.at[other], c_sem.at[group + r]))
        stores.append(pltpu.make_async_copy(out_ref.at[other], other_hbm.at[r], o_sem.at[group + r]))
        stores.append(pltpu.make_async_copy(out_ref.at[own], out_hbm.at[core * group + r], o_sem.at[r]))
    dpre_store = pltpu.make_async_copy(out_ref, dpre_hbm, d_sem.at[0])
    dmixed_store = pltpu.make_async_copy(cot_ref, dmixed_hbm, d_sem.at[1])

    @pl.when(step == 0)
    def _():
        for copy in weights + loads + values:
            copy.start()

    for c in range(chunks):
        @pl.when(step == c)
        def _():
            weights[2 * c].wait()
            weights[2 * c + 1].wait()

    @pl.when(step < chunks)
    def _():
        base = pl.multiple_of(step * chunk, chunk)
        for n in range(len(pieces)):
            cols = pl.ds(base + n * piece, piece)
            act, slope = gelu_pair(row_dot(low_ref[...], win_ref[:, cols]) + bi_ref[:, cols])
            act_ref[:, cols] = act.astype(BF)
            slope_ref[:, cols] = slope.astype(BF)
        rows = pl.ds(base, chunk)

        @pl.when(step == 0)
        def _():
            for cols in pieces:
                acc_ref[:, cols] = row_dot(act_ref[:, rows], wback_ref[rows, cols])

        @pl.when(step > 0)
        def _():
            for cols in pieces:
                acc_ref[:, cols] += row_dot(act_ref[:, rows], wback_ref[rows, cols])

    block = 256

    @pl.when(step == chunks - 1)
    def _():
        for load in loads:
            load.wait()
        gg2_ref[...] = jnp.zeros_like(gg2_ref)
        gs2_ref[...] = jnp.zeros_like(gs2_ref)
        gb2_ref[...] = jnp.zeros_like(gb2_ref)

        def token_body(i, carry):
            at = pl.ds(pl.multiple_of(i * block, block), block)
            pre = low_ref[at, :].astype(F32) + acc_ref[at, :] + bb_ref[...]
            center = pre - jnp.mean(pre, axis=-1, keepdims=True)
            inv = lax.rsqrt(jnp.mean(center * center, axis=-1, keepdims=True) + EPS)
            hat = center * inv
            out_ref[at, :] = (hat * g2_ref[...] + s2_ref[...]).astype(BF)
            dy = cot_ref[at, :].astype(F32)
            gg2_ref[...] += jnp.sum(dy * hat, axis=0, keepdims=True)
            gs2_ref[...] += jnp.sum(dy, axis=0, keepdims=True)
            g = dy * g2_ref[...]
            dpre = inv * (g - jnp.mean(g, axis=-1, keepdims=True) - hat * jnp.mean(g * hat, axis=-1, keepdims=True))
            dfeed = dpre.astype(BF)
            dfeed_ref[at, :] = dfeed
            gb2_ref[...] += jnp.sum(dfeed.astype(F32), axis=0, keepdims=True)
            return carry

        lax.fori_loop(0, total // block, token_body, 0)
        for store in stores:
            store.start()
        which = lax.broadcasted_iota(jnp.int32, (8, 1), 0)
        across = lax.broadcasted_iota(jnp.int32, (1, length), 1)
        for r in range(group):
            down = jnp.full((8, 1), -1, jnp.int32)
            for j, start in enumerate(row_starts(len_ref, core * group + r)):
                down = jnp.where(which == j, start, down)
            choose = (down == across).astype(F32).astype(BF)
            cls_ref[r] = row_dot(choose, out_ref[r * length : (r + 1) * length]).astype(BF)

    def put_grad(value, kept, sent, stack):
        if split:
            grad_ref[...] = value
            split_store(grad_ref, kept, sent, core, 2, stack)
        else:
            kept[...] = value.astype(BF)

    keep_b, keep_i = grads[0], grads[n_grads // 2]
    send_b, send_i = (grads[1], grads[3]) if split else (None, None)

    @pl.when(jnp.logical_and(step >= chunks, step < 2 * chunks))
    def _():
        base = pl.multiple_of((step - chunks) * chunk, chunk)
        rows = pl.ds(base, chunk)
        put_grad(col_dot(act_ref[:, rows], dfeed_ref[...]), keep_b, send_b, chunks)
        for n in range(len(pieces)):
            cols = pl.ds(base + n * piece, piece)
            inner = (row_dot_t(dfeed_ref[...], wback_ref[cols, :]) * slope_ref[:, cols].astype(F32)).astype(BF)
            slope_ref[:, cols] = inner
            gi_ref[:, cols] = jnp.sum(inner.astype(F32), axis=0, keepdims=True)

        @pl.when(step == chunks)
        def _():
            for cols in pieces:
                acc_ref[:, cols] = row_dot_t(slope_ref[:, rows], win_ref[cols, rows])

        @pl.when(step > chunks)
        def _():
            for cols in pieces:
                acc_ref[:, cols] += row_dot_t(slope_ref[:, rows], win_ref[cols, rows])

        put_grad(col_dot(low_ref[...], slope_ref[:, rows]), keep_i, send_i, 1)

    @pl.when(step == 2 * chunks)
    def _():
        for store in stores:
            store.wait()
        for value in values:
            value.wait()
        gg1_ref[...] = jnp.zeros_like(gg1_ref)
        gs1_ref[...] = jnp.zeros_like(gs1_ref)
        gb1_ref[...] = jnp.zeros_like(gb1_ref)

        def token_body(i, carry):
            at = pl.ds(pl.multiple_of(i * block, block), block)
            dn = dfeed_ref[at, :].astype(F32) + acc_ref[at, :]
            hat = hat1_ref[at, :].astype(F32)
            gg1_ref[...] += jnp.sum(dn * hat, axis=0, keepdims=True)
            gs1_ref[...] += jnp.sum(dn, axis=0, keepdims=True)
            g = dn * g1_ref[...]
            dpre = inv1_ref[at, :] * (g - jnp.mean(g, axis=-1, keepdims=True) - hat * jnp.mean(g * hat, axis=-1, keepdims=True))
            branch = dpre.astype(BF)
            out_ref[at, :] = branch
            gb1_ref[...] += jnp.sum(branch.astype(F32), axis=0, keepdims=True)
            return carry

        lax.fori_loop(0, total // block, token_body, 0)
        dpre_store.start()
        for cols in pieces:
            cot_ref[:, cols] = (row_dot_t(out_ref[...], wout_ref[cols, :]) * scale_ref[:, cols]).astype(BF)
        dmixed_store.start()
        put_grad(col_dot(mixed_ref[...], out_ref[...]), keep_i, send_i, 1)
        dpre_store.wait()
        dmixed_store.wait()


def feed_call(core, lengths, low, w_in, w_back, w_out, mixed, hat1, inv1, scale, cot, cot_other, vectors, dp, split):
    total, width = low.shape
    half = cot.shape[1]
    group = cot.shape[0] // 2
    hidden = w_in.shape[1]
    chunks = hidden // width

    def in_back(j):
        return jnp.clip(j - chunks, 0, chunks - 1)

    def in_inner(j):
        return jnp.clip(j - chunks, 0, chunks)

    one = jax.ShapeDtypeStruct((1, width), F32)
    row = jax.ShapeDtypeStruct((total, width), BF)
    shapes = [
        jax.ShapeDtypeStruct(cot.shape, BF),
        jax.ShapeDtypeStruct(cot_other.shape, BF),
        jax.ShapeDtypeStruct((group, 8, width), BF),
        row,
        row,
        jax.ShapeDtypeStruct((1, hidden), F32),
    ] + [one] * 6
    specs = [HBM, HBM, whole((group, 8, width)), HBM, HBM, whole((1, hidden))] + [whole((1, width))] * 6
    if split:
        rows_i = width // (2 * dp)
        devices = dp // chunks
        shapes += [jax.ShapeDtypeStruct((2 * chunks, dp, rows_i, LANES), BF)] * 2
        specs += [pl.BlockSpec((2 * chunks, devices, rows_i, LANES), lambda j, *_: (0, in_back(j), 0, 0))] * 2
        shapes += [jax.ShapeDtypeStruct((2 * (chunks + 1), dp, rows_i, LANES), BF)] * 2
        specs += [pl.BlockSpec((2, dp, rows_i, LANES), lambda j, *_: (in_inner(j), 0, 0, 0))] * 2
    else:
        shapes += [jax.ShapeDtypeStruct((hidden, width), BF), jax.ShapeDtypeStruct((width, hidden + width), BF)]
        specs += [pl.BlockSpec((width, width), lambda j, *_: (in_back(j), 0)), pl.BlockSpec((width, width), lambda j, *_: (0, in_inner(j)))]
    return pl.pallas_call(
        partial(feed_kernel, split),
        name="feed_rows",
        out_shape=shapes,
        grid_spec=pltpu.PrefetchScalarGridSpec(
            num_scalar_prefetch=2,
            grid=(2 * chunks + 1,),
            in_specs=[pl.BlockSpec((total, width), lambda *_: (0, 0), pipeline_mode=pl.Buffered(1))]
            + [ANY] * 9
            + [whole((1, hidden))]
            + [whole((width,))] * 4,
            out_specs=specs,
            scratch_shapes=[
                pltpu.VMEM(w_in.shape, BF),
                pltpu.VMEM(w_back.shape, BF),
                pltpu.VMEM(w_out.shape, BF),
                pltpu.VMEM((total, width), BF),
                pltpu.VMEM((total, width), BF),
                pltpu.VMEM((total, 1), F32),
                pltpu.VMEM((total, width), F32),
                pltpu.VMEM((total, width), BF),
                pltpu.VMEM((total, width), BF),
                pltpu.VMEM((total, hidden), BF),
                pltpu.VMEM((total, hidden), BF),
                pltpu.VMEM((total, width), F32),
                pltpu.VMEM((total, width), BF),
                pltpu.VMEM((width, width), F32),
                pltpu.SemaphoreType.DMA((2 * chunks,)),
                pltpu.SemaphoreType.DMA((5,)),
                pltpu.SemaphoreType.DMA((2 * group,)),
                pltpu.SemaphoreType.DMA((2 * group,)),
                pltpu.SemaphoreType.DMA((2,)),
            ],
        ),
        compiler_params=params(60),
        cost_estimate=pl.CostEstimate(flops=2 * total * width * (6 * hidden + 2 * width), bytes_accessed=40 << 20, transcendentals=2 * total * hidden),
    )(core, lengths, low, w_in, w_back, w_out, mixed, hat1, inv1, scale, cot, cot_other, *vectors)


def weight_grad(left, right, block_m, block_n, name):
    total, m = left.shape
    n = right.shape[1]

    def body(l_ref, r_ref, o_ref, t_ref):
        @pl.when(pl.program_id(1) == 0)
        def _():
            t_ref[...] = l_ref[...].T

        o_ref[...] = row_dot(t_ref[...], r_ref[...]).astype(BF)

    return pl.pallas_call(
        body,
        name=name,
        out_shape=jax.ShapeDtypeStruct((m, n), BF),
        grid=(m // block_m, n // block_n),
        in_specs=[pl.BlockSpec((total, block_m), lambda i, j: (0, i)), pl.BlockSpec((total, block_n), lambda i, j: (0, j))],
        out_specs=pl.BlockSpec((block_m, block_n), lambda i, j: (i, j)),
        scratch_shapes=[pltpu.VMEM((block_m, total), BF)],
        compiler_params=params(63),
        cost_estimate=pl.CostEstimate(flops=2 * total * m * n, bytes_accessed=2 * (total * (m + n) + m * n), transcendentals=0),
    )(left, right)


def attention_grad(qkv, probs, mixed, d, lower, count, partial_out=None):
    rows, length, width = mixed.shape
    pairs = width // 128
    scale = (width // HEADS) ** -0.5
    more = [] if partial_out is None else [partial_out]

    def body(q_ref, k_ref, v_ref, p_ref, m_ref, d_ref, *rest):
        out_ref, bq_ref, bv_ref = rest[-3:]

        @pl.when(pl.program_id(1) == 0)
        def _():
            bq_ref[...] = jnp.zeros_like(bq_ref)
            bv_ref[...] = jnp.zeros_like(bv_ref)

        first = lax.broadcasted_iota(jnp.int32, (1, 128), 1) < 64
        q, k, v, d = q_ref[0], k_ref[0], v_ref[0], d_ref[0]
        product = d.astype(F32) * m_ref[0].astype(F32)
        q_t, d_t, k_t = q.T, d.T, k.T
        dqs, dks, dvs = [], [], []
        for h in range(2):
            on = first if h == 0 else jnp.logical_not(first)
            part = slice(h * 64, (h + 1) * 64)
            delta = jnp.sum(jnp.where(on, product, 0.0), axis=-1, keepdims=True)
            dprobs = row_dot_t(jnp.where(on, d, jnp.zeros_like(d)), v)
            p = p_ref[0, 0, h]
            ds = (p.astype(F32) * (dprobs - delta)).astype(BF)
            dqs.append(row_dot_t(k_t[part], ds))
            dks.append(row_dot(q_t[part], ds))
            dvs.append(row_dot(d_t[part], p))
        dq = (jnp.concatenate(dqs, axis=0) * scale).T.astype(BF)
        dv = jnp.concatenate(dvs, axis=0).T.astype(BF)
        out_ref[0, 0] = dq
        out_ref[1, 0] = jnp.concatenate(dks, axis=0).T.astype(BF)
        out_ref[2, 0] = dv
        bq_ref[...] += jnp.sum(dq.astype(F32), axis=0, keepdims=True)
        bv_ref[...] += jnp.sum(dv.astype(F32), axis=0, keepdims=True)

    def cols(base):
        return pl.BlockSpec((1, length, 128), lambda p, r: (lower + r, 0, base + p))

    vec = pl.BlockSpec((1, 128), lambda p, r: (0, p))
    one = jax.ShapeDtypeStruct((1, width), F32)
    return pl.pallas_call(
        body,
        name="attention_grad",
        out_shape=[jax.ShapeDtypeStruct((3, rows, length, width), BF), one, one],
        grid=(pairs, count),
        input_output_aliases={6: 0} if more else {},
        in_specs=[cols(0), cols(pairs), cols(2 * pairs), pl.BlockSpec((1, 1, 2, length, length), lambda p, r: (lower + r, p, 0, 0, 0)), cols(0), cols(0)]
        + [ANY] * len(more),
        out_specs=[pl.BlockSpec((3, 1, length, 128), lambda p, r: (0, lower + r, 0, p)), vec, vec],
        compiler_params=params(63),
        cost_estimate=pl.CostEstimate(flops=8 * count * length * length * width, bytes_accessed=(15 * count) << 20, transcendentals=0),
    )(qkv, qkv, qkv, probs, mixed, d, *more)


def input_grad_call(core, dproj, dpre, w_qkv, half):
    _, total, width = dproj.shape
    length = 2 * half
    group = total // length

    def body(core_ref, p_ref, d_hbm, w_ref, own_hbm, other_hbm, acc_ref, out_ref, d_ref, sem, d_sem):
        step = pl.program_id(0)
        load = pltpu.make_async_copy(d_hbm, d_ref, d_sem)
        core = core_ref[0]

        @pl.when(step == 0)
        def _():
            load.start()

        value = row_dot_t(p_ref[0], w_ref[...])

        @pl.when(step == 0)
        def _():
            acc_ref[...] = value

        @pl.when(step == 1)
        def _():
            acc_ref[...] += value

        @pl.when(step == 2)
        def _():
            load.wait()
            out_ref[...] = (acc_ref[...] + value + d_ref[...].astype(F32)).astype(BF)
            stores = []
            for r in range(group):
                other = pl.ds(pl.multiple_of(r * length + (1 - core) * half, half), half)
                own = pl.ds(pl.multiple_of(r * length + core * half, half), half)
                stores.append(pltpu.make_async_copy(out_ref.at[other], other_hbm.at[r], sem.at[r]))
                stores.append(pltpu.make_async_copy(out_ref.at[own], own_hbm.at[core * group + r], sem.at[group + r]))
            for store in stores:
                store.start()
            for store in stores:
                store.wait()

    return pl.pallas_call(
        body,
        name="input_grad",
        out_shape=[jax.ShapeDtypeStruct((2 * group, half, width), BF), jax.ShapeDtypeStruct((group, half, width), BF)],
        grid_spec=pltpu.PrefetchScalarGridSpec(
            num_scalar_prefetch=1,
            grid=(3,),
            in_specs=[
                pl.BlockSpec((1, total, width), lambda n, *_: (n, 0, 0)),
                ANY,
                pl.BlockSpec((width, width), lambda n, *_: (0, n)),
            ],
            out_specs=[HBM, HBM],
            scratch_shapes=[pltpu.VMEM((total, width), F32), pltpu.VMEM((total, width), BF), pltpu.VMEM((total, width), BF), pltpu.SemaphoreType.DMA((2 * group,)), pltpu.SemaphoreType.DMA],
        ),
        compiler_params=params(63),
        cost_estimate=pl.CostEstimate(flops=6 * total * width * width, bytes_accessed=10 << 20, transcendentals=0),
    )(core, dproj, dpre, w_qkv)


def vector_table(parts, devices, more=()):
    cut = sum(p.shape[1] for p in parts) // devices

    def body(*refs):
        *ins, out = refs
        values = [ref[...] for ref in ins[: len(parts)]]
        for i, ref in enumerate(ins[len(parts) :]):
            values[i] = values[i] + ref[...]
        joined = jnp.concatenate(values, axis=1)
        out[...] = jnp.zeros_like(out)
        for d in range(devices):
            out[d : d + 1, :cut] = joined[:, d * cut : (d + 1) * cut]

    return pl.pallas_call(
        body,
        name="vector_table",
        out_shape=jax.ShapeDtypeStruct((devices, LANES), F32),
        compiler_params=params(63),
    )(*parts, *more)


def swap(value):
    return lax.ppermute(value, "seq", [(0, 1), (1, 0)])


def pick(value, index, axis):
    return lax.dynamic_index_in_dim(value, index, axis, keepdims=False)


def reduce_stages(part, order, dp_bits, dp):
    me = lax.axis_index("dp")
    n_halving = dp_bits - 2
    shape = part.shape[1:]
    current = part.reshape((2,) * dp_bits + shape)
    left = list(range(dp_bits - 1, -1, -1))
    for bit in order[:n_halving]:
        axis = left.index(bit)
        mine = (me >> bit) & 1
        pairs = [(i, i ^ (1 << bit)) for i in range(dp)]
        send = pick(current, 1 - mine, axis).astype(BF)
        got = lax.ppermute(send, "dp", pairs)
        keep = pick(current, mine, axis)
        current = (keep.astype(F32) + got.astype(F32)).astype(BF)
        left.remove(bit)
    high, low = left
    group = (((me >> high) & 1) << 1) | ((me >> low) & 1)
    current = current.reshape((4,) + shape)
    total = pick(current, group, 0).astype(F32)
    for other in (1, 2, 3):
        flip = ((other >> 1) << high) | ((other & 1) << low)
        pairs = [(i, i ^ flip) for i in range(dp)]
        send = pick(current, group ^ other, 0).astype(BF)
        total = total + lax.ppermute(send, "dp", pairs).astype(F32)
    return total


def reduce_scatter(grad, order, dp, dp_bits):
    core = lax.axis_index("seq")
    rows = grad.shape[0] // (2 * dp)
    blocks = grad.reshape(dp, 2, rows, grad.shape[1])
    send = pick(blocks, 1 - core, 1).astype(BF)
    keep = pick(blocks, core, 1)
    part = (keep.astype(F32) + swap(send).astype(F32)).astype(BF)
    return reduce_stages(part, order, dp_bits, dp)


LANES = 384


def split_store(acc_ref, keep_ref, send_ref, core, parts, stack):
    rows = keep_ref.shape[2]
    for d in range(acc_ref.shape[0] // (2 * stack * rows)):
        for ref, side in ((keep_ref, core), (send_ref, 1 - core)):
            for r in range(stack):
                value = acc_ref[pl.ds(pl.multiple_of(((2 * d + side) * stack + r) * rows, 8), rows), :].astype(BF)
                for c in range(parts):
                    ref[c * stack + r, d] = value[:, c * LANES : (c + 1) * LANES]


def grad_proj(core, left, right, vectors, more, dp):
    total, m = left.shape
    n = 2 * LANES
    rows = m // (2 * dp)
    deep = rows // 8
    blocks = 3 * deep + 1
    cut = sum(v.shape[1] for v in vectors) // (2 * dp)

    def body(core_ref, l_ref, r_ref, *refs):
        ins = refs[: len(vectors) + len(more)]
        keep_hbm, send_hbm, keep_ref, send_ref, acc_ref, table_ref, o_sem = refs[len(ins) :]
        acc_ref[...] = col_dot(l_ref[...], r_ref[0])
        core = core_ref[0]
        step = pl.program_id(0)
        for ref, side in ((keep_ref, core), (send_ref, 1 - core)):
            for d in range(dp):
                value = acc_ref[pl.ds(pl.multiple_of((2 * d + side) * rows, 8), rows), :].astype(BF)
                for c in range(2):
                    chunk = 2 * step + c
                    first = lax.div(chunk, 3) * blocks + lax.rem(chunk, 3) * deep
                    for r in range(deep):
                        ref[first + r, d] = value[8 * r : 8 * r + 8, c * LANES : (c + 1) * LANES]

        @pl.when(step == 0)
        def _():
            values = [ref[...] for ref in ins[: len(vectors)]]
            for i, ref in enumerate(ins[len(vectors) :]):
                values[i] = values[i] + ref[...]
            joined = jnp.concatenate(values, axis=1)
            table_ref[...] = jnp.zeros_like(table_ref)
            for d in range(2 * dp):
                table_ref[d : d + 1, :cut] = joined[:, d * cut : (d + 1) * cut]
            for ref, side in ((keep_ref, core), (send_ref, 1 - core)):
                for d in range(dp):
                    line = table_ref[pl.ds(2 * d + side, 1), :].astype(BF)
                    ref[blocks - 1, d] = jnp.broadcast_to(line, (8, LANES))
                    ref[2 * blocks - 1, d] = jnp.zeros((8, LANES), BF)

        stretches = [
            [(0, 2 * deep), (blocks - 1, blocks), (2 * blocks - 1, 2 * blocks)],
            [(2 * deep, 3 * deep), (blocks, blocks + deep)],
            [(blocks + deep, blocks + 3 * deep)],
        ]
        stores, count = [], 0
        for group in stretches:
            copies = []
            for start, stop in group:
                for src, dst in ((keep_ref, keep_hbm), (send_ref, send_hbm)):
                    copies.append(pltpu.make_async_copy(src.at[start:stop], dst.at[start:stop], o_sem.at[count]))
                    count += 1
            stores.append(copies)
        for n, copies in enumerate(stores):
            @pl.when(step == n)
            def _():
                for copy in copies:
                    copy.start()

        @pl.when(step == 2)
        def _():
            for copies in stores:
                for copy in copies:
                    copy.wait()

    out = jax.ShapeDtypeStruct((2 * blocks, dp, 8, LANES), BF)
    return pl.pallas_call(
        body,
        name="grad_qkv",
        out_shape=[out, out],
        grid_spec=pltpu.PrefetchScalarGridSpec(
            num_scalar_prefetch=1,
            grid=(3,),
            in_specs=[whole((total, m)), pl.BlockSpec((1, total, n), lambda j, *_: (j, 0, 0))] + [whole(v.shape) for v in (*vectors, *more)],
            out_specs=[HBM] * 2,
            scratch_shapes=[pltpu.VMEM(out.shape, BF)] * 2 + [pltpu.VMEM((m, n), F32), pltpu.VMEM((2 * dp, LANES), F32), pltpu.SemaphoreType.DMA((12,))],
        ),
        compiler_params=params(63),
        cost_estimate=pl.CostEstimate(flops=6 * total * m * n, bytes_accessed=6 * n * (total + m), transcendentals=0),
    )(core, left, right, *vectors, *more)


def add_pieces(where, groups, name):
    counts = [len(pieces([jnp.int32(0)] * 3)) for _, _, pieces, _ in groups]
    inputs = [i for g in groups for i in g[0]]
    outputs = [o for g in groups for o in g[1]]

    def body(where_ref, *refs):
        ins = refs[: len(inputs)]
        outs = refs[len(inputs) : len(inputs) + len(outputs)]
        scratch = refs[len(inputs) + len(outputs) :]
        loads, stores, sums = [], [], []
        for n, (group_in, group_out, pieces, _) in enumerate(groups):
            k_ref, g_ref, h_ref, k_sem, g_sem, h_sem, o_sem = scratch[7 * n : 7 * n + 7]
            for i, (a, a_at, b, b_at, o, o_at, *third) in enumerate(pieces([where_ref[0], where_ref[1], where_ref[2]])):
                loads.append([pltpu.make_async_copy(ins[a].at[a_at], k_ref.at[i], k_sem.at[i])])
                loads[-1].append(pltpu.make_async_copy(ins[b].at[b_at], g_ref.at[i], g_sem.at[i]))
                if third:
                    loads[-1].append(pltpu.make_async_copy(ins[third[0]].at[third[1]], h_ref.at[i], h_sem.at[i]))
                stores.append(pltpu.make_async_copy(k_ref.at[i], outs[o].at[o_at], o_sem.at[i]))
                sums.append((k_ref, g_ref, h_ref if third else None, i))
            ins = ins[len(group_in) :]
            if n + 1 < len(groups) and groups[n + 1][1]:
                outs = outs[len(group_out) :]
        for copies in loads:
            for copy in copies:
                copy.start()
        for i, (k_ref, g_ref, h_ref, at) in enumerate(sums):
            for copy in loads[i]:
                copy.wait()
            value = k_ref[at] + g_ref[at]
            k_ref[at] = value if h_ref is None else value + h_ref[at]
            stores[i].start()
        for store in stores:
            store.wait()

    scratch_shapes = []
    for (_, _, pieces, shape), count in zip(groups, counts):
        third = count if len(pieces([jnp.int32(0)] * 3)[0]) > 6 else 1
        scratch_shapes += [pltpu.VMEM((n,) + shape, BF) for n in (count, count, third)]
        scratch_shapes += [pltpu.SemaphoreType.DMA((n,)) for n in (count, count, third, count)]
    result = pl.pallas_call(
        body,
        name=name,
        out_shape=[jax.ShapeDtypeStruct(s, BF) for s in outputs],
        grid_spec=pltpu.PrefetchScalarGridSpec(
            num_scalar_prefetch=1,
            grid=(1,),
            in_specs=[ANY] * len(inputs),
            out_specs=[HBM] * len(outputs),
            scratch_shapes=scratch_shapes,
        ),
        compiler_params=params(63),
    )(where, *inputs)
    split = []
    for _, group_out, _, _ in groups:
        split.append(result[: len(group_out)])
        result = result[len(group_out) :]
    return split


def fold_first(keep, got):
    _, blocks, _, _, _, rows, lanes = keep.shape
    every = slice(None)

    def pieces(at):
        _, y, x = at
        table = []
        for z in range(4):
            for half, index in ((0, (0, every, z, every, 1 - x)), (1, (1, every, z, 1 - y))):
                table.append((0, index, 1, index, half, (every, z)))
        return table

    return (keep, got), [(blocks, 4, 2, rows, lanes)] * 2, pieces, (blocks, 2, rows, lanes)


def fold_second(keep, got, arrived):
    _, blocks, _, _, _, rows, lanes = keep.shape
    every = slice(None)

    def pieces(at):
        _, y, x = at
        table = []
        for role in (1, 0):
            ax = x if role == 0 else 1 - x
            ay = y if role == 0 else 1 - y
            for z in range(4):
                for half, index, inner in ((0, (0, every, z, ay, x), ay), (1, (1, every, z, y, ax), ax)):
                    table.append((0, index, 1, index, 2 * half + (1 - role), (every, z), 2 + half, (every, z, inner)))
        return table

    return (keep, got, *arrived), [(blocks, 4, rows, lanes)] * 4, pieces, (blocks, rows, lanes)


def fold_third(parts, got, joined=True):
    blocks, _, rows, lanes = parts[1].shape
    every = slice(None)

    def pieces(at):
        table = []
        for n in (0, 1, 2, 3) if joined else (1, 2, 3, 0):
            for half in range(2):
                index = (every, n if joined else at[0] ^ n)
                table.append((2 * half, index, 2 * half + 1, index, 0 if joined else n, (n, half) if joined else (half,)))
        return table

    shape = (2, blocks, rows, lanes)
    return (parts[1], got[0], parts[3], got[1]), [(4,) + shape] if joined else [shape] * 4, pieces, (blocks, rows, lanes)


def fold_third_pair(first, second):
    def moved(group, lower, shapes):
        inputs, _, pieces, shape = group

        def at(where):
            return [(a, a_at, b, b_at, 0, o_at + (slice(lower, lower + shape[0]),)) for a, a_at, b, b_at, _, o_at in pieces(where)]

        return inputs, shapes, at, shape

    split = first[3][0]
    joined = (4, 2, split + second[3][0]) + first[3][1:]
    return [moved(first, 0, [joined]), moved(second, split, [])]


def fold_last(parts, widths, name, stack=1, extra=0, lower=0, upper=None):
    parts = parts if isinstance(parts, list) else [parts]
    blocks, deep, lanes = parts[0].shape[-3:]
    blocks = (blocks if upper is None else upper) - lower
    chunks = sum(widths) // (2 * lanes)
    rows = (blocks * deep - extra) // (chunks * stack)

    def body(*refs):
        ins, outs = refs[: len(parts)], refs[len(parts) :]
        if len(ins) == 1:
            ins = [ins[0].at[z] for z in range(4)]

        def take(half, line, count, at, size):
            step = min(deep, count)
            pieces = []
            for start in range(line, line + count, step):
                total = None
                for ref in ins:
                    value = ref[half, lower + start // deep, start % deep : start % deep + step, at : at + size].astype(F32)
                    total = value if total is None else total + value
                pieces.append(total)
            return pieces[0] if len(pieces) == 1 else jnp.concatenate(pieces, axis=0)

        base = 0
        for out, width in zip(outs, widths):
            tiles = width // 128
            for r in range(stack):
                for t in range(tiles):
                    chunk, at = (base + t * 128) // lanes, (base + t * 128) % lanes
                    line = (chunk % chunks * stack + r) * rows
                    out[pl.ds(r * rows * tiles + t, rows, stride=tiles), :] = take(chunk // chunks, line, rows, at, 128)
            base += width
        if extra:
            outs[-1][...] = take(0, blocks * deep - extra, extra, 0, lanes)[0]

    shapes = [jax.ShapeDtypeStruct((stack * rows * w // 128, 128), F32) for w in widths]
    if extra:
        shapes.append(jax.ShapeDtypeStruct((lanes,), F32))
    return pl.pallas_call(body, name=name, out_shape=shapes, compiler_params=params(63))(*parts)


def sync(*values):
    return lax.optimization_barrier(values)


def flip(value, bits):
    return lax.ppermute(value, "dp", [(i, i ^ bits) for i in range(16)])


def on_device(tokens, lengths, w_qkv, w_out, w_in, w_back, bias_q, value_bias, bias_out, gain1, shift1, bias_in, bias_back, gain2, shift2, cotangent):
    rows_local, half, width = tokens.shape
    dp = lax.axis_size("dp")
    dp_bits = dp.bit_length() - 1
    core = lax.axis_index("seq")
    rows = rows_local // 2
    length = 2 * half
    total = rows * length
    order_a = (0, 1) + tuple(range(2, dp_bits))
    order_b = (1, 0) + tuple(range(2, dp_bits))

    def send_rows(value):
        return swap(lax.dynamic_slice_in_dim(value, (1 - core) * rows, rows, 0))

    other = send_rows(tokens)
    cot_other = send_rows(cotangent)
    bq, bv, bo, g1, s1, bi, bb, g2, s2 = (bias_q, value_bias, bias_out, gain1, shift1, bias_in, bias_back, gain2, shift2)
    core_one = core.reshape(1).astype(jnp.int32)
    me = lax.axis_index("dp")
    fast = dp == 16 and width == 2 * LANES
    qkv, probs, full_tokens, mixed, low, hat1, inv1, inverse = attention_call(core_one, lengths, tokens, other, w_qkv, w_out, (bq, bv, bo, g1, s1))

    def flat(value):
        return value.reshape(total, value.shape[-1])

    full_tokens = flat(full_tokens)
    output, output_other, cls_own, dpre1, dmixed, g_bias_in, g_gain2, g_shift2, g_bias_back, g_gain1, g_shift1, g_bias_out, *grads = feed_call(
        core_one, lengths, flat(low), w_in, w_back, w_out, flat(mixed), flat(hat1), flat(inv1), flat(inverse), cotangent, cot_other,
        (bi.reshape(1, -1), bb, g1, g2, s2), dp, fast,
    )
    dmixed = dmixed.reshape(rows, length, width)
    cls_own = cls_own[:, : lengths.shape[1]]
    if fast:
        where = jnp.stack([me >> 2, (me >> 1) & 1, me & 1]).astype(jnp.int32)

        def view(value):
            return value.reshape((2, value.shape[0] // 2, 4, 2, 2) + value.shape[2:])

        def cross(parts, bit_a, bit_b):
            return flip(parts[0], bit_a), flip(parts[len(parts) // 2], bit_b)

        def along_z(parts):
            return lax.all_to_all(parts, "dp", 0, 0, axis_index_groups=[[i, i + 4, i + 8, i + 12] for i in range(4)], tiled=True)

        keep_b, send_b, keep_i, send_i = grads
        got_b = swap(send_b)
        base_b = view(keep_b), view(got_b)
        (back,) = add_pieces(where, [fold_first(*base_b)], "fold_a")
        dmixed, back, send_i, output_other = sync(dmixed, back, send_i, output_other)
        got_b = cross(back, 1, 2)
        got_i = swap(send_i)
        output_got = swap(output_other)
        dproj, *bias_a = attention_grad(qkv, probs, mixed, dmixed, 0, 1)
        dproj, got_i, keep_i, output_got = sync(dproj, got_i, keep_i, output_got)
        base_i = view(keep_i), view(got_i)
        (inner,) = add_pieces(where, [fold_first(*base_i)], "fold_b")
        inner, got_b = sync(inner, got_b)
        got_i = cross(inner, 1, 2)
        (back,) = add_pieces(where, [fold_second(*base_b, got_b)], "fold_b2")
        dmixed, back = sync(dmixed, back)
        got_b = cross(back, 2, 1)
        dproj, *bias_b = attention_grad(qkv, probs, mixed, dmixed, 1, 1, dproj)
        keep_q, send_q = grad_proj(
            core_one, full_tokens, dproj.reshape(3, total, width),
            (bias_a[0], bias_a[1], g_bias_out, g_gain1, g_shift1, g_bias_in, g_bias_back, g_gain2, g_shift2), bias_b, dp,
        )
        send_q, keep_q, got_b, got_i = sync(send_q, keep_q, got_b, got_i)
        got_q = swap(send_q)
        (inner,) = add_pieces(where, [fold_second(*base_i, got_i)], "fold_c")
        inner, got_q, keep_q, cls_own = sync(inner, got_q, keep_q, cls_own)
        got_i = cross(inner, 2, 1)
        cls_got = swap(cls_own)
        base_q = view(keep_q), view(got_q)
        (proj,) = add_pieces(where, [fold_first(*base_q)], "fold_d")
        proj, got_i, cls_got = sync(proj, got_i, cls_got)
        got_q = cross(proj, 1, 2)
        split = back[1].shape[0]
        joint = add_pieces(where, fold_third_pair(fold_third(back, got_b), fold_third(inner, got_i)), "fold_e")[0][0]
        dproj, joint = sync(dproj, joint)
        got_i = along_z(joint)
        dinput, dinput_other = input_grad_call(core_one, dproj.reshape(3, total, width), dpre1, w_qkv, half)
        dinput, dinput_other, got_q, output = sync(dinput, dinput_other, got_q, output)
        (proj,) = add_pieces(where, [fold_second(*base_q, got_q)], "fold_f")
        proj, dinput_other, output = sync(proj, dinput_other, output)
        got_q = cross(proj, 2, 1)
        dinput_got = swap(dinput_other)
        output = lax.dynamic_update_slice_in_dim(output, output_got, (1 - core) * rows, 0)
        output, got_q, dinput_got = sync(output, got_q, dinput_got)
        (proj,) = add_pieces(where, [fold_third(proj, got_q, False)], "fold_g")
        got_q = [proj[0]] + [flip(proj[n], 4 * n) for n in (1, 2, 3)]
        dinput, proj = sync(dinput, proj)
        dinput = lax.dynamic_update_slice_in_dim(dinput, dinput_got, (1 - core) * rows, 0)
        (r_back,) = fold_last(got_i, (width,), "back_sum", w_back.shape[0] // width, 0, 0, split)
        r_in, r_out = fold_last(got_i, (w_in.shape[1], width), "inner_sum", 1, 0, split)
        r_in, r_back, got_q, dinput = sync(r_in, r_back, got_q, dinput)
        r_qkv, r_vec = fold_last(got_q, (3 * width,), "proj_sum", 1, 8)
        r_vec = r_vec[: (8 * width + w_in.shape[1]) // (2 * dp)]
    else:
        g_back, g_inner = grads
        r_back = reduce_scatter(g_back, order_a, dp, dp_bits)
        r_inner = reduce_scatter(g_inner, order_b, dp, dp_bits)
        r_in, r_out = r_inner[:, :-width], r_inner[:, -width:]
        output_got, cls_got = swap(output_other), swap(cls_own)
        dproj, g_bias_q, g_bias_v = attention_grad(qkv, probs, mixed, dmixed, 0, rows)
        dproj = dproj.reshape(3, total, width)
        g_qkv = jnp.concatenate([weight_grad(full_tokens, dproj[n], width, width, "grad_qkv") for n in range(3)], axis=1)
        r_qkv = reduce_scatter(g_qkv, order_b, dp, dp_bits)
        dinput, dinput_other = input_grad_call(core_one, dproj, dpre1, w_qkv, half)
        dinput_got = swap(dinput_other)
    if not fast:
        table = vector_table((g_bias_q, g_bias_v, g_bias_out, g_gain1, g_shift1, g_bias_in, g_bias_back, g_gain2, g_shift2), 2 * dp)
        r_vec = jnp.sum(lax.all_to_all(table, ("dp", "seq"), 0, 0, tiled=True), axis=0)[: (8 * width + w_in.shape[1]) // (2 * dp)]
        output = lax.dynamic_update_slice_in_dim(output, output_got, (1 - core) * rows, 0)
        dinput = lax.dynamic_update_slice_in_dim(dinput, dinput_got, (1 - core) * rows, 0)
    cls = jnp.where(core == 0, jnp.concatenate([cls_own, cls_got], axis=0), jnp.concatenate([cls_got, cls_own], axis=0))
    return (
        output,
        cls,
        dinput,
        r_qkv.reshape(-1),
        r_out.reshape(-1),
        r_in.reshape(-1),
        r_back.reshape(-1),
        r_vec,
    )


def solution(mesh):
    row = P("dp", "seq", None)
    both = P(("dp", "seq"))
    return jax.shard_map(
        on_device,
        mesh=mesh,
        in_specs=(row, P("dp", None)) + (P(),) * 13 + (row,),
        out_specs=(row, P("dp", None, None), row, both, both, both, both, both),
        check_vma=False,
    )
```

```python
from functools import partial

import jax
import jax.numpy as jnp
from jax import lax
from jax.experimental import pallas as pl
from jax.experimental.pallas import tpu as pltpu
from jax.sharding import PartitionSpec as P

HEADS = 12
EPS = 1e-12
BF = jnp.bfloat16
F32 = jnp.float32
VMEM_LIMIT = 60 << 20
RSQRT2 = 0.7071067811865476
RSQRT2PI = 0.3989422804014327


def row_dot(left, right):
    return lax.dot_general(left, right, (((1,), (0,)), ((), ())), preferred_element_type=F32)


def row_dot_t(left, right):
    return lax.dot_general(left, right, (((1,), (1,)), ((), ())), preferred_element_type=F32)


def col_dot(left, right):
    return lax.dot_general(left, right, (((0,), (0,)), ((), ())), preferred_element_type=F32)


def gelu_pair(value):
    expo = jnp.exp(value * value * -0.5)
    phi = 0.5 + 0.5 * lax.erf(value * RSQRT2)
    return value * phi, phi + value * expo * RSQRT2PI


def whole(shape):
    return pl.BlockSpec(shape, lambda *_: (0,) * len(shape))


ANY = pl.BlockSpec(memory_space=pl.ANY)
HBM = pl.BlockSpec(memory_space=pltpu.HBM)


def params(mib):
    return pltpu.CompilerParams(vmem_limit_bytes=(mib << 20) + (896 << 10))


def row_starts(len_ref, row):
    starts = [jnp.int32(0)]
    for j in range(len_ref.shape[1] - 1):
        starts.append(starts[-1] + len_ref[row, j])
    return starts


def attention_kernel(
    core_ref, len_ref, own_ref, other_ref, wqkv_hbm, wout_hbm, bq_ref, bv_ref, bo_ref, g1_ref, s1_ref,
    qkv_hbm, probs_hbm, x_ref, mixed_ref, low_ref, hat1_ref, inv1_ref, scale_ref,
    bias_ref, ahead0_ref, ahead1_ref, qkv_ref, wqkv_ref, wout_ref, p_ref, w_sem, p_sem, q_sem,
):
    step = pl.program_id(0)
    core = core_ref[0]
    rows = pl.num_programs(0)
    half, width = own_ref.shape[1:]
    length = 2 * half
    pairs = width // 128
    parts = [slice(n * width, (n + 1) * width) for n in range(3)]
    copies = [pltpu.make_async_copy(wqkv_hbm.at[:, part], wqkv_ref.at[:, part], w_sem.at[n]) for n, part in enumerate(parts)]
    copies.append(pltpu.make_async_copy(wout_hbm, wout_ref, w_sem.at[3]))

    @pl.when(step == 0)
    def _():
        for copy in copies:
            copy.start()

    x_ref[0, pl.ds(pl.multiple_of(core * half, half), half), :] = own_ref[0]
    x_ref[0, pl.ds(pl.multiple_of((1 - core) * half, half), half), :] = other_ref[0]
    starts = row_starts(len_ref, core * rows + step)
    down = lax.broadcasted_iota(jnp.int32, (length, 1), 0)
    across = lax.broadcasted_iota(jnp.int32, (1, length), 1)
    seg_down = jnp.zeros((length, 1), jnp.int32)
    seg_across = jnp.zeros((1, length), jnp.int32)
    for start in starts[1:]:
        seg_down += (down >= start).astype(jnp.int32)
        seg_across += (across >= start).astype(jnp.int32)
    bias_ref[...] = jnp.where(seg_down == seg_across, 0.0, -1e30)

    for n, part in enumerate(parts):
        @pl.when(step == 0)
        def _():
            copies[n].wait()

        value = row_dot(x_ref[0], wqkv_ref[:, part])
        if n == 0:
            value = (value + bq_ref[...]) * (width // HEADS) ** -0.5
        if n == 2:
            value = value + bv_ref[...]
        qkv_ref[:, part] = value.astype(BF)
    save = pltpu.make_async_copy(qkv_ref, qkv_hbm.at[step], q_sem)
    save.start()

    first = lax.broadcasted_iota(jnp.int32, (1, 128), 1) < 64

    def columns(part, pair):
        return pl.ds(pl.multiple_of(part * width + pair * 128, 128), 128)

    def scores(pair, into):
        q_pair = qkv_ref[:, columns(0, pair)]
        k_pair = qkv_ref[:, columns(1, pair)]
        for h in range(2):
            on = first if h == 0 else jnp.logical_not(first)
            into[h] = row_dot_t(jnp.where(on, q_pair, jnp.zeros_like(q_pair)), k_pair)

    def finish(pair, held, slot):
        out_copy = pltpu.make_async_copy(p_ref.at[slot], probs_hbm.at[step, pair], p_sem.at[slot])

        @pl.when(pair >= 2)
        def _():
            out_copy.wait()

        v_pair = qkv_ref[:, columns(2, pair)]
        outs = []
        for h in range(2):
            on = first if h == 0 else jnp.logical_not(first)
            s = held[h] + bias_ref[...]
            e = jnp.exp(s - jnp.max(s, axis=-1, keepdims=True)).astype(BF)
            p_ref[slot, h] = e
            outs.append(row_dot(e, jnp.where(on, v_pair, jnp.ones_like(v_pair))))
        sums = pltpu.roll(jnp.where(first, outs[1], outs[0]), 64, 1)
        inverse = 1.0 / sums
        scale_ref[0, :, columns(0, pair)] = inverse
        mixed_ref[0, :, columns(0, pair)] = (jnp.where(first, outs[0], outs[1]) * inverse).astype(BF)
        out_copy.start()

    scores(0, ahead0_ref)

    def two_pairs(i, carry):
        scores(2 * i + 1, ahead1_ref)
        finish(2 * i, ahead0_ref, 0)
        scores(jnp.minimum(2 * i + 2, pairs - 1), ahead0_ref)
        finish(2 * i + 1, ahead1_ref, 1)
        return carry

    lax.fori_loop(0, pairs // 2, two_pairs, 0, unroll=True)
    for tail in (pairs - 2, pairs - 1):
        pltpu.make_async_copy(p_ref.at[tail % 2], probs_hbm.at[step, tail], p_sem.at[tail % 2]).wait()

    @pl.when(step == 0)
    def _():
        copies[3].wait()

    pre = x_ref[0].astype(F32) + row_dot(mixed_ref[0], wout_ref[...]) + bo_ref[...]
    center = pre - jnp.mean(pre, axis=-1, keepdims=True)
    inv = lax.rsqrt(jnp.mean(center * center, axis=-1, keepdims=True) + EPS)
    hat = center * inv
    hat1_ref[0] = hat.astype(BF)
    inv1_ref[0] = inv
    low_ref[0] = (hat * g1_ref[...] + s1_ref[...]).astype(BF)
    save.wait()


def attention_call(core, lengths, tokens, other, w_qkv, w_out, vectors):
    rows_local, half, width = tokens.shape
    rows = rows_local // 2
    length = 2 * half
    pairs = width // 128

    def full(n):
        return pl.BlockSpec((1, length, n), lambda r, *_: (r, 0, 0))

    def row(n, kind=BF):
        return jax.ShapeDtypeStruct((rows, length, n), kind)

    return pl.pallas_call(
        attention_kernel,
        name="attention_rows",
        out_shape=[
            row(3 * width), jax.ShapeDtypeStruct((rows, pairs, 2, length, length), BF), row(width), row(width), row(width), row(width),
            row(1, F32), row(width, F32),
        ],
        grid_spec=pltpu.PrefetchScalarGridSpec(
            num_scalar_prefetch=2,
            grid=(rows,),
            in_specs=[
                pl.BlockSpec((1, half, width), lambda r, core, lens: (core[0] * rows + r, 0, 0)),
                pl.BlockSpec((1, half, width), lambda r, *_: (r, 0, 0)),
                ANY,
                ANY,
            ]
            + [whole(v.shape) for v in vectors],
            out_specs=[HBM, HBM] + [full(width)] * 4 + [full(1), full(width)],
            scratch_shapes=[
                pltpu.VMEM((length, length), F32),
                pltpu.VMEM((2, length, length), F32),
                pltpu.VMEM((2, length, length), F32),
                pltpu.VMEM((length, 3 * width), BF),
                pltpu.VMEM(w_qkv.shape, BF),
                pltpu.VMEM(w_out.shape, BF),
                pltpu.VMEM((2, 2, length, length), BF),
                pltpu.SemaphoreType.DMA((4,)),
                pltpu.SemaphoreType.DMA((2,)),
                pltpu.SemaphoreType.DMA,
            ],
        ),
        compiler_params=params(62),
        cost_estimate=pl.CostEstimate(
            flops=8 * rows * length * width * width + 4 * rows * length * length * width,
            bytes_accessed=35 << 20,
            transcendentals=rows * HEADS * length * length,
        ),
    )(core, lengths, tokens, other, w_qkv, w_out, *vectors)


def feed_kernel(
    split, core_ref, len_ref, low_ref, win_hbm, wback_hbm, wout_hbm, mixed_hbm, hat1_hbm, inv1_hbm, scale_hbm, cot_hbm, cot_other_hbm,
    bi_ref, bb_ref, g1_ref, g2_ref, s2_ref,
    out_hbm, other_hbm, cls_ref, dpre_hbm, dmixed_hbm, gi_ref, gg2_ref, gs2_ref, gb2_ref, gg1_ref, gs1_ref, gb1_ref, *rest
):
    n_grads = 4 if split else 2
    grads = rest[:n_grads]
    (win_ref, wback_ref, wout_ref, mixed_ref, hat1_ref, inv1_ref, scale_ref, cot_ref, out_ref, act_ref, slope_ref, acc_ref, dfeed_ref,
     grad_ref, w_sem, v_sem, c_sem, o_sem, d_sem) = rest[n_grads:]
    step = pl.program_id(0)
    core = core_ref[0]
    total, width = low_ref.shape
    length = 2 * cot_other_hbm.shape[1]
    half = length // 2
    group = total // length
    hidden = act_ref.shape[1]
    chunk = width
    chunks = hidden // chunk
    piece = 768
    pieces = [slice(n * piece, (n + 1) * piece) for n in range(chunk // piece)]
    weights = []
    for c in range(chunks):
        part = slice(c * chunk, (c + 1) * chunk)
        weights.append(pltpu.make_async_copy(win_hbm.at[:, part], win_ref.at[:, part], w_sem.at[2 * c]))
        weights.append(pltpu.make_async_copy(wback_hbm.at[part], wback_ref.at[part], w_sem.at[2 * c + 1]))
    values = [
        pltpu.make_async_copy(src, dst, v_sem.at[i])
        for i, (src, dst) in enumerate(
            ((hat1_hbm, hat1_ref), (inv1_hbm, inv1_ref), (wout_hbm, wout_ref), (scale_hbm, scale_ref), (mixed_hbm, mixed_ref))
        )
    ]
    loads, stores = [], []
    for r in range(group):
        own = pl.ds(pl.multiple_of(r * length + core * half, half), half)
        other = pl.ds(pl.multiple_of(r * length + (1 - core) * half, half), half)
        loads.append(pltpu.make_async_copy(cot_hbm.at[core * group + r], cot_ref.at[own], c_sem.at[r]))
        loads.append(pltpu.make_async_copy(cot_other_hbm.at[r], cot_ref.at[other], c_sem.at[group + r]))
        stores.append(pltpu.make_async_copy(out_ref.at[other], other_hbm.at[r], o_sem.at[group + r]))
        stores.append(pltpu.make_async_copy(out_ref.at[own], out_hbm.at[core * group + r], o_sem.at[r]))
    dpre_store = pltpu.make_async_copy(out_ref, dpre_hbm, d_sem.at[0])
    dmixed_store = pltpu.make_async_copy(cot_ref, dmixed_hbm, d_sem.at[1])

    @pl.when(step == 0)
    def _():
        for copy in weights + loads + values:
            copy.start()

    for c in range(chunks):
        @pl.when(step == c)
        def _():
            weights[2 * c].wait()
            weights[2 * c + 1].wait()

    @pl.when(step < chunks)
    def _():
        base = pl.multiple_of(step * chunk, chunk)
        for n in range(len(pieces)):
            cols = pl.ds(base + n * piece, piece)
            act, slope = gelu_pair(row_dot(low_ref[...], win_ref[:, cols]) + bi_ref[:, cols])
            act_ref[:, cols] = act.astype(BF)
            slope_ref[:, cols] = slope.astype(BF)
        rows = pl.ds(base, chunk)

        @pl.when(step == 0)
        def _():
            for cols in pieces:
                acc_ref[:, cols] = row_dot(act_ref[:, rows], wback_ref[rows, cols])

        @pl.when(step > 0)
        def _():
            for cols in pieces:
                acc_ref[:, cols] += row_dot(act_ref[:, rows], wback_ref[rows, cols])

    block = 256

    @pl.when(step == chunks - 1)
    def _():
        for load in loads:
            load.wait()
        gg2_ref[...] = jnp.zeros_like(gg2_ref)
        gs2_ref[...] = jnp.zeros_like(gs2_ref)
        gb2_ref[...] = jnp.zeros_like(gb2_ref)

        def token_body(i, carry):
            at = pl.ds(pl.multiple_of(i * block, block), block)
            pre = low_ref[at, :].astype(F32) + acc_ref[at, :] + bb_ref[...]
            center = pre - jnp.mean(pre, axis=-1, keepdims=True)
            inv = lax.rsqrt(jnp.mean(center * center, axis=-1, keepdims=True) + EPS)
            hat = center * inv
            out_ref[at, :] = (hat * g2_ref[...] + s2_ref[...]).astype(BF)
            dy = cot_ref[at, :].astype(F32)
            gg2_ref[...] += jnp.sum(dy * hat, axis=0, keepdims=True)
            gs2_ref[...] += jnp.sum(dy, axis=0, keepdims=True)
            g = dy * g2_ref[...]
            dpre = inv * (g - jnp.mean(g, axis=-1, keepdims=True) - hat * jnp.mean(g * hat, axis=-1, keepdims=True))
            dfeed = dpre.astype(BF)
            dfeed_ref[at, :] = dfeed
            gb2_ref[...] += jnp.sum(dfeed.astype(F32), axis=0, keepdims=True)
            return carry

        lax.fori_loop(0, total // block, token_body, 0)
        for store in stores:
            store.start()
        which = lax.broadcasted_iota(jnp.int32, (8, 1), 0)
        across = lax.broadcasted_iota(jnp.int32, (1, length), 1)
        for r in range(group):
            down = jnp.full((8, 1), -1, jnp.int32)
            for j, start in enumerate(row_starts(len_ref, core * group + r)):
                down = jnp.where(which == j, start, down)
            choose = (down == across).astype(F32).astype(BF)
            cls_ref[r] = row_dot(choose, out_ref[r * length : (r + 1) * length]).astype(BF)

    def put_grad(value, kept, sent, stack):
        if split:
            grad_ref[...] = value
            split_store(grad_ref, kept, sent, core, 2, stack)
        else:
            kept[...] = value.astype(BF)

    keep_b, keep_i = grads[0], grads[n_grads // 2]
    send_b, send_i = (grads[1], grads[3]) if split else (None, None)

    @pl.when(jnp.logical_and(step >= chunks, step < 2 * chunks))
    def _():
        base = pl.multiple_of((step - chunks) * chunk, chunk)
        rows = pl.ds(base, chunk)
        put_grad(col_dot(act_ref[:, rows], dfeed_ref[...]), keep_b, send_b, chunks)
        for n in range(len(pieces)):
            cols = pl.ds(base + n * piece, piece)
            inner = (row_dot_t(dfeed_ref[...], wback_ref[cols, :]) * slope_ref[:, cols].astype(F32)).astype(BF)
            slope_ref[:, cols] = inner
            gi_ref[:, cols] = jnp.sum(inner.astype(F32), axis=0, keepdims=True)

        @pl.when(step == chunks)
        def _():
            for cols in pieces:
                acc_ref[:, cols] = row_dot_t(slope_ref[:, rows], win_ref[cols, rows])

        @pl.when(step > chunks)
        def _():
            for cols in pieces:
                acc_ref[:, cols] += row_dot_t(slope_ref[:, rows], win_ref[cols, rows])

        put_grad(col_dot(low_ref[...], slope_ref[:, rows]), keep_i, send_i, 1)

    @pl.when(step == 2 * chunks)
    def _():
        for store in stores:
            store.wait()
        for value in values:
            value.wait()
        gg1_ref[...] = jnp.zeros_like(gg1_ref)
        gs1_ref[...] = jnp.zeros_like(gs1_ref)
        gb1_ref[...] = jnp.zeros_like(gb1_ref)

        def token_body(i, carry):
            at = pl.ds(pl.multiple_of(i * block, block), block)
            dn = dfeed_ref[at, :].astype(F32) + acc_ref[at, :]
            hat = hat1_ref[at, :].astype(F32)
            gg1_ref[...] += jnp.sum(dn * hat, axis=0, keepdims=True)
            gs1_ref[...] += jnp.sum(dn, axis=0, keepdims=True)
            g = dn * g1_ref[...]
            dpre = inv1_ref[at, :] * (g - jnp.mean(g, axis=-1, keepdims=True) - hat * jnp.mean(g * hat, axis=-1, keepdims=True))
            branch = dpre.astype(BF)
            out_ref[at, :] = branch
            gb1_ref[...] += jnp.sum(branch.astype(F32), axis=0, keepdims=True)
            return carry

        lax.fori_loop(0, total // block, token_body, 0)
        dpre_store.start()
        for cols in pieces:
            cot_ref[:, cols] = (row_dot_t(out_ref[...], wout_ref[cols, :]) * scale_ref[:, cols]).astype(BF)
        dmixed_store.start()
        put_grad(col_dot(mixed_ref[...], out_ref[...]), keep_i, send_i, 1)
        dpre_store.wait()
        dmixed_store.wait()


def feed_call(core, lengths, low, w_in, w_back, w_out, mixed, hat1, inv1, scale, cot, cot_other, vectors, dp, split):
    total, width = low.shape
    half = cot.shape[1]
    group = cot.shape[0] // 2
    hidden = w_in.shape[1]
    chunks = hidden // width

    def in_back(j):
        return jnp.clip(j - chunks, 0, chunks - 1)

    def in_inner(j):
        return jnp.clip(j - chunks, 0, chunks)

    one = jax.ShapeDtypeStruct((1, width), F32)
    row = jax.ShapeDtypeStruct((total, width), BF)
    shapes = [
        jax.ShapeDtypeStruct(cot.shape, BF),
        jax.ShapeDtypeStruct(cot_other.shape, BF),
        jax.ShapeDtypeStruct((group, 8, width), BF),
        row,
        row,
        jax.ShapeDtypeStruct((1, hidden), F32),
    ] + [one] * 6
    specs = [HBM, HBM, whole((group, 8, width)), HBM, HBM, whole((1, hidden))] + [whole((1, width))] * 6
    if split:
        rows_i = width // (2 * dp)
        devices = dp // chunks
        shapes += [jax.ShapeDtypeStruct((2 * chunks, dp, rows_i, LANES), BF)] * 2
        specs += [pl.BlockSpec((2 * chunks, devices, rows_i, LANES), lambda j, *_: (0, in_back(j), 0, 0))] * 2
        shapes += [jax.ShapeDtypeStruct((2 * (chunks + 1), dp, rows_i, LANES), BF)] * 2
        specs += [pl.BlockSpec((2, dp, rows_i, LANES), lambda j, *_: (in_inner(j), 0, 0, 0))] * 2
    else:
        shapes += [jax.ShapeDtypeStruct((hidden, width), BF), jax.ShapeDtypeStruct((width, hidden + width), BF)]
        specs += [pl.BlockSpec((width, width), lambda j, *_: (in_back(j), 0)), pl.BlockSpec((width, width), lambda j, *_: (0, in_inner(j)))]
    return pl.pallas_call(
        partial(feed_kernel, split),
        name="feed_rows",
        out_shape=shapes,
        grid_spec=pltpu.PrefetchScalarGridSpec(
            num_scalar_prefetch=2,
            grid=(2 * chunks + 1,),
            in_specs=[pl.BlockSpec((total, width), lambda *_: (0, 0), pipeline_mode=pl.Buffered(1))]
            + [ANY] * 9
            + [whole((1, hidden))]
            + [whole((width,))] * 4,
            out_specs=specs,
            scratch_shapes=[
                pltpu.VMEM(w_in.shape, BF),
                pltpu.VMEM(w_back.shape, BF),
                pltpu.VMEM(w_out.shape, BF),
                pltpu.VMEM((total, width), BF),
                pltpu.VMEM((total, width), BF),
                pltpu.VMEM((total, 1), F32),
                pltpu.VMEM((total, width), F32),
                pltpu.VMEM((total, width), BF),
                pltpu.VMEM((total, width), BF),
                pltpu.VMEM((total, hidden), BF),
                pltpu.VMEM((total, hidden), BF),
                pltpu.VMEM((total, width), F32),
                pltpu.VMEM((total, width), BF),
                pltpu.VMEM((width, width), F32),
                pltpu.SemaphoreType.DMA((2 * chunks,)),
                pltpu.SemaphoreType.DMA((5,)),
                pltpu.SemaphoreType.DMA((2 * group,)),
                pltpu.SemaphoreType.DMA((2 * group,)),
                pltpu.SemaphoreType.DMA((2,)),
            ],
        ),
        compiler_params=params(61),
        cost_estimate=pl.CostEstimate(flops=2 * total * width * (6 * hidden + 2 * width), bytes_accessed=40 << 20, transcendentals=2 * total * hidden),
    )(core, lengths, low, w_in, w_back, w_out, mixed, hat1, inv1, scale, cot, cot_other, *vectors)


def weight_grad(left, right, block_m, block_n, name):
    total, m = left.shape
    n = right.shape[1]

    def body(l_ref, r_ref, o_ref, t_ref):
        @pl.when(pl.program_id(1) == 0)
        def _():
            t_ref[...] = l_ref[...].T

        o_ref[...] = row_dot(t_ref[...], r_ref[...]).astype(BF)

    return pl.pallas_call(
        body,
        name=name,
        out_shape=jax.ShapeDtypeStruct((m, n), BF),
        grid=(m // block_m, n // block_n),
        in_specs=[pl.BlockSpec((total, block_m), lambda i, j: (0, i)), pl.BlockSpec((total, block_n), lambda i, j: (0, j))],
        out_specs=pl.BlockSpec((block_m, block_n), lambda i, j: (i, j)),
        scratch_shapes=[pltpu.VMEM((block_m, total), BF)],
        compiler_params=params(63),
        cost_estimate=pl.CostEstimate(flops=2 * total * m * n, bytes_accessed=2 * (total * (m + n) + m * n), transcendentals=0),
    )(left, right)


def attention_grad(qkv, probs, mixed, d, lower, count, partial_out=None):
    rows, length, width = mixed.shape
    pairs = width // 128
    scale = (width // HEADS) ** -0.5
    more = [] if partial_out is None else [partial_out]

    def body(q_ref, k_ref, v_ref, p_ref, m_ref, d_ref, *rest):
        out_ref, bq_ref, bv_ref = rest[-3:]

        @pl.when(pl.program_id(1) == 0)
        def _():
            bq_ref[...] = jnp.zeros_like(bq_ref)
            bv_ref[...] = jnp.zeros_like(bv_ref)

        first = lax.broadcasted_iota(jnp.int32, (1, 128), 1) < 64
        q, k, v, d = q_ref[0], k_ref[0], v_ref[0], d_ref[0]
        product = d.astype(F32) * m_ref[0].astype(F32)
        q_t, d_t, k_t = q.T, d.T, k.T
        dqs, dks, dvs = [], [], []
        for h in range(2):
            on = first if h == 0 else jnp.logical_not(first)
            part = slice(h * 64, (h + 1) * 64)
            delta = jnp.sum(jnp.where(on, product, 0.0), axis=-1, keepdims=True)
            dprobs = row_dot_t(jnp.where(on, d, jnp.zeros_like(d)), v)
            p = p_ref[0, 0, h]
            ds = (p.astype(F32) * (dprobs - delta)).astype(BF)
            dqs.append(row_dot_t(k_t[part], ds))
            dks.append(row_dot(q_t[part], ds))
            dvs.append(row_dot(d_t[part], p))
        dq = (jnp.concatenate(dqs, axis=0) * scale).T.astype(BF)
        dv = jnp.concatenate(dvs, axis=0).T.astype(BF)
        out_ref[0, 0] = dq
        out_ref[1, 0] = jnp.concatenate(dks, axis=0).T.astype(BF)
        out_ref[2, 0] = dv
        bq_ref[...] += jnp.sum(dq.astype(F32), axis=0, keepdims=True)
        bv_ref[...] += jnp.sum(dv.astype(F32), axis=0, keepdims=True)

    def cols(base):
        return pl.BlockSpec((1, length, 128), lambda p, r: (lower + r, 0, base + p))

    vec = pl.BlockSpec((1, 128), lambda p, r: (0, p))
    one = jax.ShapeDtypeStruct((1, width), F32)
    return pl.pallas_call(
        body,
        name="attention_grad",
        out_shape=[jax.ShapeDtypeStruct((3, rows, length, width), BF), one, one],
        grid=(pairs, count),
        input_output_aliases={6: 0} if more else {},
        in_specs=[cols(0), cols(pairs), cols(2 * pairs), pl.BlockSpec((1, 1, 2, length, length), lambda p, r: (lower + r, p, 0, 0, 0)), cols(0), cols(0)]
        + [ANY] * len(more),
        out_specs=[pl.BlockSpec((3, 1, length, 128), lambda p, r: (0, lower + r, 0, p)), vec, vec],
        compiler_params=params(63),
        cost_estimate=pl.CostEstimate(flops=8 * count * length * length * width, bytes_accessed=(15 * count) << 20, transcendentals=0),
    )(qkv, qkv, qkv, probs, mixed, d, *more)


def input_grad_call(core, dproj, dpre, w_qkv, half):
    _, total, width = dproj.shape
    length = 2 * half
    group = total // length

    def body(core_ref, p_ref, d_hbm, w_ref, own_hbm, other_hbm, acc_ref, out_ref, d_ref, sem, d_sem):
        step = pl.program_id(0)
        load = pltpu.make_async_copy(d_hbm, d_ref, d_sem)
        core = core_ref[0]

        @pl.when(step == 0)
        def _():
            load.start()

        value = row_dot_t(p_ref[0], w_ref[...])

        @pl.when(step == 0)
        def _():
            acc_ref[...] = value

        @pl.when(step == 1)
        def _():
            acc_ref[...] += value

        @pl.when(step == 2)
        def _():
            load.wait()
            out_ref[...] = (acc_ref[...] + value + d_ref[...].astype(F32)).astype(BF)
            stores = []
            for r in range(group):
                other = pl.ds(pl.multiple_of(r * length + (1 - core) * half, half), half)
                own = pl.ds(pl.multiple_of(r * length + core * half, half), half)
                stores.append(pltpu.make_async_copy(out_ref.at[other], other_hbm.at[r], sem.at[r]))
                stores.append(pltpu.make_async_copy(out_ref.at[own], own_hbm.at[core * group + r], sem.at[group + r]))
            for store in stores:
                store.start()
            for store in stores:
                store.wait()

    return pl.pallas_call(
        body,
        name="input_grad",
        out_shape=[jax.ShapeDtypeStruct((2 * group, half, width), BF), jax.ShapeDtypeStruct((group, half, width), BF)],
        grid_spec=pltpu.PrefetchScalarGridSpec(
            num_scalar_prefetch=1,
            grid=(3,),
            in_specs=[
                pl.BlockSpec((1, total, width), lambda n, *_: (n, 0, 0)),
                ANY,
                pl.BlockSpec((width, width), lambda n, *_: (0, n)),
            ],
            out_specs=[HBM, HBM],
            scratch_shapes=[pltpu.VMEM((total, width), F32), pltpu.VMEM((total, width), BF), pltpu.VMEM((total, width), BF), pltpu.SemaphoreType.DMA((2 * group,)), pltpu.SemaphoreType.DMA],
        ),
        compiler_params=params(63),
        cost_estimate=pl.CostEstimate(flops=6 * total * width * width, bytes_accessed=10 << 20, transcendentals=0),
    )(core, dproj, dpre, w_qkv)


def vector_table(parts, devices, more=()):
    cut = sum(p.shape[1] for p in parts) // devices

    def body(*refs):
        *ins, out = refs
        values = [ref[...] for ref in ins[: len(parts)]]
        for i, ref in enumerate(ins[len(parts) :]):
            values[i] = values[i] + ref[...]
        joined = jnp.concatenate(values, axis=1)
        out[...] = jnp.zeros_like(out)
        for d in range(devices):
            out[d : d + 1, :cut] = joined[:, d * cut : (d + 1) * cut]

    return pl.pallas_call(
        body,
        name="vector_table",
        out_shape=jax.ShapeDtypeStruct((devices, LANES), F32),
        compiler_params=params(63),
    )(*parts, *more)


def swap(value):
    return lax.ppermute(value, "seq", [(0, 1), (1, 0)])


def pick(value, index, axis):
    return lax.dynamic_index_in_dim(value, index, axis, keepdims=False)


def reduce_stages(part, order, dp_bits, dp):
    me = lax.axis_index("dp")
    n_halving = dp_bits - 2
    shape = part.shape[1:]
    current = part.reshape((2,) * dp_bits + shape)
    left = list(range(dp_bits - 1, -1, -1))
    for bit in order[:n_halving]:
        axis = left.index(bit)
        mine = (me >> bit) & 1
        pairs = [(i, i ^ (1 << bit)) for i in range(dp)]
        send = pick(current, 1 - mine, axis).astype(BF)
        got = lax.ppermute(send, "dp", pairs)
        keep = pick(current, mine, axis)
        current = (keep.astype(F32) + got.astype(F32)).astype(BF)
        left.remove(bit)
    high, low = left
    group = (((me >> high) & 1) << 1) | ((me >> low) & 1)
    current = current.reshape((4,) + shape)
    total = pick(current, group, 0).astype(F32)
    for other in (1, 2, 3):
        flip = ((other >> 1) << high) | ((other & 1) << low)
        pairs = [(i, i ^ flip) for i in range(dp)]
        send = pick(current, group ^ other, 0).astype(BF)
        total = total + lax.ppermute(send, "dp", pairs).astype(F32)
    return total


def reduce_scatter(grad, order, dp, dp_bits):
    core = lax.axis_index("seq")
    rows = grad.shape[0] // (2 * dp)
    blocks = grad.reshape(dp, 2, rows, grad.shape[1])
    send = pick(blocks, 1 - core, 1).astype(BF)
    keep = pick(blocks, core, 1)
    part = (keep.astype(F32) + swap(send).astype(F32)).astype(BF)
    return reduce_stages(part, order, dp_bits, dp)


LANES = 384


def split_store(acc_ref, keep_ref, send_ref, core, parts, stack):
    rows = keep_ref.shape[2]
    for d in range(acc_ref.shape[0] // (2 * stack * rows)):
        for ref, side in ((keep_ref, core), (send_ref, 1 - core)):
            for r in range(stack):
                value = acc_ref[pl.ds(pl.multiple_of(((2 * d + side) * stack + r) * rows, 8), rows), :].astype(BF)
                for c in range(parts):
                    ref[c * stack + r, d] = value[:, c * LANES : (c + 1) * LANES]


def grad_proj(core, left, right, vectors, more, dp):
    total, m = left.shape
    n = 2 * LANES
    rows = m // (2 * dp)
    deep = rows // 8
    blocks = 3 * deep + 1
    cut = sum(v.shape[1] for v in vectors) // (2 * dp)

    def body(core_ref, l_ref, r_ref, *refs):
        ins = refs[: len(vectors) + len(more)]
        keep_hbm, send_hbm, keep_ref, send_ref, acc_ref, table_ref, o_sem = refs[len(ins) :]
        acc_ref[...] = col_dot(l_ref[...], r_ref[0])
        core = core_ref[0]
        step = pl.program_id(0)
        for ref, side in ((keep_ref, core), (send_ref, 1 - core)):
            for d in range(dp):
                value = acc_ref[pl.ds(pl.multiple_of((2 * d + side) * rows, 8), rows), :].astype(BF)
                for c in range(2):
                    chunk = 2 * step + c
                    first = lax.div(chunk, 3) * blocks + lax.rem(chunk, 3) * deep
                    for r in range(deep):
                        ref[first + r, d] = value[8 * r : 8 * r + 8, c * LANES : (c + 1) * LANES]

        @pl.when(step == 0)
        def _():
            values = [ref[...] for ref in ins[: len(vectors)]]
            for i, ref in enumerate(ins[len(vectors) :]):
                values[i] = values[i] + ref[...]
            joined = jnp.concatenate(values, axis=1)
            table_ref[...] = jnp.zeros_like(table_ref)
            for d in range(2 * dp):
                table_ref[d : d + 1, :cut] = joined[:, d * cut : (d + 1) * cut]
            for ref, side in ((keep_ref, core), (send_ref, 1 - core)):
                for d in range(dp):
                    line = table_ref[pl.ds(2 * d + side, 1), :].astype(BF)
                    ref[blocks - 1, d] = jnp.broadcast_to(line, (8, LANES))
                    ref[2 * blocks - 1, d] = jnp.zeros((8, LANES), BF)

        stretches = [
            [(0, 2 * deep), (blocks - 1, blocks), (2 * blocks - 1, 2 * blocks)],
            [(2 * deep, 3 * deep), (blocks, blocks + deep)],
            [(blocks + deep, blocks + 3 * deep)],
        ]
        stores, count = [], 0
        for group in stretches:
            copies = []
            for start, stop in group:
                for src, dst in ((keep_ref, keep_hbm), (send_ref, send_hbm)):
                    copies.append(pltpu.make_async_copy(src.at[start:stop], dst.at[start:stop], o_sem.at[count]))
                    count += 1
            stores.append(copies)
        for n, copies in enumerate(stores):
            @pl.when(step == n)
            def _():
                for copy in copies:
                    copy.start()

        @pl.when(step == 2)
        def _():
            for copies in stores:
                for copy in copies:
                    copy.wait()

    out = jax.ShapeDtypeStruct((2 * blocks, dp, 8, LANES), BF)
    return pl.pallas_call(
        body,
        name="grad_qkv",
        out_shape=[out, out],
        grid_spec=pltpu.PrefetchScalarGridSpec(
            num_scalar_prefetch=1,
            grid=(3,),
            in_specs=[whole((total, m)), pl.BlockSpec((1, total, n), lambda j, *_: (j, 0, 0))] + [whole(v.shape) for v in (*vectors, *more)],
            out_specs=[HBM] * 2,
            scratch_shapes=[pltpu.VMEM(out.shape, BF)] * 2 + [pltpu.VMEM((m, n), F32), pltpu.VMEM((2 * dp, LANES), F32), pltpu.SemaphoreType.DMA((12,))],
        ),
        compiler_params=params(63),
        cost_estimate=pl.CostEstimate(flops=6 * total * m * n, bytes_accessed=6 * n * (total + m), transcendentals=0),
    )(core, left, right, *vectors, *more)


def add_pieces(where, groups, name):
    counts = [len(pieces([jnp.int32(0)] * 3)) for _, _, pieces, _ in groups]
    inputs = [i for g in groups for i in g[0]]
    outputs = [o for g in groups for o in g[1]]

    def body(where_ref, *refs):
        ins = refs[: len(inputs)]
        outs = refs[len(inputs) : len(inputs) + len(outputs)]
        scratch = refs[len(inputs) + len(outputs) :]
        loads, stores, sums = [], [], []
        for n, (group_in, group_out, pieces, _) in enumerate(groups):
            k_ref, g_ref, h_ref, k_sem, g_sem, h_sem, o_sem = scratch[7 * n : 7 * n + 7]
            for i, (a, a_at, b, b_at, o, o_at, *third) in enumerate(pieces([where_ref[0], where_ref[1], where_ref[2]])):
                loads.append([pltpu.make_async_copy(ins[a].at[a_at], k_ref.at[i], k_sem.at[i])])
                loads[-1].append(pltpu.make_async_copy(ins[b].at[b_at], g_ref.at[i], g_sem.at[i]))
                if third:
                    loads[-1].append(pltpu.make_async_copy(ins[third[0]].at[third[1]], h_ref.at[i], h_sem.at[i]))
                stores.append(pltpu.make_async_copy(k_ref.at[i], outs[o].at[o_at], o_sem.at[i]))
                sums.append((k_ref, g_ref, h_ref if third else None, i))
            ins = ins[len(group_in) :]
            if n + 1 < len(groups) and groups[n + 1][1]:
                outs = outs[len(group_out) :]
        for copies in loads:
            for copy in copies:
                copy.start()
        for i, (k_ref, g_ref, h_ref, at) in enumerate(sums):
            for copy in loads[i]:
                copy.wait()
            value = k_ref[at] + g_ref[at]
            k_ref[at] = value if h_ref is None else value + h_ref[at]
            stores[i].start()
        for store in stores:
            store.wait()

    scratch_shapes = []
    for (_, _, pieces, shape), count in zip(groups, counts):
        third = count if len(pieces([jnp.int32(0)] * 3)[0]) > 6 else 1
        scratch_shapes += [pltpu.VMEM((n,) + shape, BF) for n in (count, count, third)]
        scratch_shapes += [pltpu.SemaphoreType.DMA((n,)) for n in (count, count, third, count)]
    result = pl.pallas_call(
        body,
        name=name,
        out_shape=[jax.ShapeDtypeStruct(s, BF) for s in outputs],
        grid_spec=pltpu.PrefetchScalarGridSpec(
            num_scalar_prefetch=1,
            grid=(1,),
            in_specs=[ANY] * len(inputs),
            out_specs=[HBM] * len(outputs),
            scratch_shapes=scratch_shapes,
        ),
        compiler_params=params(63),
    )(where, *inputs)
    split = []
    for _, group_out, _, _ in groups:
        split.append(result[: len(group_out)])
        result = result[len(group_out) :]
    return split


def fold_first(keep, got):
    _, blocks, _, _, _, rows, lanes = keep.shape
    every = slice(None)

    def pieces(at):
        _, y, x = at
        table = []
        for z in range(4):
            for half, index in ((0, (0, every, z, every, 1 - x)), (1, (1, every, z, 1 - y))):
                table.append((0, index, 1, index, half, (every, z)))
        return table

    return (keep, got), [(blocks, 4, 2, rows, lanes)] * 2, pieces, (blocks, 2, rows, lanes)


def fold_second(keep, got, arrived):
    _, blocks, _, _, _, rows, lanes = keep.shape
    every = slice(None)

    def pieces(at):
        _, y, x = at
        table = []
        for role in (1, 0):
            ax = x if role == 0 else 1 - x
            ay = y if role == 0 else 1 - y
            for z in range(4):
                for half, index, inner in ((0, (0, every, z, ay, x), ay), (1, (1, every, z, y, ax), ax)):
                    table.append((0, index, 1, index, 2 * half + (1 - role), (every, z), 2 + half, (every, z, inner)))
        return table

    return (keep, got, *arrived), [(blocks, 4, rows, lanes)] * 4, pieces, (blocks, rows, lanes)


def fold_third(parts, got, joined=True):
    blocks, _, rows, lanes = parts[1].shape
    every = slice(None)

    def pieces(at):
        table = []
        for n in (0, 1, 2, 3) if joined else (1, 2, 3, 0):
            for half in range(2):
                index = (every, n if joined else at[0] ^ n)
                table.append((2 * half, index, 2 * half + 1, index, 0 if joined else n, (n, half) if joined else (half,)))
        return table

    shape = (2, blocks, rows, lanes)
    return (parts[1], got[0], parts[3], got[1]), [(4,) + shape] if joined else [shape] * 4, pieces, (blocks, rows, lanes)


def fold_third_pair(first, second):
    def moved(group, lower, shapes):
        inputs, _, pieces, shape = group

        def at(where):
            return [(a, a_at, b, b_at, 0, o_at + (slice(lower, lower + shape[0]),)) for a, a_at, b, b_at, _, o_at in pieces(where)]

        return inputs, shapes, at, shape

    split = first[3][0]
    joined = (4, 2, split + second[3][0]) + first[3][1:]
    return [moved(first, 0, [joined]), moved(second, split, [])]


def fold_last(parts, widths, name, stack=1, extra=0, lower=0, upper=None):
    parts = parts if isinstance(parts, list) else [parts]
    blocks, deep, lanes = parts[0].shape[-3:]
    blocks = (blocks if upper is None else upper) - lower
    chunks = sum(widths) // (2 * lanes)
    rows = (blocks * deep - extra) // (chunks * stack)

    def body(*refs):
        ins, outs = refs[: len(parts)], refs[len(parts) :]
        if len(ins) == 1:
            ins = [ins[0].at[z] for z in range(4)]

        def take(half, line, count, at, size):
            step = min(deep, count)
            pieces = []
            for start in range(line, line + count, step):
                total = None
                for ref in ins:
                    value = ref[half, lower + start // deep, start % deep : start % deep + step, at : at + size].astype(F32)
                    total = value if total is None else total + value
                pieces.append(total)
            return pieces[0] if len(pieces) == 1 else jnp.concatenate(pieces, axis=0)

        base = 0
        for out, width in zip(outs, widths):
            tiles = width // 128
            for r in range(stack):
                for t in range(tiles):
                    chunk, at = (base + t * 128) // lanes, (base + t * 128) % lanes
                    line = (chunk % chunks * stack + r) * rows
                    out[pl.ds(r * rows * tiles + t, rows, stride=tiles), :] = take(chunk // chunks, line, rows, at, 128)
            base += width
        if extra:
            outs[-1][...] = take(0, blocks * deep - extra, extra, 0, lanes)[0]

    shapes = [jax.ShapeDtypeStruct((stack * rows * w // 128, 128), F32) for w in widths]
    if extra:
        shapes.append(jax.ShapeDtypeStruct((lanes,), F32))
    return pl.pallas_call(body, name=name, out_shape=shapes, compiler_params=params(63))(*parts)


def sync(*values):
    return lax.optimization_barrier(values)


def flip(value, bits):
    return lax.ppermute(value, "dp", [(i, i ^ bits) for i in range(16)])


def on_device(tokens, lengths, w_qkv, w_out, w_in, w_back, bias_q, value_bias, bias_out, gain1, shift1, bias_in, bias_back, gain2, shift2, cotangent):
    rows_local, half, width = tokens.shape
    dp = lax.axis_size("dp")
    dp_bits = dp.bit_length() - 1
    core = lax.axis_index("seq")
    rows = rows_local // 2
    length = 2 * half
    total = rows * length
    order_a = (0, 1) + tuple(range(2, dp_bits))
    order_b = (1, 0) + tuple(range(2, dp_bits))

    def send_rows(value):
        return swap(lax.dynamic_slice_in_dim(value, (1 - core) * rows, rows, 0))

    other = send_rows(tokens)
    cot_other = send_rows(cotangent)
    bq, bv, bo, g1, s1, bi, bb, g2, s2 = (bias_q, value_bias, bias_out, gain1, shift1, bias_in, bias_back, gain2, shift2)
    core_one = core.reshape(1).astype(jnp.int32)
    me = lax.axis_index("dp")
    fast = dp == 16 and width == 2 * LANES
    qkv, probs, full_tokens, mixed, low, hat1, inv1, inverse = attention_call(core_one, lengths, tokens, other, w_qkv, w_out, (bq, bv, bo, g1, s1))

    def flat(value):
        return value.reshape(total, value.shape[-1])

    full_tokens = flat(full_tokens)
    output, output_other, cls_own, dpre1, dmixed, g_bias_in, g_gain2, g_shift2, g_bias_back, g_gain1, g_shift1, g_bias_out, *grads = feed_call(
        core_one, lengths, flat(low), w_in, w_back, w_out, flat(mixed), flat(hat1), flat(inv1), flat(inverse), cotangent, cot_other,
        (bi.reshape(1, -1), bb, g1, g2, s2), dp, fast,
    )
    dmixed = dmixed.reshape(rows, length, width)
    cls_own = cls_own[:, : lengths.shape[1]]
    if fast:
        where = jnp.stack([me >> 2, (me >> 1) & 1, me & 1]).astype(jnp.int32)

        def view(value):
            return value.reshape((2, value.shape[0] // 2, 4, 2, 2) + value.shape[2:])

        def cross(parts, bit_a, bit_b):
            return flip(parts[0], bit_a), flip(parts[len(parts) // 2], bit_b)

        def along_z(parts):
            return lax.all_to_all(parts, "dp", 0, 0, axis_index_groups=[[i, i + 4, i + 8, i + 12] for i in range(4)], tiled=True)

        keep_b, send_b, keep_i, send_i = grads
        got_b = swap(send_b)
        base_b = view(keep_b), view(got_b)
        (back,) = add_pieces(where, [fold_first(*base_b)], "fold_a")
        dmixed, back, send_i, output_other = sync(dmixed, back, send_i, output_other)
        got_b = cross(back, 1, 2)
        got_i = swap(send_i)
        output_got = swap(output_other)
        dproj, *bias_a = attention_grad(qkv, probs, mixed, dmixed, 0, 1)
        dproj, got_i, keep_i, output_got = sync(dproj, got_i, keep_i, output_got)
        base_i = view(keep_i), view(got_i)
        (inner,) = add_pieces(where, [fold_first(*base_i)], "fold_b")
        inner, got_b = sync(inner, got_b)
        got_i = cross(inner, 1, 2)
        (back,) = add_pieces(where, [fold_second(*base_b, got_b)], "fold_b2")
        dmixed, back = sync(dmixed, back)
        got_b = cross(back, 2, 1)
        dproj, *bias_b = attention_grad(qkv, probs, mixed, dmixed, 1, 1, dproj)
        keep_q, send_q = grad_proj(
            core_one, full_tokens, dproj.reshape(3, total, width),
            (bias_a[0], bias_a[1], g_bias_out, g_gain1, g_shift1, g_bias_in, g_bias_back, g_gain2, g_shift2), bias_b, dp,
        )
        send_q, keep_q, got_b, got_i = sync(send_q, keep_q, got_b, got_i)
        got_q = swap(send_q)
        (inner,) = add_pieces(where, [fold_second(*base_i, got_i)], "fold_c")
        inner, got_q, keep_q, cls_own = sync(inner, got_q, keep_q, cls_own)
        got_i = cross(inner, 2, 1)
        cls_got = swap(cls_own)
        base_q = view(keep_q), view(got_q)
        (proj,) = add_pieces(where, [fold_first(*base_q)], "fold_d")
        proj, got_i, cls_got = sync(proj, got_i, cls_got)
        got_q = cross(proj, 1, 2)
        split = back[1].shape[0]
        joint = add_pieces(where, fold_third_pair(fold_third(back, got_b), fold_third(inner, got_i)), "fold_e")[0][0]
        dproj, joint = sync(dproj, joint)
        got_i = along_z(joint)
        dinput, dinput_other = input_grad_call(core_one, dproj.reshape(3, total, width), dpre1, w_qkv, half)
        dinput, dinput_other, got_q, output = sync(dinput, dinput_other, got_q, output)
        (proj,) = add_pieces(where, [fold_second(*base_q, got_q)], "fold_f")
        proj, dinput_other, output = sync(proj, dinput_other, output)
        got_q = cross(proj, 2, 1)
        dinput_got = swap(dinput_other)
        output = lax.dynamic_update_slice_in_dim(output, output_got, (1 - core) * rows, 0)
        output, got_q, dinput_got = sync(output, got_q, dinput_got)
        (proj,) = add_pieces(where, [fold_third(proj, got_q, False)], "fold_g")
        got_q = [proj[0]] + [flip(proj[n], 4 * n) for n in (1, 2, 3)]
        dinput, proj = sync(dinput, proj)
        dinput = lax.dynamic_update_slice_in_dim(dinput, dinput_got, (1 - core) * rows, 0)
        (r_back,) = fold_last(got_i, (width,), "back_sum", w_back.shape[0] // width, 0, 0, split)
        r_in, r_out = fold_last(got_i, (w_in.shape[1], width), "inner_sum", 1, 0, split)
        r_in, r_back, got_q, dinput = sync(r_in, r_back, got_q, dinput)
        r_qkv, r_vec = fold_last(got_q, (3 * width,), "proj_sum", 1, 8)
        r_vec = r_vec[: (8 * width + w_in.shape[1]) // (2 * dp)]
    else:
        g_back, g_inner = grads
        r_back = reduce_scatter(g_back, order_a, dp, dp_bits)
        r_inner = reduce_scatter(g_inner, order_b, dp, dp_bits)
        r_in, r_out = r_inner[:, :-width], r_inner[:, -width:]
        output_got, cls_got = swap(output_other), swap(cls_own)
        dproj, g_bias_q, g_bias_v = attention_grad(qkv, probs, mixed, dmixed, 0, rows)
        dproj = dproj.reshape(3, total, width)
        g_qkv = jnp.concatenate([weight_grad(full_tokens, dproj[n], width, width, "grad_qkv") for n in range(3)], axis=1)
        r_qkv = reduce_scatter(g_qkv, order_b, dp, dp_bits)
        dinput, dinput_other = input_grad_call(core_one, dproj, dpre1, w_qkv, half)
        dinput_got = swap(dinput_other)
    if not fast:
        table = vector_table((g_bias_q, g_bias_v, g_bias_out, g_gain1, g_shift1, g_bias_in, g_bias_back, g_gain2, g_shift2), 2 * dp)
        r_vec = jnp.sum(lax.all_to_all(table, ("dp", "seq"), 0, 0, tiled=True), axis=0)[: (8 * width + w_in.shape[1]) // (2 * dp)]
        output = lax.dynamic_update_slice_in_dim(output, output_got, (1 - core) * rows, 0)
        dinput = lax.dynamic_update_slice_in_dim(dinput, dinput_got, (1 - core) * rows, 0)
    cls = jnp.where(core == 0, jnp.concatenate([cls_own, cls_got], axis=0), jnp.concatenate([cls_got, cls_own], axis=0))
    return (
        output,
        cls,
        dinput,
        r_qkv.reshape(-1),
        r_out.reshape(-1),
        r_in.reshape(-1),
        r_back.reshape(-1),
        r_vec,
    )


def solution(mesh):
    row = P("dp", "seq", None)
    both = P(("dp", "seq"))
    return jax.shard_map(
        on_device,
        mesh=mesh,
        in_specs=(row, P("dp", None)) + (P(),) * 13 + (row,),
        out_specs=(row, P("dp", None, None), row, both, both, both, both, both),
        check_vma=False,
    )
```
